32 devices in a mesh: dp: 8 (over z, x), tensor: 4 (over y, core).
Axes of the slice: x: 2, y: 2, z: 4, core: 2. Of those that a mesh axis runs over, the one named last changes fastest.
Arguments:
- tokens: bfloat16 [32768, 768], P('dp'), may hold values from -6 to 6
- cotangent: bfloat16 [32768, 768], P('dp'), may hold values from -6 to 6
- short_len: int32 [128], P('dp'), may hold values from 64 to 128, as said below
- long_len: int32 [32], P('dp'), may hold values from 256 to 512, as said below
- short_count: int32 [8], P('dp'), may hold values from 8 to 16, as said below
- long_count: int32 [8], P('dp'), may hold values from 0 to 4, as said below
- query_weight: bfloat16 [768, 768], P(None, 'tensor'), may hold values from -0.3125 to 0.3125
- query_bias: bfloat16 [768], P('tensor'), may hold values from -3 to 3
- key_weight: bfloat16 [768, 768], P(None, 'tensor'), may hold values from -0.3125 to 0.3125
- value_weight: bfloat16 [768, 768], P(None, 'tensor'), may hold values from -0.21875 to 0.21875
- value_bias: bfloat16 [768], P('tensor'), may hold values from -3 to 3
- output_weight: bfloat16 [768, 768], P('tensor'), may hold values from -0.875 to 0.875
- output_bias: bfloat16 [768], replicated, may hold values from -3 to 3
- first_gain: bfloat16 [768], replicated, may hold values from 0.5 to 1.5
- first_shift: bfloat16 [768], replicated, may hold values from -3 to 3
- up_weight: bfloat16 [768, 3072], P(None, 'tensor'), may hold values from -0.21875 to 0.21875
- up_bias: bfloat16 [3072], P('tensor'), may hold values from -3 to 3
- down_weight: bfloat16 [3072, 768], P('tensor'), may hold values from -0.109375 to 0.109375
- down_bias: bfloat16 [768], replicated, may hold values from -2 to 2
- second_gain: bfloat16 [768], replicated, may hold values from 0.5 to 1.5
- second_shift: bfloat16 [768], replicated, may hold values from -3 to 3
Outputs:
- layer_output: bfloat16 [32768, 768], P('dp')
- input_grad: float32 [32768, 768], P('dp')
- grad_query_weight: float32 [768, 768], P(None, 'tensor')
- grad_query_bias: float32 [768], P('tensor')
- grad_key_weight: float32 [768, 768], P(None, 'tensor')
- grad_value_weight: float32 [768, 768], P(None, 'tensor')
- grad_value_bias: float32 [768], P('tensor')
- grad_output_weight: float32 [768, 768], P('tensor')
- grad_output_bias: float32 [768], replicated
- grad_first_gain: float32 [768], replicated
- grad_first_shift: float32 [768], replicated
- grad_up_weight: float32 [768, 3072], P(None, 'tensor')
- grad_up_bias: float32 [3072], P('tensor')
- grad_down_weight: float32 [3072, 768], P('tensor')
- grad_down_bias: float32 [768], replicated
- grad_second_gain: float32 [768], replicated
- grad_second_shift: float32 [768], replicated
The draws below stay inside these ranges and needn't reach their ends.
Inputs may be any that keep to these rules, and one draw needn't show every extreme that they name: `short_len`: some slot has exactly 128 valid tokens. `long_len`: some slot has exactly 512 valid tokens. `short_count`: slots at or beyond the count hold no valid tokens; some index of dp has all 16 live. `long_count`: slots at or beyond the count hold no valid tokens; some index of dp has all 4 live.
All inputs are finite; a program needn't handle non-finite values.
Results may differ from the reference program's by a relative error of at most 0.02.
Values may be sent and summed in bfloat16 or wider, within the bound.
No kernel may reach another device: no remote copies, remote signals or barrier semaphores. Data moves between devices by JAX's collectives and lax.ppermute only.
A program may use at most 256 MiB of HBM per device.

```python
import jax
import jax.numpy as jnp
from jax import lax

D = 768
HEADS = 12
HEAD_DIM = 64
FF = 3072
SHORT_LEN = 128
LONG_LEN = 512
SHORT_CAP = 16
LONG_CAP = 4
TOK_DEV = 4096
GROUPS = 8
TOKENS = 32768
SHORT_SEQS = 128
LONG_SEQS = 32
N_TENSOR = 4


def force_top(key, values, top_value):
    spot = jax.random.randint(key, (), 0, values.shape[0])
    return jnp.where(jnp.arange(values.shape[0]) == spot, top_value, values).astype(jnp.int32)


def draw_short_len(key, part):
    values = jax.random.randint(jax.random.fold_in(key, 101), (SHORT_SEQS,), SHORT_LEN // 2, SHORT_LEN + 1)
    return force_top(jax.random.fold_in(key, 102), values, SHORT_LEN)


def draw_long_len(key, part):
    values = jax.random.randint(jax.random.fold_in(key, 201), (LONG_SEQS,), LONG_LEN // 2, LONG_LEN + 1)
    return force_top(jax.random.fold_in(key, 202), values, LONG_LEN)


def draw_short_count(key, part):
    values = jax.random.randint(jax.random.fold_in(key, 301), (GROUPS,), SHORT_CAP // 2, SHORT_CAP + 1)
    return force_top(jax.random.fold_in(key, 302), values, SHORT_CAP)


def draw_long_count(key, part):
    values = jax.random.randint(jax.random.fold_in(key, 401), (GROUPS,), 0, LONG_CAP + 1)
    return force_top(jax.random.fold_in(key, 402), values, LONG_CAP)


def levels(rng, shape, cuts, least, high):
    factor_of, own = 1.0, jax.random.fold_in(rng, 6)
    for axis_at, shards_of in cuts:
        heights = jnp.exp(jax.random.uniform(jax.random.fold_in(own, axis_at), (shards_of,), jnp.float32, least / len(cuts), high / len(cuts)))
        factor_of = factor_of * jnp.repeat(heights, shape[axis_at] // shards_of).reshape([-1 if axis == axis_at else 1 for axis in range(len(shape))])
    return factor_of


def centred(own_key, dims, width, limit, shards=(), held_as=jnp.bfloat16):
    values = jax.random.normal(own_key, dims, jnp.float32) * width
    if len(shards) > 0:
        values = levels(own_key, dims, shards, -0.22, 0.18) * values
    return jnp.clip(values, min=-limit, max=limit).astype(held_as)


def setup_inputs(seed: int = 0) -> dict:
    key_list = jax.random.split(jax.random.key(seed), 22)
    return {
        "tokens": centred(key_list[0], (TOKENS, D), 1.0, 6.0, ((0, 8),)),
        "cotangent": centred(key_list[1], (TOKENS, D), 1.0, 6.0, ((0, 8),)),
        "short_len": draw_short_len(jax.random.fold_in(key_list[21], 71), 0),
        "long_len": draw_long_len(jax.random.fold_in(key_list[21], 71), 0),
        "short_count": draw_short_count(jax.random.fold_in(key_list[21], 71), 0),
        "long_count": draw_long_count(jax.random.fold_in(key_list[21], 71), 0),
        "query_weight": centred(key_list[6], (D, D), (D // 2) ** -0.5, 0.3125, ((1, 4),)),
        "query_bias": centred(key_list[7], (D,), 0.5, 3.0, ((0, 4),)),
        "key_weight": centred(key_list[8], (D, D), (D // 2) ** -0.5, 0.3125, ((1, 4),)),
        "value_weight": centred(key_list[9], (D, D), D ** -0.5, 0.21875, ((1, 4),)),
        "value_bias": centred(key_list[10], (D,), 0.5, 3.0, ((0, 4),)),
        "output_weight": centred(key_list[11], (D, D), (D // 16) ** -0.5, 0.875, ((0, 4),)),
        "output_bias": centred(key_list[12], (D,), 0.5, 3.0),
        "first_gain": jnp.clip(1.0 + 0.1 * jax.random.normal(key_list[13], (D,), jnp.float32), 0.5, 1.5).astype(jnp.bfloat16),
        "first_shift": centred(key_list[14], (D,), 0.5, 3.0),
        "up_weight": centred(key_list[15], (D, FF), D ** -0.5, 0.21875, ((1, 4),)),
        "up_bias": centred(key_list[16], (FF,), 0.5, 3.0, ((0, 4),)),
        "down_weight": centred(key_list[17], (FF, D), FF ** -0.5, 0.109375, ((0, 4),)),
        "down_bias": centred(key_list[18], (D,), 0.3, 2.0),
        "second_gain": jnp.clip(1.0 + 0.1 * jax.random.normal(key_list[19], (D,), jnp.float32), 0.5, 1.5).astype(jnp.bfloat16),
        "second_shift": centred(key_list[20], (D,), 0.5, 3.0),
    }


@jax.custom_vjp
def low(v):
    return lax.optimization_barrier(v.astype(jnp.bfloat16)).astype(jnp.float32)

@jax.custom_vjp
def low_back(v):
    return v

def low_keep(v):
    return (low(v), None)

def low_pass(kept, grad):
    return (grad,)

def back_keep(v):
    return (v, None)

def back_low(kept, grad):
    return (low(grad),)
low.defvjp(low_keep, low_pass)
low_back.defvjp(back_keep, back_low)

def matmul(left_side, right_side):
    return jnp.dot(left_side, right_side, precision=lax.Precision.HIGHEST)

def layer_norm(values, norm_gain, norm_shift):
    centre = values - lax.optimization_barrier(jnp.mean(values, axis=-1, keepdims=True))
    spread = lax.optimization_barrier(jnp.mean(centre * centre, axis=-1, keepdims=True))
    return centre * lax.rsqrt(spread + 1e-12) * norm_gain + norm_shift

def token_masks(lengths, live_count, slot_count, slot_width):
    position = jnp.arange(slot_width, dtype=jnp.int32)
    live_slots = jnp.arange(slot_count, dtype=jnp.int32) < live_count
    return (position[None, :] < lengths[:, None]) & live_slots[:, None]

def attention(queries, key_states, value_states, valid_keys):
    scale_factor = HEAD_DIM ** (-0.5)
    scores = jnp.einsum('bqhe,bkhe->bhqk', queries, key_states, precision=lax.Precision.HIGHEST) * scale_factor
    scores = low_back(jnp.where(valid_keys[:, None, None, :], scores, -30000.0))
    softmax_out = low(jax.nn.softmax(scores, axis=-1))
    mixed_heads = jnp.einsum('bhqk,bkhe->bqhe', softmax_out, value_states, precision=lax.Precision.HIGHEST)
    return low_back(low(mixed_heads))

def block_forward(block_rows, params, short_valid, long_valid):
    query_weight, query_bias, key_weight, value_weight, value_bias, output_weight, output_bias, first_gain, first_shift, up_weight, up_bias, down_weight, down_bias, second_gain, second_shift = params
    head_width = D // N_TENSOR
    unit_width = FF // N_TENSOR
    heads_group = HEADS // N_TENSOR
    short_rows = SHORT_CAP * SHORT_LEN
    short_shape = (SHORT_CAP, SHORT_LEN, heads_group, HEAD_DIM)
    long_shape = (LONG_CAP, LONG_LEN, heads_group, HEAD_DIM)
    attn_total = jnp.zeros_like(block_rows)
    for group_index in range(N_TENSOR):
        column_start = group_index * head_width
        column_stop = column_start + head_width
        source = low_back(block_rows)
        queries = low(low_back(matmul(source, query_weight[:, column_start:column_stop])) + query_bias[column_start:column_stop])
        key_states = low(low_back(matmul(source, key_weight[:, column_start:column_stop])))
        value_states = low(low_back(matmul(source, value_weight[:, column_start:column_stop])) + value_bias[column_start:column_stop])
        short_mixed = attention(queries[:short_rows].reshape(short_shape), key_states[:short_rows].reshape(short_shape), value_states[:short_rows].reshape(short_shape), short_valid)
        long_mixed = attention(queries[short_rows:].reshape(long_shape), key_states[short_rows:].reshape(long_shape), value_states[short_rows:].reshape(long_shape), long_valid)
        mixed_heads = jnp.concatenate([short_mixed.reshape(short_rows, head_width), long_mixed.reshape(LONG_CAP * LONG_LEN, head_width)], axis=0)
        attn_total = attn_total + low(matmul(mixed_heads, output_weight[column_start:column_stop]))
    hidden = block_rows + (low_back(attn_total) + output_bias)
    first_norm = layer_norm(hidden, first_gain, first_shift)
    first_low = low(first_norm)
    ffn_total = jnp.zeros_like(block_rows)
    for group_index in range(N_TENSOR):
        column_start = group_index * unit_width
        column_stop = column_start + unit_width
        up_inner = low_back(matmul(low_back(first_low), up_weight[:, column_start:column_stop])) + up_bias[column_start:column_stop]
        active = low(jax.nn.gelu(up_inner, approximate=False))
        ffn_total = ffn_total + low(matmul(active, down_weight[column_start:column_stop]))
    second_input = first_norm + (low_back(ffn_total) + down_bias)
    return layer_norm(second_input, second_gain, second_shift)

def add_up(running, extra):
    return running + extra

def reference(tokens, cotangent, short_len, long_len, short_count, long_count, query_weight, query_bias, key_weight, value_weight, value_bias, output_weight, output_bias, first_gain, first_shift, up_weight, up_bias, down_weight, down_bias, second_gain, second_shift):
    params = tuple((weight.astype(jnp.float32) for weight in (query_weight, query_bias, key_weight, value_weight, value_bias, output_weight, output_bias, first_gain, first_shift, up_weight, up_bias, down_weight, down_bias, second_gain, second_shift)))
    token_blocks = tokens.reshape(GROUPS, TOK_DEV, D)
    cotangent_blocks = cotangent.reshape(GROUPS, TOK_DEV, D)
    short_lengths = short_len.reshape(GROUPS, SHORT_CAP)
    long_lengths = long_len.reshape(GROUPS, LONG_CAP)

    def one_block(totals, index):
        block_rows = token_blocks[index].astype(jnp.float32)
        short_valid = token_masks(short_lengths[index], short_count[index], SHORT_CAP, SHORT_LEN)
        long_valid = token_masks(long_lengths[index], long_count[index], LONG_CAP, LONG_LEN)
        valid_rows = jnp.concatenate([short_valid.reshape(-1), long_valid.reshape(-1)]).astype(jnp.float32)

        def forward(rows_in, weights_in):
            return block_forward(rows_in, weights_in, short_valid, long_valid)
        result, pullback = jax.vjp(forward, block_rows, params)
        upstream = cotangent_blocks[index].astype(jnp.float32) * valid_rows[:, None]
        row_grad, weight_grads = pullback(upstream)
        totals = jax.tree.map(add_up, totals, weight_grads)
        return (totals, (result.astype(jnp.bfloat16), row_grad))
    zeros = jax.tree.map(jnp.zeros_like, params)
    totals, (outputs, row_grads) = lax.scan(one_block, zeros, jnp.arange(GROUPS, dtype=jnp.int32))
    return (outputs.reshape(TOKENS, D), row_grads.reshape(TOKENS, D), totals[0], totals[1], totals[2], totals[3], totals[4], totals[5], totals[6], totals[7], totals[8], totals[9], totals[10], totals[11], totals[12], totals[13], totals[14])
```

```python
import functools

import jax
import jax.numpy as jnp
from jax import lax
from jax.experimental import pallas as pl
from jax.experimental.pallas import tpu as pltpu
from jax.sharding import PartitionSpec as P

HEAD_DIM = 64
SHORT_LEN = 128
LONG_LEN = 512
ROWS = 512
SLOTS = ROWS // SHORT_LEN
PAIR = 2 * HEAD_DIM
MASKED = -30000.0
F32 = jnp.float32
BF16 = jnp.bfloat16
VMEM_LIMIT = 62 * 1024 * 1024


def nn(left, right):
    return lax.dot_general(left, right, (((1,), (0,)), ((), ())), preferred_element_type=F32)


def nt(left, right):
    return lax.dot_general(left, right, (((1,), (1,)), ((), ())), preferred_element_type=F32)


def tn(left, right):
    return lax.dot_general(left, right, (((0,), (0,)), ((), ())), preferred_element_type=F32)


def fold_rows(values):
    return jnp.sum(values.reshape(-1, 8, values.shape[-1]), axis=0)


def total_rows(values):
    return jnp.sum(values, axis=0, keepdims=True)


def half_mask(which):
    lanes = lax.broadcasted_iota(jnp.int32, (1, PAIR), 1)
    return (lanes >= HEAD_DIM) if which else (lanes < HEAD_DIM)


def short_valid(meta, block, slot):
    index = SLOTS * (2 * block + meta[0][0]) + slot
    return jnp.where(index < meta[3][0], meta[1][index], 0)


def long_valid(meta, block, short_blocks):
    index = 2 * (block - short_blocks) + 1 - meta[0][0]
    return jnp.where(index < meta[4][0], meta[2][index], 0)


def norm_rows(values):
    centre = values - jnp.mean(values, axis=-1, keepdims=True)
    scale = lax.rsqrt(jnp.mean(centre * centre, axis=-1, keepdims=True) + 1e-12)
    return centre * scale, scale


def norm_back(incoming, normed, scale, gain):
    grad = incoming * gain
    inner = grad - jnp.mean(grad, axis=-1, keepdims=True)
    inner = inner - normed * jnp.mean(grad * normed, axis=-1, keepdims=True)
    return scale * inner


def load_attention_weights(pieces, wqkv, wout, bias, sems):
    width = wqkv.shape[0] // 12
    copies = []
    for j, piece in enumerate(pieces):
        for k in range(3):
            copies.append(
                (piece.at[pl.ds(k * width, width)], wqkv.at[pl.ds((4 * k + j) * width, width)])
            )
        copies.append((piece.at[pl.ds(3 * width, width)], wout.at[pl.ds(j * width, width)]))
        copies.append((piece.at[pl.ds(4 * width, 16)], bias.at[pl.ds(16 * j, 16)]))
    started = [pltpu.make_async_copy(s, d, sems.at[n]) for n, (s, d) in enumerate(copies)]
    for copy in started:
        copy.start()
    for copy in started:
        copy.wait()


def attention_forward_kernel(
    short_blocks, core, slen, llen, scount, lcount, x, a0, a1, a2, a3, vec,
    qkv, mixed, normed, stat, wqkv, wout, bias, sems,
):
    meta = (core, slen, llen, scount, lcount)
    block = pl.program_id(0)
    width = wout.shape[0]

    @pl.when(block == 0)
    def _():
        load_attention_weights((a0, a1, a2, a3), wqkv, wout, bias, sems)

    low = x[...]
    small = bias[...].astype(F32)
    query_bias = sum(small[16 * j + 1 + j : 16 * j + 2 + j] for j in range(4))
    value_bias = sum(small[16 * j + 5 + j : 16 * j + 6 + j] for j in range(4))
    qkv[:, 0:width] = (nt(low, wqkv[0:width]) + query_bias).astype(BF16)
    qkv[:, width : 2 * width] = nt(low, wqkv[width : 2 * width]).astype(BF16)
    qkv[:, 2 * width : 3 * width] = (nt(low, wqkv[2 * width : 3 * width]) + value_bias).astype(BF16)
    stat[...] = jnp.zeros_like(stat)
    lanes = lax.broadcasted_iota(jnp.int32, (1, 128), 1)

    def one_tile(pair, query_at, queries, key_at, keys, valid):
        column = pl.multiple_of(pair * PAIR, PAIR)
        q = qkv[query_at : query_at + queries, pl.ds(column, PAIR)] * jnp.asarray(0.125, BF16)
        k = qkv[key_at : key_at + keys, pl.ds(width + column, PAIR)]
        v = qkv[key_at : key_at + keys, pl.ds(2 * width + column, PAIR)]
        live = lax.broadcasted_iota(jnp.int32, (1, keys), 1) < valid
        parts = []
        logs = stat[query_at : query_at + queries]
        for e in range(2):
            scores = nt(jnp.where(half_mask(e), q, jnp.zeros_like(q)), k)
            scores = jnp.where(live, scores, MASKED)
            top = jnp.max(scores, axis=-1, keepdims=True)
            weights = jnp.exp(scores - top)
            total = jnp.sum(weights, axis=-1, keepdims=True)
            parts.append(nn(weights.astype(BF16), v) * (1.0 / total))
            logs = jnp.where(lanes == 2 * pair + e, top + jnp.log(total), logs)
        stat[query_at : query_at + queries] = logs
        mixed[query_at : query_at + queries, pl.ds(column, PAIR)] = jnp.where(
            half_mask(0), parts[0], parts[1]
        ).astype(BF16)

    @pl.when(block < short_blocks)
    def _():
        def body(pair, carry):
            for slot in range(SLOTS):
                at = slot * SHORT_LEN
                one_tile(pair, at, SHORT_LEN, at, SHORT_LEN, short_valid(meta, block, slot))
            return carry

        lax.fori_loop(0, width // PAIR, body, 0)

    @pl.when(block >= short_blocks)
    def _():
        valid = long_valid(meta, block, short_blocks)

        def body(pair, carry):
            for part in range(2):
                one_tile(pair, part * 256, 256, 0, LONG_LEN, valid)
            return carry

        lax.fori_loop(0, width // PAIR, body, 0)

    hidden = low.astype(F32) + (nn(mixed[...], wout[...]) + vec[0:1])
    rows, scale = norm_rows(hidden)
    normed[...] = rows.astype(BF16)
    stat[...] = jnp.where(lanes == 12, scale, stat[...])


def ffn_forward_kernel(
    short_blocks, core, slen, llen, scount, lcount, normed, cotangent, u0, u1, u2, u3,
    d0, d1, d2, d3, b0, b1, b2, b3, vec,
    layer_out, grad_low, slope, down_grad, sums, active, down_sum, vec_sum,
):
    meta = (core, slen, llen, scount, lcount)
    block = pl.program_id(0)
    width = u0.shape[1]

    @pl.when(block == 0)
    def _():
        down_sum[...] = jnp.zeros_like(down_sum)
        vec_sum[...] = jnp.zeros_like(vec_sum)

    first = normed[...].astype(F32) * vec[1:2] + vec[2:3]
    first_low = first.astype(BF16)
    total = first + vec[3:4]
    for j, (up, down, bias) in enumerate(((u0, d0, b0), (u1, d1, b1), (u2, d2, b2), (u3, d3, b3))):
        inner = nn(first_low, up[...]) + bias[0:1].astype(F32)
        chance = 0.5 * (1.0 + lax.erf(inner * 0.7071067811865476))
        units = (inner * chance).astype(BF16)
        slope[:, j * width : (j + 1) * width] = (
            chance + inner * jnp.exp(-0.5 * inner * inner) * 0.3989422804014327
        ).astype(BF16)
        if j < 2:
            active[j] = units
        total = total + nn(units, down[...])
    rows, scale = norm_rows(total)
    layer_out[...] = (rows * vec[4:5] + vec[5:6]).astype(BF16)
    position = lax.broadcasted_iota(jnp.int32, (ROWS, 1), 0)
    slot = position // SHORT_LEN
    short_limit = jnp.zeros((ROWS, 1), jnp.int32)
    for n in range(SLOTS):
        short_limit = jnp.where(slot == n, short_valid(meta, jnp.minimum(block, short_blocks - 1), n), short_limit)
    long_limit = long_valid(meta, jnp.maximum(block, short_blocks), short_blocks)
    is_short = block < short_blocks
    alive = jnp.where(is_short, position % SHORT_LEN, position) < jnp.where(
        is_short, short_limit, long_limit
    )
    upstream = jnp.where(alive, cotangent[...].astype(F32), 0.0)
    grad = norm_back(upstream, rows, scale, vec[4:5])
    low = grad.astype(BF16)
    grad_low[...] = low
    vec_sum[0] += fold_rows(upstream * rows)
    vec_sum[1] += fold_rows(upstream)
    vec_sum[2] += fold_rows(grad)
    for j in range(2):
        down_sum[j] += tn(active[j], low)

    @pl.when(block == pl.num_programs(0) - 1)
    def _():
        down_grad[...] = down_sum[...].astype(BF16)
        sums[...] = jnp.zeros_like(sums)
        for n in range(3):
            sums[n : n + 1] = total_rows(vec_sum[n])


def ffn_backward_kernel(
    grad_low, slope, normed, u0, u1, u2, u3, d0, d1, d2, d3, vec,
    first_grad, up_grad, sums, up_sum, vec_sum,
):
    block = pl.program_id(0)
    width = u0.shape[1]

    @pl.when(block == 0)
    def _():
        up_sum[...] = jnp.zeros_like(up_sum)
        vec_sum[...] = jnp.zeros_like(vec_sum)

    low = grad_low[...]
    first_low = (normed[...].astype(F32) * vec[1:2] + vec[2:3]).astype(BF16)
    total = low.astype(F32)
    for j, (up, down) in enumerate(((u0, d0), (u1, d1), (u2, d2), (u3, d3))):
        inner = nt(low, down[...]) * slope[:, j * width : (j + 1) * width].astype(F32)
        inner_low = inner.astype(BF16)
        total = total + nt(inner_low, up[...])
        if j < 2:
            vec_sum[j] += fold_rows(inner)
            up_sum[j] += tn(first_low, inner_low)
    first_grad[...] = total.astype(BF16)

    @pl.when(block == pl.num_programs(0) - 1)
    def _():
        up_grad[...] = up_sum[...].astype(BF16)
        sums[...] = jnp.zeros_like(sums)
        for n in range(2):
            sums[n : n + 1] = total_rows(vec_sum[n])


def attention_backward_kernel(
    short_blocks, core, slen, llen, scount, lcount, first_grad, normed, stat, qkv, mixed, x,
    a0, a1, a2, a3, vec,
    input_grad, out_grad, qkv_grad, sums, wqkv, wout, bias, sems, low_qkv, mixed_grad,
    out_sum, qkv_sum, vec_sum,
):
    meta = (core, slen, llen, scount, lcount)
    block = pl.program_id(0)
    width = wout.shape[0]
    half = width // 2

    @pl.when(block == 0)
    def _():
        load_attention_weights((a0, a1, a2, a3), wqkv, wout, bias, sems)
        out_sum[...] = jnp.zeros_like(out_sum)
        qkv_sum[...] = jnp.zeros_like(qkv_sum)
        vec_sum[...] = jnp.zeros_like(vec_sum)

    incoming = first_grad[...].astype(F32)
    rows = normed[...].astype(F32)
    grad = norm_back(incoming, rows, stat[:, 12:13], vec[1:2])
    low = grad.astype(BF16)
    vec_sum[0] += fold_rows(incoming * rows)
    vec_sum[1] += fold_rows(incoming)
    vec_sum[2] += fold_rows(grad)
    out_sum[...] += tn(mixed[:, 0:half], low)
    mixed_grad[...] = nt(low, wout[...]).astype(BF16)

    def one_tile(pair, at, size, valid):
        column = pl.multiple_of(pair * PAIR, PAIR)
        span = pl.ds(at, size)
        q = qkv[span, pl.ds(column, PAIR)] * jnp.asarray(0.125, BF16)
        k = qkv[span, pl.ds(width + column, PAIR)]
        v = qkv[span, pl.ds(2 * width + column, PAIR)]
        g = mixed_grad[span, pl.ds(column, PAIR)]
        own = g.astype(F32) * mixed[span, pl.ds(column, PAIR)].astype(F32)
        live = lax.broadcasted_iota(jnp.int32, (1, size), 1) < valid
        logs = stat[span]
        lanes = lax.broadcasted_iota(jnp.int32, (1, 128), 1)
        parts = []
        for e in range(2):
            pick = half_mask(e)
            q_e = jnp.where(pick, q, jnp.zeros_like(q))
            g_e = jnp.where(pick, g, jnp.zeros_like(g))
            k_e = jnp.where(pick, k, jnp.zeros_like(k))
            log = jnp.sum(jnp.where(lanes == 2 * pair + e, logs, 0.0), axis=-1, keepdims=True)
            delta = jnp.sum(jnp.where(pick, own, 0.0), axis=-1, keepdims=True)
            probs = jnp.where(live, jnp.exp(nt(q_e, k) - log), 0.0)
            scores = (probs * (nt(g_e, v) - delta)).astype(BF16)
            parts.append((nn(scores, k_e), tn(scores, q_e), tn(probs.astype(BF16), g_e)))
        dq = (parts[0][0] + parts[1][0]) * 0.125
        dk = parts[0][1] + parts[1][1]
        dv = parts[0][2] + parts[1][2]
        low_qkv[span, pl.ds(column, PAIR)] = dq.astype(BF16)
        low_qkv[span, pl.ds(width + column, PAIR)] = dk.astype(BF16)
        low_qkv[span, pl.ds(2 * width + column, PAIR)] = dv.astype(BF16)

    @pl.when(block < short_blocks)
    def _():
        def body(pair, carry):
            for slot in range(SLOTS):
                one_tile(pair, slot * SHORT_LEN, SHORT_LEN, short_valid(meta, block, slot))
            return carry

        lax.fori_loop(0, width // PAIR, body, 0)

    @pl.when(block >= short_blocks)
    def _():
        valid = long_valid(meta, block, short_blocks)

        def body(pair, carry):
            one_tile(pair, 0, LONG_LEN, valid)
            return carry

        lax.fori_loop(0, width // PAIR, body, 0)

    vec_sum[3] += fold_rows(low_qkv[:, 0:width].astype(F32))
    vec_sum[4] += fold_rows(low_qkv[:, 2 * width : 3 * width].astype(F32))
    for k in range(3):
        qkv_sum[k] += tn(low_qkv[:, k * width : k * width + half], x[...])
    input_grad[...] = (grad + nn(low_qkv[...], wqkv[...])).astype(BF16)

    @pl.when(block == pl.num_programs(0) - 1)
    def _():
        out_grad[...] = out_sum[...].astype(BF16)
        qkv_grad[...] = qkv_sum[...].astype(BF16)
        sums[...] = jnp.zeros_like(sums)
        for n in range(5):
            sums[n : n + 1] = total_rows(vec_sum[n])


def const_spec(shape):
    return pl.BlockSpec(
        shape, lambda *_: (0,) * len(shape), pipeline_mode=pl.Buffered(1)
    )


def any_spec():
    return pl.BlockSpec(memory_space=pl.ANY)


def own_spec(width):
    return pl.BlockSpec((ROWS, width), lambda i, *_: (i, 0))


def compute(meta, tokens, cotangent, pieces, ups, downs, vec, short_blocks, long_blocks):
    blocks = short_blocks + long_blocks
    rows = blocks * ROWS
    d = tokens.shape[1]
    width = ups[0].shape[1]
    half = d // 2

    def global_block(i, core, *_):
        return (2 * i + jnp.where(i < short_blocks, core[0], 1 - core[0]), 0)

    global_spec = pl.BlockSpec((ROWS, d), global_block)
    bias_spec = pl.BlockSpec((16, d), lambda *_: (d // 16, 0), pipeline_mode=pl.Buffered(1))
    vec_spec = const_spec((8, d))
    params = pltpu.CompilerParams(
        dimension_semantics=("arbitrary",), vmem_limit_bytes=VMEM_LIMIT
    )
    weights_scratch = [
        pltpu.VMEM((3 * d, d), BF16),
        pltpu.VMEM((d, d), BF16),
        pltpu.VMEM((64, d), BF16),
        pltpu.SemaphoreType.DMA((20,)),
    ]
    sds = jax.ShapeDtypeStruct

    qkv, mixed, normed, stat = pl.pallas_call(
        functools.partial(attention_forward_kernel, short_blocks),
        name="attention_forward",
        grid_spec=pltpu.PrefetchScalarGridSpec(
            num_scalar_prefetch=5,
            grid=(blocks,),
            in_specs=[global_spec] + [any_spec()] * 4 + [vec_spec],
            out_specs=[own_spec(3 * d), own_spec(d), own_spec(d), own_spec(128)],
            scratch_shapes=weights_scratch,
        ),
        out_shape=[sds((rows, 3 * d), BF16), sds((rows, d), BF16), sds((rows, d), BF16), sds((rows, 128), F32)],
        compiler_params=params,
        cost_estimate=pl.CostEstimate(
            flops=2 * rows * d * 4 * d + 4 * rows * 320 * d,
            bytes_accessed=rows * d * 12 + 8 * d * d,
            transcendentals=rows * 320 * 12,
        ),
    )(*meta, tokens, *pieces, vec)

    layer_out, grad_low, slope, down_grad, sums_two = pl.pallas_call(
        functools.partial(ffn_forward_kernel, short_blocks),
        name="ffn_forward",
        grid_spec=pltpu.PrefetchScalarGridSpec(
            num_scalar_prefetch=5,
            grid=(blocks,),
            in_specs=[own_spec(d), global_spec] + [const_spec((d, width))] * 4
            + [const_spec((width, d))] * 4 + [bias_spec] * 4 + [vec_spec],
            out_specs=[own_spec(d), own_spec(d), own_spec(4 * width),
                       const_spec((2, width, d)), const_spec((8, d))],
            scratch_shapes=[pltpu.VMEM((2, ROWS, width), BF16), pltpu.VMEM((2, width, d), F32),
                            pltpu.VMEM((3, 8, d), F32)],
        ),
        out_shape=[sds((rows, d), BF16), sds((rows, d), BF16), sds((rows, 4 * width), BF16),
                   sds((2, width, d), BF16), sds((8, d), F32)],
        compiler_params=params,
        cost_estimate=pl.CostEstimate(
            flops=2 * rows * d * 10 * width, bytes_accessed=rows * d * 20, transcendentals=rows * 8 * width
        ),
    )(*meta, normed, cotangent, *ups, *downs, *pieces, vec)

    first_grad, up_grad, sums_up = pl.pallas_call(
        ffn_backward_kernel,
        name="ffn_backward",
        grid_spec=pltpu.PrefetchScalarGridSpec(
            num_scalar_prefetch=0,
            grid=(blocks,),
            in_specs=[own_spec(d), own_spec(4 * width), own_spec(d)] + [const_spec((d, width))] * 4
            + [const_spec((width, d))] * 4 + [vec_spec],
            out_specs=[own_spec(d), const_spec((2, d, width)), const_spec((8, width))],
            scratch_shapes=[pltpu.VMEM((2, d, width), F32), pltpu.VMEM((2, 8, width), F32)],
        ),
        out_shape=[sds((rows, d), BF16), sds((2, d, width), BF16), sds((8, width), F32)],
        compiler_params=params,
        cost_estimate=pl.CostEstimate(
            flops=2 * rows * d * 10 * width, bytes_accessed=rows * d * 16, transcendentals=0
        ),
    )(grad_low, slope, normed, *ups, *downs, vec)

    input_grad, out_grad, qkv_grad, sums_one = pl.pallas_call(
        functools.partial(attention_backward_kernel, short_blocks),
        name="attention_backward",
        grid_spec=pltpu.PrefetchScalarGridSpec(
            num_scalar_prefetch=5,
            grid=(blocks,),
            in_specs=[own_spec(d), own_spec(d), own_spec(128), own_spec(3 * d), own_spec(d), global_spec]
            + [any_spec()] * 4 + [vec_spec],
            out_specs=[own_spec(d), const_spec((half, d)), const_spec((3, half, d)), const_spec((8, d))],
            scratch_shapes=weights_scratch
            + [pltpu.VMEM((ROWS, 3 * d), BF16), pltpu.VMEM((ROWS, d), BF16), pltpu.VMEM((half, d), F32),
               pltpu.VMEM((3, half, d), F32), pltpu.VMEM((5, 8, d), F32)],
        ),
        out_shape=[sds((rows, d), BF16), sds((half, d), BF16), sds((3, half, d), BF16), sds((8, d), F32)],
        compiler_params=params,
        cost_estimate=pl.CostEstimate(
            flops=2 * rows * d * 6 * d + 10 * rows * 320 * d,
            bytes_accessed=rows * d * 16,
            transcendentals=rows * 320 * 12,
        ),
    )(*meta, first_grad, normed, stat, qkv, mixed, tokens, *pieces, vec)
    return layer_out, input_grad, down_grad, up_grad, out_grad, qkv_grad, sums_two, sums_up, sums_one


def per_device(
    tokens,
    cotangent,
    short_len,
    long_len,
    short_count,
    long_count,
    query_weight,
    query_bias,
    key_weight,
    value_weight,
    value_bias,
    output_weight,
    output_bias,
    first_gain,
    first_shift,
    up_weight,
    up_bias,
    down_weight,
    down_bias,
    second_gain,
    second_shift,
):
    d = tokens.shape[1]
    head_width = query_weight.shape[1]
    short_blocks = short_len.shape[0] * SHORT_LEN // (2 * ROWS)
    long_blocks = long_len.shape[0] * LONG_LEN // (2 * ROWS)
    blocks = short_blocks + long_blocks
    core = lax.axis_index("tensor") % 2
    meta = (core.astype(jnp.int32).reshape(1), short_len, long_len, short_count, long_count)

    def swap(values, bit):
        size = lax.axis_size("tensor")
        return lax.ppermute(values, "tensor", [(i, i ^ bit) for i in range(size)])

    def gather(piece):
        across = swap(piece, 2)
        return (piece, swap(piece, 1), across, swap(across, 1))

    def placed(vector, slot):
        return jnp.pad(vector, (slot * head_width, d - (slot + 1) * head_width))

    biases = jnp.stack(
        [up_bias]
        + [placed(query_bias, j) for j in range(4)]
        + [placed(value_bias, j) for j in range(4)]
        + [jnp.zeros_like(up_bias)] * 7
    )
    piece = jnp.concatenate(
        [query_weight.T, key_weight.T, value_weight.T, output_weight, biases], axis=0
    )
    pieces = gather(piece)
    ups = gather(up_weight)
    downs = gather(down_weight)
    vec = jnp.stack(
        [output_bias, first_gain, first_shift, down_bias, second_gain, second_shift, down_bias, down_bias]
    ).astype(F32)

    out_rows, in_rows, down_grad, up_grad, out_grad, qkv_grad, sums_two, sums_up, sums_one = compute(
        meta, tokens, cotangent, pieces, ups, downs, vec, short_blocks, long_blocks
    )

    def whole_rows(own):
        other = swap(own, 1)
        own = own.reshape(blocks, 1, ROWS, d)
        other = other.reshape(blocks, 1, ROWS, d)
        is_long = (jnp.arange(blocks) >= short_blocks).astype(jnp.int32)
        mine_first = (core == is_long).reshape(blocks, 1, 1, 1)
        lead = jnp.where(mine_first, own, other)
        trail = jnp.where(mine_first, other, own)
        return jnp.concatenate([lead, trail], axis=1).reshape(2 * blocks * ROWS, d)

    layer_output = whole_rows(out_rows)
    input_grad = whole_rows(in_rows).astype(F32)

    def both(mine, partner):
        return (mine.astype(F32) + swap(partner, 1).astype(F32)).astype(BF16)

    def reduced(values):
        return lax.psum(values, "dp")

    grad_down = reduced(both(down_grad[0], down_grad[1])).astype(F32)
    grad_up = reduced(both(up_grad[0], up_grad[1])).astype(F32)
    grad_out = both(out_grad[:head_width], out_grad[head_width:])
    grad_qkv = both(qkv_grad[:, :head_width], qkv_grad[:, head_width:])
    shared = jnp.concatenate([sums_two[0:3], sums_one[0:3]], axis=0)
    shared = (shared + swap(shared, 1)).astype(BF16)
    mine = jnp.concatenate(
        [sums_up[0], sums_one[3, :head_width], sums_one[4, :head_width]]
    )
    partner = jnp.concatenate(
        [sums_up[1], sums_one[3, head_width : 2 * head_width], sums_one[4, head_width : 2 * head_width]]
    )
    split = both(mine, partner)
    small = jnp.concatenate([shared.reshape(-1), split])
    small = jnp.pad(small, (0, 16 * d - small.shape[0])).reshape(16, d)
    last = jnp.concatenate([grad_out, grad_qkv.reshape(3 * head_width, d), small], axis=0)
    last = reduced(last).astype(F32)
    w = head_width
    small = last[4 * w :].reshape(-1)
    grad_up_bias = small[6 * d : 7 * d]
    grad_query_bias = small[7 * d : 7 * d + w]
    grad_value_bias = small[7 * d + w : 7 * d + 2 * w]
    return (
        layer_output,
        input_grad,
        last[w : 2 * w].T,
        grad_query_bias,
        last[2 * w : 3 * w].T,
        last[3 * w : 4 * w].T,
        grad_value_bias,
        last[0:w],
        small[5 * d : 6 * d],
        small[3 * d : 4 * d],
        small[4 * d : 5 * d],
        grad_up,
        grad_up_bias,
        grad_down,
        small[2 * d : 3 * d],
        small[0:d],
        small[d : 2 * d],
    )


def solution(mesh):
    return jax.shard_map(
        per_device,
        mesh=mesh,
        in_specs=(
            P("dp", None),
            P("dp", None),
            P("dp"),
            P("dp"),
            P("dp"),
            P("dp"),
            P(None, "tensor"),
            P("tensor"),
            P(None, "tensor"),
            P(None, "tensor"),
            P("tensor"),
            P("tensor", None),
            P(),
            P(),
            P(),
            P(None, "tensor"),
            P("tensor"),
            P("tensor", None),
            P(),
            P(),
            P(),
        ),
        out_specs=(
            P("dp", None),
            P("dp", None),
            P(None, "tensor"),
            P("tensor"),
            P(None, "tensor"),
            P(None, "tensor"),
            P("tensor"),
            P("tensor", None),
            P(),
            P(),
            P(),
            P(None, "tensor"),
            P("tensor"),
            P("tensor", None),
            P(),
            P(),
            P(),
        ),
        check_vma=False,
    )
```

```python
import functools

import jax
import jax.numpy as jnp
from jax import lax
from jax.experimental import pallas as pl
from jax.experimental.pallas import tpu as pltpu
from jax.sharding import PartitionSpec as P

HEAD_DIM = 64
SHORT_LEN = 128
LONG_LEN = 512
ROWS = 512
SLOTS = ROWS // SHORT_LEN
PAIR = 2 * HEAD_DIM
MASKED = -30000.0
F32 = jnp.float32
BF16 = jnp.bfloat16
VMEM_LIMIT = 62 * 1024 * 1024


def nn(left, right):
    return lax.dot_general(left, right, (((1,), (0,)), ((), ())), preferred_element_type=F32)


def nt(left, right):
    return lax.dot_general(left, right, (((1,), (1,)), ((), ())), preferred_element_type=F32)


def tn(left, right):
    return lax.dot_general(left, right, (((0,), (0,)), ((), ())), preferred_element_type=F32)


def fold_rows(values):
    return jnp.sum(values.reshape(-1, 8, values.shape[-1]), axis=0)


def total_rows(values):
    return jnp.sum(values, axis=0, keepdims=True)


def half_mask(which):
    lanes = lax.broadcasted_iota(jnp.int32, (1, PAIR), 1)
    return (lanes >= HEAD_DIM) if which else (lanes < HEAD_DIM)


def short_valid(meta, block, slot):
    index = SLOTS * (2 * block + meta[0][0]) + slot
    return jnp.where(index < meta[3][0], meta[1][index], 0)


def long_valid(meta, block, short_blocks):
    index = 2 * (block - short_blocks) + 1 - meta[0][0]
    return jnp.where(index < meta[4][0], meta[2][index], 0)


def norm_rows(values):
    centre = values - jnp.mean(values, axis=-1, keepdims=True)
    scale = lax.rsqrt(jnp.mean(centre * centre, axis=-1, keepdims=True) + 1e-12)
    return centre * scale, scale


def norm_back(incoming, normed, scale, gain):
    grad = incoming * gain
    inner = grad - jnp.mean(grad, axis=-1, keepdims=True)
    inner = inner - normed * jnp.mean(grad * normed, axis=-1, keepdims=True)
    return scale * inner


def load_attention_weights(pieces, wqkv, wout, bias, sems):
    width = wqkv.shape[0] // 6
    copies = []
    for j, piece in enumerate(pieces):
        for k in range(3):
            copies.append(
                (piece.at[pl.ds(k * width, width)], wqkv.at[pl.ds((2 * k + j) * width, width)])
            )
        copies.append((piece.at[pl.ds(3 * width, width)], wout.at[pl.ds(j * width, width)]))
        copies.append((piece.at[pl.ds(4 * width, 16)], bias.at[pl.ds(16 * j, 16)]))
    started = [pltpu.make_async_copy(s, d, sems.at[n]) for n, (s, d) in enumerate(copies)]
    for copy in started:
        copy.start()
    for copy in started:
        copy.wait()


def flat_row(ref):
    return ref[...].astype(F32).reshape(1, ref.shape[0])


def pack_kernel(at, wq, wk, wv, wo, qb, vb, ub, ob, g1, s1, db, g2, s2, piece, vec, wide):
    width = wq.shape[0]
    d = piece.shape[1]
    piece[0:width] = wq[...]
    piece[width : 2 * width] = wk[...]
    piece[2 * width : 3 * width] = wv[...]
    piece[3 * width : 4 * width] = wo[...]
    index = lax.broadcasted_iota(jnp.int32, (16, 1), 0)
    wide[...] = jnp.zeros_like(wide)
    wide[0:1, 0:width] = flat_row(qb)
    wide[1:2, 0:width] = flat_row(vb)
    row_q, row_v, row_u = wide[0:1], wide[1:2], flat_row(ub)
    lead = jnp.where(lax.broadcasted_iota(jnp.int32, (1, d), 1) < d // 2, row_u, 0.0)
    trail = pltpu.roll(row_u - lead, d // 2, 1)
    mine = jnp.where(at[0] == 0, lead, trail)
    far = jnp.where(at[0] == 0, trail, lead)
    rows = [row_u, row_q, pltpu.roll(row_q, width, 1), row_v, pltpu.roll(row_v, width, 1)]
    block = jnp.zeros((16, d), F32)
    for n, row in enumerate(rows + [None] * 4 + [mine, far]):
        if row is not None:
            block = jnp.where(index == n, row, block)
    piece[4 * width : 4 * width + 16] = block.astype(BF16)
    for n, row in enumerate((ob, g1, s1, db, g2, s2)):
        vec[n : n + 1] = flat_row(row)
    vec[6:8] = jnp.zeros((2, d), F32)


def place_kernel(core, other, whole, out):
    out[...] = other[...].astype(out.dtype)


def route_halves_kernel(at, mine, partner, keep, send):
    half = keep.shape[0]
    for out, which in ((keep, at[0]), (send, 1 - at[0])):
        span = pl.ds(pl.multiple_of(which * half, 16), half)
        out[...] = (mine[span].astype(F32) + partner[span].astype(F32)).astype(BF16)


def route_quarters_kernel(at, keep, other, *outs):
    size = outs[0].shape[0]
    for k, out in enumerate(outs):
        span = pl.ds(pl.multiple_of((at[0] ^ k) * size, 16), size)
        out[...] = (keep[span].astype(F32) + other[span].astype(F32)).astype(BF16)


def add_kernel(at, *refs):
    total = refs[0][...].astype(F32)
    for ref in refs[1:-1]:
        total = total + ref[...].astype(F32)
    refs[-1][...] = total.astype(BF16)


def join_kernel(at, *refs):
    out = refs[-1]
    size = refs[0].shape[0]
    for k, ref in enumerate(refs[:-1]):
        out[pl.ds(pl.multiple_of((at[0] ^ k) * size, 16), size)] = ref[...].astype(out.dtype)


def finish_kernel(at, own, other, *refs):
    outs, whole = refs[:-1], refs[-1]
    join_kernel(at, own, other, whole)
    start = 0
    for out in outs:
        out[...] = whole[start : start + out.shape[0]]
        start += out.shape[0]


def stacked(values):
    zero = jnp.zeros_like(values)
    return jnp.concatenate([jnp.where(half_mask(e), values, zero) for e in range(2)], axis=0)


def unstacked(values):
    size = values.shape[0] // 2
    return jnp.where(half_mask(0), values[:size], values[size:])


def attention_heads_forward(start, count, short_blocks, meta, x, weights, qkv, mixed, logs, stat):
    wqkv, bias = weights
    block = pl.program_id(0) + start
    half = mixed.shape[1]
    low = x[...]
    small = bias[...].astype(F32)
    query_bias = (small[1:2] + small[18:19])[:, 0:half]
    value_bias = (small[3:4] + small[20:21])[:, 0:half]
    qkv[:, 0:half] = (nt(low, wqkv[0:half]) + query_bias).astype(BF16)
    qkv[:, half : 2 * half] = nt(low, wqkv[half : 2 * half]).astype(BF16)
    qkv[:, 2 * half : 3 * half] = (nt(low, wqkv[2 * half : 3 * half]) + value_bias).astype(BF16)
    stat[...] = jnp.zeros_like(stat)
    lanes = lax.broadcasted_iota(jnp.int32, (1, 128), 1)

    def tiles(pair, spans):
        column = pl.multiple_of(pair * PAIR, PAIR)
        q, scores = [], []
        for query_at, queries, key_at, keys, valid in spans:
            part = qkv[query_at : query_at + queries, pl.ds(column, PAIR)] * jnp.asarray(0.125, BF16)
            key_part = qkv[key_at : key_at + keys, pl.ds(half + column, PAIR)]
            scores.append(nt(stacked(part), key_part))
        live = [lax.broadcasted_iota(jnp.int32, (1, t[3]), 1) < t[4] for t in spans]
        scores = [jnp.where(a, v, MASKED) for a, v in zip(live, scores)]
        top = [jnp.max(v, axis=-1, keepdims=True) for v in scores]
        weights = [jnp.exp(v - m) for v, m in zip(scores, top)]
        total = [jnp.sum(v, axis=-1, keepdims=True) for v in weights]
        out = [
            nn(v.astype(BF16), qkv[t[2] : t[2] + t[3], pl.ds(2 * half + column, PAIR)])
            for v, t in zip(weights, spans)
        ]
        for (query_at, queries, *_), m, n, v in zip(spans, top, total, out):
            log = m + jnp.log(n)
            rows = stat[query_at : query_at + queries]
            rows = jnp.where(lanes == 2 * pair, log[:queries], rows)
            stat[query_at : query_at + queries] = jnp.where(lanes == 2 * pair + 1, log[queries:], rows)
            mixed[query_at : query_at + queries, pl.ds(column, PAIR)] = unstacked(v * (1.0 / n)).astype(BF16)

    def short_path():
        spans = [
            (slot * SHORT_LEN, SHORT_LEN, slot * SHORT_LEN, SHORT_LEN, short_valid(meta, block, slot))
            for slot in range(SLOTS)
        ]

        def body(pair, carry):
            tiles(pair, spans)
            return carry

        lax.fori_loop(0, half // PAIR, body, 0)

    def long_path():
        valid = long_valid(meta, block, short_blocks)
        spans = [(part * 256, 256, 0, LONG_LEN, valid) for part in range(2)]

        def body(pair, carry):
            tiles(pair, spans)
            return carry

        lax.fori_loop(0, half // PAIR, body, 0)

    if start < short_blocks:
        pl.when(block < short_blocks)(short_path)
    if start + count > short_blocks:
        pl.when(block >= short_blocks)(long_path)
    logs[...] = stat[...].T[0:8]


def attention_forward_kernel(
    start, count, short_blocks, core, slen, llen, scount, lcount, x, a0, a1, qkv, mixed, logs,
    wqkv, wout, bias, sems, stat,
):
    @pl.when(pl.program_id(0) == 0)
    def _():
        load_attention_weights((a0, a1), wqkv, wout, bias, sems)

    meta = (core, slen, llen, scount, lcount)
    attention_heads_forward(start, count, short_blocks, meta, x, (wqkv, bias), qkv, mixed, logs, stat)


def attention_finish_kernel(
    start, count, short_blocks, core, slen, llen, scount, lcount, x, a2, a3, mixed_near, a0, a1, vec, *rest,
):
    qkv, mixed, logs, normed, scale_rows, wqkv, wout, bias, near_out, sems, stat = rest[-11:]

    @pl.when(pl.program_id(0) == 0)
    def _():
        width = near_out.shape[0] // 2
        near = [
            pltpu.make_async_copy(
                piece.at[pl.ds(3 * width, width)], near_out.at[pl.ds(j * width, width)], sems.at[10 + j]
            )
            for j, piece in enumerate((a0, a1))
        ]
        for copy in near:
            copy.start()
        load_attention_weights((a2, a3), wqkv, wout, bias, sems)
        for copy in near:
            copy.wait()

    meta = (core, slen, llen, scount, lcount)
    attention_heads_forward(start, count, short_blocks, meta, x, (wqkv, bias), qkv, mixed, logs, stat)
    hidden = x[...].astype(F32) + vec[0:1]
    hidden = hidden + nn(mixed_near[...], near_out[...]) + nn(mixed[...], wout[...])
    rows, scale = norm_rows(hidden)
    normed[...] = rows.astype(BF16)
    scale_rows[...] = jnp.broadcast_to(scale, scale_rows.shape)


def down_groups(side, downs):
    half = downs[0].shape[0] // 2
    spans = [pl.ds(pl.multiple_of(at * half, 16), half) for at in (side[0], 1 - side[0])]
    return [downs[0][...], downs[1][...]] + [downs[2 + j][span] for span in spans for j in range(2)]


def ffn_forward_kernel(short_blocks, core, slen, llen, scount, lcount, side, normed, cotangent, *rest):
    ups, downs, biases = rest[0:6], rest[6:10], rest[10:14]
    vec, layer_out, layer_rows, grad_low, slope, down_mine, down_partner, sums, active, down_sum, vec_sum = rest[14:]
    meta = (core, slen, llen, scount, lcount)
    block = pl.program_id(0)
    half = ups[2].shape[1]

    @pl.when(block == 0)
    def _():
        down_sum[...] = jnp.zeros_like(down_sum)
        vec_sum[...] = jnp.zeros_like(vec_sum)

    first = normed[...].astype(F32) * vec[1:2] + vec[2:3]
    first_low = first.astype(BF16)
    total = first + vec[3:4]
    at = 0
    for j, (up, down) in enumerate(zip(ups, down_groups(side, downs))):
        size = up.shape[1]
        if j < 2:
            bias = biases[j][0:1]
        else:
            bias = biases[2 + j % 2][9 + j // 4 : 10 + j // 4, 0:half]
        inner = nn(first_low, up[...]) + bias.astype(F32)
        chance = 0.5 * (1.0 + lax.erf(inner * 0.7071067811865476))
        units = (inner * chance).astype(BF16)
        slope[:, at : at + size] = (
            chance + inner * jnp.exp(-0.5 * inner * inner) * 0.3989422804014327
        ).astype(BF16)
        if j < 2:
            active[j] = units
        total = total + nn(units, down)
        at += size
    rows, scale = norm_rows(total)
    result = (rows * vec[4:5] + vec[5:6]).astype(BF16)
    layer_out[...] = result
    layer_rows[...] = result
    position = lax.broadcasted_iota(jnp.int32, (ROWS, 1), 0)
    slot = position // SHORT_LEN
    short_limit = jnp.zeros((ROWS, 1), jnp.int32)
    for n in range(SLOTS):
        short_limit = jnp.where(slot == n, short_valid(meta, jnp.minimum(block, short_blocks - 1), n), short_limit)
    long_limit = long_valid(meta, jnp.maximum(block, short_blocks), short_blocks)
    is_short = block < short_blocks
    alive = jnp.where(is_short, position % SHORT_LEN, position) < jnp.where(
        is_short, short_limit, long_limit
    )
    upstream = jnp.where(alive, cotangent[...].astype(F32), 0.0)
    grad = norm_back(upstream, rows, scale, vec[4:5])
    low = grad.astype(BF16)
    grad_low[...] = low
    vec_sum[0] += fold_rows(upstream * rows)
    vec_sum[1] += fold_rows(upstream)
    vec_sum[2] += fold_rows(grad)
    for j in range(2):
        down_sum[j] += tn(active[j], low)

    @pl.when(block == pl.num_programs(0) - 1)
    def _():
        down_mine[...] = down_sum[0].astype(BF16)
        down_partner[...] = down_sum[1].astype(BF16)
        sums[...] = jnp.zeros_like(sums)
        for n in range(3):
            sums[n : n + 1] = total_rows(vec_sum[n])


def ffn_backward_kernel(side, grad_low, slope, normed, stat, mixed, sums_two, *rest):
    ups, downs = rest[0:6], rest[6:10]
    vec, hidden_low, mine, partner, up_sum, out_sum, vec_sum, kept = rest[10:]
    block = pl.program_id(0)
    units = up_sum.shape[1]
    width = mixed.shape[1] // 2

    @pl.when(block == 0)
    def _():
        up_sum[...] = jnp.zeros_like(up_sum)
        out_sum[...] = jnp.zeros_like(out_sum)
        vec_sum[...] = jnp.zeros_like(vec_sum)

    low = grad_low[...]
    rows = normed[...].astype(F32)
    first_low = (rows * vec[1:2] + vec[2:3]).astype(BF16)
    total = low.astype(F32)
    at = 0
    for j, (up, down) in enumerate(zip(ups, down_groups(side, downs))):
        size = up.shape[1]
        inner = nt(low, down) * slope[:, at : at + size].astype(F32)
        inner_low = inner.astype(BF16)
        total = total + nt(inner_low, up[...])
        if j < 2:
            vec_sum[j] += fold_rows(inner)
            kept[j] = inner_low
        at += size
    for j in range(2):
        up_sum[j] += tn(first_low, kept[j])
    grad = norm_back(total, rows, stat[:, 0:1], vec[1:2])
    vec_sum[2] += fold_rows(total * rows)
    vec_sum[3] += fold_rows(total)
    vec_sum[4] += fold_rows(grad)
    grad_attn = grad.astype(BF16)
    hidden_low[...] = grad_attn
    out_sum[...] += tn(mixed[...], grad_attn)

    @pl.when(block == pl.num_programs(0) - 1)
    def _():
        index = lax.broadcasted_iota(jnp.int32, (16, 1), 0)
        shared = [sums_two[n : n + 1] for n in range(3)] + [total_rows(vec_sum[n]) for n in range(2, 5)]
        for j, out in enumerate((mine, partner)):
            out[0:units] = up_sum[j].astype(BF16)
            out[units : units + width] = out_sum[j * width : (j + 1) * width].astype(BF16)
            out[units + width :] = jnp.zeros((out.shape[0] - units - width, out.shape[1]), BF16)
            rows_out = jnp.zeros((16, out.shape[1]), F32)
            for n, row in enumerate(shared + [total_rows(vec_sum[j])]):
                rows_out = jnp.where(index == n, row, rows_out)
            out[units + width : units + width + 16] = rows_out.astype(BF16)


def attention_heads_backward(start, short_blocks, meta, logs, qkv, mixed, mixed_grad, low_qkv, delta):
    block = pl.program_id(0) + start
    half = mixed.shape[1]
    own = (mixed_grad[...].astype(F32) * mixed[...].astype(F32)).astype(BF16)
    head = lax.broadcasted_iota(jnp.int32, (8, half), 1) // HEAD_DIM
    pick = jnp.where(head == lax.broadcasted_iota(jnp.int32, (8, half), 0), 1.0, 0.0)
    delta[...] = nt(pick.astype(BF16), own)

    index = lax.broadcasted_iota(jnp.int32, (8, 1), 0)

    def tiles(pair, size, valids):
        column = pl.multiple_of(pair * PAIR, PAIR)
        spans = [pl.ds(n * size, size) for n in range(len(valids))]

        def rows(ref, span):
            picked = [total_rows(jnp.where(index == 2 * pair + e, ref[:, span], 0.0)) for e in range(2)]
            return jnp.concatenate(picked, axis=1)

        q = [stacked(qkv[t, pl.ds(column, PAIR)] * jnp.asarray(0.125, BF16)) for t in spans]
        g = [stacked(mixed_grad[t, pl.ds(column, PAIR)]) for t in spans]
        k = [qkv[t, pl.ds(half + column, PAIR)] for t in spans]
        scores = [nt(b, a) for a, b in zip(q, k)]
        grads = [nt(qkv[t, pl.ds(2 * half + column, PAIR)], a) for t, a in zip(spans, g)]
        place = lax.broadcasted_iota(jnp.int32, (size, 1), 0)
        probs = [
            jnp.where(place < valid, jnp.exp(v - rows(logs, t)), 0.0)
            for v, t, valid in zip(scores, spans, valids)
        ]
        scores = [(p * (v - rows(delta, t))).astype(BF16) for p, v, t in zip(probs, grads, spans)]
        dq = [tn(v, b) for v, b in zip(scores, k)]
        dk = [nn(v, a) for v, a in zip(scores, q)]
        dv = [nn(p.astype(BF16), a) for p, a in zip(probs, g)]
        for t, a, b, c in zip(spans, dq, dk, dv):
            low_qkv[t, pl.ds(column, PAIR)] = (unstacked(a) * 0.125).astype(BF16)
            low_qkv[t, pl.ds(half + column, PAIR)] = b.astype(BF16)
            low_qkv[t, pl.ds(2 * half + column, PAIR)] = c.astype(BF16)

    if start < short_blocks:
        valids = [short_valid(meta, block, slot) for slot in range(SLOTS)]
        size = SHORT_LEN
    else:
        valids = [long_valid(meta, block, short_blocks)]
        size = LONG_LEN

    def body(pair, carry):
        tiles(pair, size, valids)
        return carry

    lax.fori_loop(0, half // PAIR, body, 0)


def attention_backward_kernel(
    start, short_blocks, core, slen, llen, scount, lcount, hidden_low, stat, qkv, mixed, x,
    a0, a1, *rest,
):
    if start:
        sums_in, vec_in, low_qkv, mine, partner = rest[:5]
    else:
        low_qkv, qkv_out, vec_out = rest[:3]
    wqkv, wout, bias, sems, mixed_grad, delta, qkv_sum, vec_sum = rest[-8:]
    meta = (core, slen, llen, scount, lcount)
    block = pl.program_id(0)
    half = mixed.shape[1]
    width = half // 2

    @pl.when(block == 0)
    def _():
        load_attention_weights((a0, a1), wqkv, wout, bias, sems)
        if start:
            qkv_sum[...] = sums_in[...]
            vec_sum[...] = vec_in[...]
        else:
            qkv_sum[...] = jnp.zeros_like(qkv_sum)
            vec_sum[...] = jnp.zeros_like(vec_sum)

    mixed_grad[...] = nt(hidden_low[...], wout[...]).astype(BF16)
    attention_heads_backward(start, short_blocks, meta, stat, qkv, mixed, mixed_grad, low_qkv, delta)
    vec_sum[0] += fold_rows(low_qkv[:, 0:half].astype(F32))
    vec_sum[1] += fold_rows(low_qkv[:, 2 * half : 3 * half].astype(F32))
    for k in range(3):
        qkv_sum[k] += tn(low_qkv[:, k * half : (k + 1) * half], x[...])

    @pl.when(block == pl.num_programs(0) - 1)
    def _():
        if not start:
            qkv_out[...] = qkv_sum[...]
            vec_out[...] = vec_sum[...]
        else:
            index = lax.broadcasted_iota(jnp.int32, (16, 1), 0)
            heads = [total_rows(vec_sum[n]) for n in range(2)]
            for j, out in enumerate((mine, partner)):
                for k in range(3):
                    out[k * width : (k + 1) * width] = qkv_sum[k, j * width : (j + 1) * width].astype(BF16)
                out[3 * width :] = jnp.zeros((out.shape[0] - 3 * width, out.shape[1]), BF16)
                rows_out = jnp.zeros((16, half), F32)
                for n, row in enumerate(heads):
                    row = pltpu.roll(row, half - width, 1) if j else row
                    rows_out = jnp.where(index == n, row, rows_out)
                out[3 * width : 3 * width + 16, 0:half] = rows_out.astype(BF16)


def attention_input_kernel(
    start, short_blocks, core, slen, llen, scount, lcount, hidden_low, stat, qkv, mixed, low_near,
    a2, a3, a0, a1, *rest,
):
    input_rows, input_grad = rest[-10:-8]
    wqkv, wout, bias, near_qkv, sems, low_qkv, mixed_grad, delta = rest[-8:]
    meta = (core, slen, llen, scount, lcount)

    @pl.when(pl.program_id(0) == 0)
    def _():
        width = near_qkv.shape[0] // 6
        near = [
            pltpu.make_async_copy(
                piece.at[pl.ds(k * width, width)],
                near_qkv.at[pl.ds((2 * k + j) * width, width)],
                sems.at[10 + 2 * k + j],
            )
            for k in range(3)
            for j, piece in enumerate((a0, a1))
        ]
        for copy in near:
            copy.start()
        load_attention_weights((a2, a3), wqkv, wout, bias, sems)
        for copy in near:
            copy.wait()

    low = hidden_low[...]
    mixed_grad[...] = nt(low, wout[...]).astype(BF16)
    attention_heads_backward(start, short_blocks, meta, stat, qkv, mixed, mixed_grad, low_qkv, delta)
    total = low.astype(F32) + nn(low_near[...], near_qkv[...]) + nn(low_qkv[...], wqkv[...])
    input_rows[...] = total.astype(BF16)
    input_grad[...] = total


def const_spec(shape):
    return pl.BlockSpec(
        shape, lambda *_: (0,) * len(shape), pipeline_mode=pl.Buffered(1)
    )


def any_spec():
    return pl.BlockSpec(memory_space=pl.ANY)


def own_spec(width, start=0):
    return pl.BlockSpec((ROWS, width), lambda i, *_: (i + start, 0))


def whole_call(body, name, which, operands, shapes, scratch=()):
    inner = pltpu.VMEM
    moved = sum(v.size * v.dtype.itemsize for v in list(operands) + list(shapes))
    return pl.pallas_call(
        body,
        name=name,
        in_specs=[pl.BlockSpec(memory_space=pltpu.SMEM)] + [pl.BlockSpec(memory_space=inner)] * len(operands),
        out_specs=[pl.BlockSpec(memory_space=inner)] * len(shapes),
        out_shape=shapes,
        scratch_shapes=list(scratch),
        cost_estimate=pl.CostEstimate(flops=0, bytes_accessed=moved, transcendentals=0),
    )(which, *operands)


def spread(body, name, grid, in_specs, out_specs, out_shape, scratch=(), prefetch=0, flops=0, moved=0, exps=0, alias=None):
    return pl.pallas_call(
        body,
        name=name,
        grid_spec=pltpu.PrefetchScalarGridSpec(
            num_scalar_prefetch=prefetch,
            grid=grid,
            in_specs=in_specs,
            out_specs=out_specs,
            scratch_shapes=list(scratch),
        ),
        out_shape=out_shape,
        input_output_aliases=alias or {},
        compiler_params=pltpu.CompilerParams(
            dimension_semantics=("arbitrary",), vmem_limit_bytes=VMEM_LIMIT
        ),
        cost_estimate=pl.CostEstimate(flops=flops, bytes_accessed=moved, transcendentals=exps),
    )


def per_device(
    tokens,
    cotangent,
    short_len,
    long_len,
    short_count,
    long_count,
    query_weight,
    query_bias,
    key_weight,
    value_weight,
    value_bias,
    output_weight,
    output_bias,
    first_gain,
    first_shift,
    up_weight,
    up_bias,
    down_weight,
    down_bias,
    second_gain,
    second_shift,
):
    d = tokens.shape[1]
    width = query_weight.shape[1]
    units = up_weight.shape[1]
    half = 2 * width
    piece_rows = 4 * width + 16
    short_blocks = short_len.shape[0] * SHORT_LEN // (2 * ROWS)
    long_blocks = long_len.shape[0] * LONG_LEN // (2 * ROWS)
    blocks = short_blocks + long_blocks
    rows = blocks * ROWS
    core = lax.axis_index("tensor") % 2
    side = lax.axis_index("dp") % 2
    core_id = core.astype(jnp.int32).reshape(1)
    meta = (core_id, short_len, long_len, short_count, long_count)
    sds = jax.ShapeDtypeStruct

    def swap(values, bit, axis="tensor"):
        size = lax.axis_size(axis)
        return lax.ppermute(values, axis, [(i, i ^ bit) for i in range(size)])

    def after(value, *others):
        return lax.optimization_barrier((value,) + others)[0]

    def global_spec(start=0, flip=0):
        def index(i, core, *_):
            i = i + start
            first = core[0] if flip == 0 else 1 - core[0]
            return (2 * i + jnp.where(i < short_blocks, first, 1 - first), 0)

        return pl.BlockSpec((ROWS, d), index)

    vec_spec = const_spec((8, d))
    row_spec = own_spec(d)

    side_id = side.astype(jnp.int32).reshape(1)
    line_id = (lax.axis_index("dp") // 2).astype(jnp.int32).reshape(1)
    vectors = [query_bias, value_bias, up_bias, output_bias, first_gain, first_shift,
               down_bias, second_gain, second_shift]
    a0, vec = whole_call(
        pack_kernel, "pack", side_id,
        [query_weight.T, key_weight.T, value_weight.T, output_weight, *vectors],
        [sds((piece_rows, d), BF16), sds((8, d), F32)], [pltpu.VMEM((8, d), F32)],
    )
    up_split = lax.dynamic_slice_in_dim(up_weight, side * (units // 2), units // 2, 1)
    def boundary(lead, *values):
        out = lax.optimization_barrier((lead,) + values)
        return out[0], list(out[1:])

    a1 = swap(a0, 1)
    a2 = swap(a0, 2)

    weight_scratch = [
        pltpu.VMEM((3 * half, d), BF16),
        pltpu.VMEM((half, d), BF16),
        pltpu.VMEM((32, d), BF16),
    ]
    sems = pltpu.SemaphoreType.DMA((16,))
    stat_scratch = pltpu.VMEM((ROWS, 128), F32)

    def log_spec(start=0):
        return pl.BlockSpec((8, ROWS), lambda i, *_: (i + start, 0))

    head_shapes = [sds((rows, 3 * half), BF16), sds((rows, half), BF16), sds((8 * blocks, ROWS), F32)]
    head_flops = 2 * rows * d * 3 * half + 4 * rows * 320 * half
    qkv_near, mixed_near, stat_near = spread(
        functools.partial(attention_forward_kernel, 0, blocks, short_blocks), "attention_near", (blocks,),
        [global_spec()] + [any_spec()] * 2, [own_spec(3 * half), own_spec(half), log_spec()], head_shapes,
        weight_scratch + [sems, stat_scratch], 5,
        head_flops, rows * d * 8, rows * 320 * 6,
    )(*meta, tokens, a0, a1)

    stat_near, (a2,) = boundary(stat_near, a2)
    a3 = swap(a2, 1)
    a3, (u2, d2, up_near) = boundary(a3, up_split, down_weight, up_weight)
    u2 = swap(u2, 2)
    d2 = swap(d2, 2)
    u1 = swap(up_near, 1)

    def far_forward(start, count, extra, alias):
        return spread(
            functools.partial(attention_finish_kernel, start, count, short_blocks), "attention_far", (count,),
            [global_spec(start)] + [any_spec()] * 2 + [own_spec(half, start)] + [any_spec()] * 2 + [vec_spec]
            + [any_spec()] * len(extra),
            [own_spec(3 * half, start), own_spec(half, start), log_spec(start), own_spec(d, start), own_spec(128, start)],
            head_shapes + [sds((rows, d), BF16), sds((rows, 128), F32)],
            weight_scratch + [pltpu.VMEM((half, d), BF16), sems, stat_scratch], 5,
            (head_flops + 2 * rows * d * d) * count // blocks, count * ROWS * d * 10, count * ROWS * 320 * 6, alias,
        )(*meta, tokens, a2, a3, mixed_near, a0, a1, vec, *extra)

    far = list(far_forward(0, short_blocks, [], None))
    far[3], (u2, u1, down_near) = boundary(far[3], u2, u1, down_weight)
    u4 = swap(u2, 1, "dp")
    u3, d1 = swap(u2, 1), swap(down_near, 1)
    qkv_far, mixed_far, stat_far, normed, scale_one = far_forward(
        short_blocks, long_blocks, far, {12 + n: n for n in range(5)}
    )
    normed, (u4, u3, d2, d1) = boundary(normed, u4, u3, d2, d1)
    u5, d3 = swap(u4, 1), swap(d2, 1)
    ups = (up_weight, u1, u2, u3, u4, u5)
    downs = (down_weight, d1, d2, d3)
    bias_spec = pl.BlockSpec((16, d), lambda *_: (4 * width // 16, 0), pipeline_mode=pl.Buffered(1))
    up_specs = [const_spec(v.shape) for v in ups]
    down_specs = [const_spec(v.shape) for v in downs]
    whole_out, out_rows, grad_low, slope, down_mine, down_partner, sums_two = spread(
        functools.partial(ffn_forward_kernel, short_blocks), "ffn_forward", (blocks,),
        [row_spec, global_spec()] + up_specs + down_specs + [bias_spec] * 4 + [vec_spec],
        [global_spec(), row_spec, row_spec, own_spec(4 * units)] + [const_spec((units, d))] * 2 + [vec_spec],
        [sds((2 * rows, d), BF16), sds((rows, d), BF16), sds((rows, d), BF16), sds((rows, 4 * units), BF16)]
        + [sds((units, d), BF16)] * 2 + [sds((8, d), F32)],
        [pltpu.VMEM((2, ROWS, units), BF16), pltpu.VMEM((2, units, d), F32), pltpu.VMEM((3, 8, d), F32)],
        6, 2 * rows * d * 10 * units, rows * d * 20, rows * 8 * units,
    )(*meta, side_id, normed, cotangent, *ups, *downs, a0, a1, a2, a3, vec)

    custom = lax.axis_size("dp") == 8

    class Reduction:
        def __init__(self, mine, partner):
            self.mine, self.size = mine, mine.shape[0]
            self.moved = [swap(partner, 1)]
            self.stage = 0

        def part(self, count):
            return sds((self.size // count, d), BF16)

        def step(self):
            got = self.moved
            stage, self.stage = self.stage, self.stage + 1
            if not custom:
                if stage == 0:
                    total = (self.mine.astype(F32) + got[0].astype(F32)).astype(BF16)
                    self.moved = [lax.psum(total, "dp")]
                return self.moved[0]
            if stage == 0:
                self.keep, send = whole_call(
                    route_halves_kernel, "halves", side_id, [self.mine, got[0]], [self.part(2)] * 2
                )
                sent, self.moved = [send], [swap(send, 1, "dp")]
            elif stage == 1:
                self.keep, *sent = whole_call(
                    route_quarters_kernel, "quarters", line_id, [self.keep, got[0]], [self.part(8)] * 4
                )
                self.moved = [swap(v, 2 * (k + 1), "dp") for k, v in enumerate(sent)]
            elif stage == 2:
                (self.keep,) = whole_call(add_kernel, "add", line_id, [self.keep, *got], [self.part(8)])
                sent = [self.keep]
                self.moved = [swap(self.keep, 2 * k, "dp") for k in (1, 2, 3)]
            elif stage == 3:
                (self.keep,) = whole_call(
                    join_kernel, "join_quarters", line_id, [self.keep, *got], [self.part(2)]
                )
                sent, self.moved = [self.keep], [swap(self.keep, 1, "dp")]
            return sent[0]

        def finish(self, *sizes):
            shapes = [sds((n, d), F32) for n in sizes]
            if not custom:
                total = self.moved[0].astype(F32)
                cuts = [sum(sizes[:n]) for n in range(len(sizes))]
                return [total[at : at + n] for at, n in zip(cuts, sizes)]
            operands = [self.keep, self.moved[0]]
            return whole_call(
                finish_kernel, "finish", side_id, operands, shapes, [pltpu.VMEM((self.size, d), F32)]
            )

    def settle(lead, reductions, *extra):
        lead, values = boundary(lead, *[v for r in reductions for v in r.moved], *extra)
        for r in reductions:
            count = len(r.moved)
            r.moved, values = values[:count], values[count:]
        return (lead, *values)

    grad_low, down_mine, down_partner = lax.optimization_barrier((grad_low, down_mine, down_partner))
    down_reduce = Reduction(down_mine, down_partner)
    tie = down_reduce.step()
    grad_low = after(grad_low, tie)
    moved_out = swap(after(out_rows, tie), 1)

    pack_rows = units + width + 64
    hidden_low, mine, partner = spread(
        ffn_backward_kernel, "ffn_backward", (blocks,),
        [row_spec, own_spec(4 * units), row_spec, own_spec(128), own_spec(half), vec_spec]
        + up_specs + down_specs + [vec_spec],
        [row_spec] + [const_spec((pack_rows, d))] * 2,
        [sds((rows, d), BF16)] + [sds((pack_rows, d), BF16)] * 2,
        [pltpu.VMEM((2, d, units), F32), pltpu.VMEM((half, d), F32), pltpu.VMEM((5, 8, d), F32),
         pltpu.VMEM((2, ROWS, units), BF16)],
        1, 2 * rows * d * 10 * units, rows * d * 16, 0,
    )(side_id, grad_low, slope, normed, scale_one, mixed_near, sums_two, *ups, *downs, vec)
    hidden_low, mine, partner, moved_out = settle(hidden_low, [down_reduce], mine, partner, moved_out)
    tie = down_reduce.step()
    partner = after(partner, tie)
    up_reduce = Reduction(mine, partner)
    tie = up_reduce.step()
    hidden_low = after(hidden_low, tie)

    qkv_rows = 3 * width + 64
    sums = [sds((3, half, d), F32), sds((2, 8, half), F32)]
    sum_specs = [const_spec(v.shape) for v in sums]

    def near_backward(start, count, extra, extra_specs, outs, out_specs, alias):
        return spread(
            functools.partial(attention_backward_kernel, start, short_blocks), "attention_near_backward", (count,),
            [own_spec(d, start), log_spec(start), own_spec(3 * half, start), own_spec(half, start), global_spec(start)]
            + [any_spec()] * 2 + extra_specs,
            [own_spec(3 * half)] + out_specs,
            [sds((count * ROWS, 3 * half), BF16)] + outs,
            weight_scratch + [sems, pltpu.VMEM((ROWS, half), BF16), pltpu.VMEM((8, ROWS), F32),
                              pltpu.VMEM((3, half, d), F32), pltpu.VMEM((2, 8, half), F32)],
            5, count * ROWS * (10 * d * half + 3200 * half), count * ROWS * d * 16, count * ROWS * 320 * 6,
        )(*meta, hidden_low, stat_near, qkv_near, mixed_near, tokens, a0, a1, *extra)

    low_short, *sums_short = near_backward(0, short_blocks, [], [], sums, sum_specs, None)
    (low_short,) = settle(low_short, [down_reduce, up_reduce])
    tie = down_reduce.step()
    tie_two = up_reduce.step()
    sums_short[1] = after(sums_short[1], tie, tie_two)
    low_long, mine, partner = near_backward(
        short_blocks, long_blocks, sums_short, sum_specs,
        [sds((qkv_rows, d), BF16)] * 2, [const_spec((qkv_rows, d))] * 2, None,
    )
    low_long, mine, partner = settle(low_long, [down_reduce, up_reduce], mine, partner)
    ties = [down_reduce.step(), up_reduce.step()]
    qkv_reduce = Reduction(mine, after(partner, *ties))
    ties += [qkv_reduce.step()]

    def far_backward(start, count, low_near, extra, alias):
        return spread(
            functools.partial(attention_input_kernel, start, short_blocks), "attention_far_backward", (count,),
            [own_spec(d, start), log_spec(start), own_spec(3 * half, start), own_spec(half, start), own_spec(3 * half)]
            + [any_spec()] * (4 + len(extra)),
            [row_spec, global_spec(start)], [sds((count * ROWS, d), BF16), sds((2 * rows, d), F32)],
            weight_scratch + [pltpu.VMEM((3 * half, d), BF16), sems, pltpu.VMEM((ROWS, 3 * half), BF16),
                              pltpu.VMEM((ROWS, half), BF16), pltpu.VMEM((8, ROWS), F32)],
            5, count * ROWS * (14 * d * half + 3200 * half), count * ROWS * d * 16, count * ROWS * 320 * 6, alias,
        )(*meta, hidden_low, stat_far, qkv_far, mixed_far, low_near, a2, a3, a0, a1, *extra)

    low_short = after(low_short, *ties)
    rows_short, whole_in = far_backward(0, short_blocks, low_short, [], None)
    (rows_short,) = settle(rows_short, [down_reduce, up_reduce, qkv_reduce])
    ties = [up_reduce.step(), qkv_reduce.step()]
    (grad_down,) = down_reduce.finish(units)
    moved_short = swap(after(rows_short, *ties), 1)
    low_long = after(low_long, *ties, grad_down)
    rows_long, whole_in = far_backward(short_blocks, long_blocks, low_long, [whole_in], {14: 1})
    rows_long, moved_short = settle(rows_long, [up_reduce, qkv_reduce], moved_short)
    tie = qkv_reduce.step()
    moved_long = swap(after(rows_long, tie), 1)

    def place(whole, other, start, count):
        return spread(
            place_kernel, "place", (count,), [own_spec(d), any_spec()], global_spec(start, 1),
            sds(whole.shape, whole.dtype), (), 1, 0, other.size * 6, 0, {2: 0},
        )(core_id, other, whole)

    layer_output = place(whole_out, after(moved_out, tie), 0, blocks)
    input_grad = place(whole_in, after(moved_short, tie), 0, short_blocks)
    layer_output, input_grad, moved_long = settle(layer_output, [qkv_reduce], input_grad, moved_long)
    tie = qkv_reduce.step()
    input_grad = place(input_grad, after(moved_long, tie), short_blocks, long_blocks)
    up_reduce.moved[0] = after(up_reduce.moved[0], tie)
    grad_up, grad_out, small = up_reduce.finish(units, width, 16)
    grad_up, input_grad = settle(grad_up, [qkv_reduce], input_grad)
    grad_query, grad_key, grad_value, heads = qkv_reduce.finish(width, width, width, 16)
    return (
        layer_output,
        input_grad,
        grad_query.T,
        heads[0, :width],
        grad_key.T,
        grad_value.T,
        heads[1, :width],
        grad_out,
        small[5],
        small[3],
        small[4],
        grad_up,
        small[6],
        grad_down,
        small[2],
        small[0],
        small[1],
    )

def solution(mesh):
    return jax.shard_map(
        per_device,
        mesh=mesh,
        in_specs=(
            P("dp", None),
            P("dp", None),
            P("dp"),
            P("dp"),
            P("dp"),
            P("dp"),
            P(None, "tensor"),
            P("tensor"),
            P(None, "tensor"),
            P(None, "tensor"),
            P("tensor"),
            P("tensor", None),
            P(),
            P(),
            P(),
            P(None, "tensor"),
            P("tensor"),
            P("tensor", None),
            P(),
            P(),
            P(),
        ),
        out_specs=(
            P("dp", None),
            P("dp", None),
            P(None, "tensor"),
            P("tensor"),
            P(None, "tensor"),
            P(None, "tensor"),
            P("tensor"),
            P("tensor", None),
            P(),
            P(),
            P(),
            P(None, "tensor"),
            P("tensor"),
            P("tensor", None),
            P(),
            P(),
            P(),
        ),
        check_vma=False,
    )
```

```python
import functools

import jax
import jax.numpy as jnp
from jax import lax
from jax.experimental import pallas as pl
from jax.experimental.pallas import tpu as pltpu
from jax.sharding import PartitionSpec as P

HEAD_DIM = 64
SHORT_LEN = 128
LONG_LEN = 512
ROWS = 512
SLOTS = ROWS // SHORT_LEN
PAIR = 2 * HEAD_DIM
MASKED = -30000.0
F32 = jnp.float32
BF16 = jnp.bfloat16
VMEM_LIMIT = 60 * 1024 * 1024


def nn(left, right):
    return lax.dot_general(left, right, (((1,), (0,)), ((), ())), preferred_element_type=F32)


def nt(left, right):
    return lax.dot_general(left, right, (((1,), (1,)), ((), ())), preferred_element_type=F32)


def tn(left, right):
    return lax.dot_general(left, right, (((0,), (0,)), ((), ())), preferred_element_type=F32)


def fold_rows(values):
    return jnp.sum(values.reshape(-1, 8, values.shape[-1]), axis=0)


def total_rows(values):
    return jnp.sum(values, axis=0, keepdims=True)


def half_mask(which):
    lanes = lax.broadcasted_iota(jnp.int32, (1, PAIR), 1)
    return (lanes >= HEAD_DIM) if which else (lanes < HEAD_DIM)


def short_valid(meta, block, slot):
    index = SLOTS * (2 * block + meta[0][0]) + slot
    return jnp.where(index < meta[3][0], meta[1][index], 0)


def long_valid(meta, block, short_blocks):
    index = 2 * (block - short_blocks) + 1 - meta[0][0]
    return jnp.where(index < meta[4][0], meta[2][index], 0)


def norm_rows(values):
    centre = values - jnp.mean(values, axis=-1, keepdims=True)
    scale = lax.rsqrt(jnp.mean(centre * centre, axis=-1, keepdims=True) + 1e-12)
    return centre * scale, scale


def norm_back(incoming, normed, scale, gain):
    grad = incoming * gain
    inner = grad - jnp.mean(grad, axis=-1, keepdims=True)
    inner = inner - normed * jnp.mean(grad * normed, axis=-1, keepdims=True)
    return scale * inner


def load_attention_weights(pieces, wqkv, wout, bias, sems):
    width = wqkv.shape[0] // 6
    copies = []
    for j, piece in enumerate(pieces):
        for k in range(3):
            copies.append(
                (piece.at[pl.ds(k * width, width)], wqkv.at[pl.ds((2 * k + j) * width, width)])
            )
        copies.append((piece.at[pl.ds(3 * width, width)], wout.at[pl.ds(j * width, width)]))
        copies.append((piece.at[pl.ds(4 * width, 16)], bias.at[pl.ds(16 * j, 16)]))
    started = [pltpu.make_async_copy(s, d, sems.at[n]) for n, (s, d) in enumerate(copies)]
    for copy in started:
        copy.start()
    for copy in started:
        copy.wait()


def flat_row(ref):
    return ref[...].astype(F32).reshape(1, ref.shape[0])


def pack_kernel(at, wq, wk, wv, wo, qb, vb, ub, ob, g1, s1, db, g2, s2, piece, vec, wide):
    width = wq.shape[0]
    d = piece.shape[1]
    piece[0:width] = wq[...]
    piece[width : 2 * width] = wk[...]
    piece[2 * width : 3 * width] = wv[...]
    piece[3 * width : 4 * width] = wo[...]
    index = lax.broadcasted_iota(jnp.int32, (16, 1), 0)
    wide[...] = jnp.zeros_like(wide)
    wide[0:1, 0:width] = flat_row(qb)
    wide[1:2, 0:width] = flat_row(vb)
    row_q, row_v, row_u = wide[0:1], wide[1:2], flat_row(ub)
    lead = jnp.where(lax.broadcasted_iota(jnp.int32, (1, d), 1) < d // 2, row_u, 0.0)
    trail = pltpu.roll(row_u - lead, d // 2, 1)
    mine = jnp.where(at[0] == 0, lead, trail)
    far = jnp.where(at[0] == 0, trail, lead)
    rows = [row_u, row_q, pltpu.roll(row_q, width, 1), row_v, pltpu.roll(row_v, width, 1)]
    block = jnp.zeros((16, d), F32)
    for n, row in enumerate(rows + [None] * 4 + [mine, far]):
        if row is not None:
            block = jnp.where(index == n, row, block)
    piece[4 * width : 4 * width + 16] = block.astype(BF16)
    for n, row in enumerate((ob, g1, s1, db, g2, s2)):
        vec[n : n + 1] = flat_row(row)
    vec[6:8] = jnp.zeros((2, d), F32)


def place_kernel(core, other, whole, out):
    out[...] = other[...].astype(out.dtype)


def route_halves_kernel(at, mine, partner, keep, send):
    half = keep.shape[0]
    for out, which in ((keep, at[0]), (send, 1 - at[0])):
        span = pl.ds(pl.multiple_of(which * half, 16), half)
        out[...] = (mine[span].astype(F32) + partner[span].astype(F32)).astype(BF16)


def route_quarters_kernel(at, keep, other, *outs):
    size = outs[0].shape[0]
    for k, out in enumerate(outs):
        span = pl.ds(pl.multiple_of((at[0] ^ k) * size, 16), size)
        out[...] = (keep[span].astype(F32) + other[span].astype(F32)).astype(BF16)


def add_kernel(at, *refs):
    total = refs[0][...].astype(F32)
    for ref in refs[1:-1]:
        total = total + ref[...].astype(F32)
    refs[-1][...] = total.astype(BF16)


def choose_kernel(at, own, other, out):
    central = jnp.logical_or(at[0] == 1, at[0] == 2)

    @pl.when(central)
    def _():
        out[...] = own[...]

    @pl.when(jnp.logical_not(central))
    def _():
        out[...] = other[...]


def join_kernel(at, *refs):
    out = refs[-1]
    size = refs[0].shape[0]
    for k, ref in enumerate(refs[:-1]):
        out[pl.ds(pl.multiple_of((at[0] ^ k) * size, 16), size)] = ref[...].astype(out.dtype)


def finish_kernel(at, own, other, *refs):
    outs, whole = refs[:-1], refs[-1]
    join_kernel(at, own, other, whole)
    start = 0
    for out in outs:
        out[...] = whole[start : start + out.shape[0]]
        start += out.shape[0]


def stacked(values):
    zero = jnp.zeros_like(values)
    return jnp.concatenate([jnp.where(half_mask(e), values, zero) for e in range(2)], axis=0)


def unstacked(values):
    size = values.shape[0] // 2
    return jnp.where(half_mask(0), values[:size], values[size:])


def attention_heads_forward(start, count, short_blocks, meta, x, weights, qkv, mixed, logs, stat):
    wqkv, bias = weights
    block = pl.program_id(0) + start
    half = mixed.shape[1]
    low = x[...]
    small = bias[...].astype(F32)
    query_bias = (small[1:2] + small[18:19])[:, 0:half]
    value_bias = (small[3:4] + small[20:21])[:, 0:half]
    qkv[:, 0:half] = (nt(low, wqkv[0:half]) + query_bias).astype(BF16)
    qkv[:, half : 2 * half] = nt(low, wqkv[half : 2 * half]).astype(BF16)
    qkv[:, 2 * half : 3 * half] = (nt(low, wqkv[2 * half : 3 * half]) + value_bias).astype(BF16)
    stat[...] = jnp.zeros_like(stat)
    lanes = lax.broadcasted_iota(jnp.int32, (1, 128), 1)

    def tiles(pair, spans):
        column = pl.multiple_of(pair * PAIR, PAIR)
        q, scores = [], []
        for query_at, queries, key_at, keys, valid in spans:
            part = qkv[query_at : query_at + queries, pl.ds(column, PAIR)] * jnp.asarray(0.125, BF16)
            key_part = qkv[key_at : key_at + keys, pl.ds(half + column, PAIR)]
            scores.append(nt(stacked(part), key_part))
        live = [lax.broadcasted_iota(jnp.int32, (1, t[3]), 1) < t[4] for t in spans]
        scores = [jnp.where(a, v, MASKED) for a, v in zip(live, scores)]
        top = [jnp.max(v, axis=-1, keepdims=True) for v in scores]
        weights = [jnp.exp(v - m) for v, m in zip(scores, top)]
        total = [jnp.sum(v, axis=-1, keepdims=True) for v in weights]
        out = [
            nn(v.astype(BF16), qkv[t[2] : t[2] + t[3], pl.ds(2 * half + column, PAIR)])
            for v, t in zip(weights, spans)
        ]
        for (query_at, queries, *_), m, n, v in zip(spans, top, total, out):
            log = m + jnp.log(n)
            rows = stat[query_at : query_at + queries]
            rows = jnp.where(lanes == 2 * pair, log[:queries], rows)
            stat[query_at : query_at + queries] = jnp.where(lanes == 2 * pair + 1, log[queries:], rows)
            mixed[query_at : query_at + queries, pl.ds(column, PAIR)] = unstacked(v * (1.0 / n)).astype(BF16)

    def short_path():
        spans = [
            (slot * SHORT_LEN, SHORT_LEN, slot * SHORT_LEN, SHORT_LEN, short_valid(meta, block, slot))
            for slot in range(SLOTS)
        ]

        def body(pair, carry):
            tiles(pair, spans)
            return carry

        lax.fori_loop(0, half // PAIR, body, 0)

    def long_path():
        valid = long_valid(meta, block, short_blocks)
        spans = [(part * 256, 256, 0, LONG_LEN, valid) for part in range(2)]

        def body(pair, carry):
            tiles(pair, spans)
            return carry

        lax.fori_loop(0, half // PAIR, body, 0)

    if start < short_blocks:
        pl.when(block < short_blocks)(short_path)
    if start + count > short_blocks:
        pl.when(block >= short_blocks)(long_path)
    logs[...] = stat[...].T[0:8]


def attention_forward_kernel(
    start, count, short_blocks, core, slen, llen, scount, lcount, x, a0, a1, qkv, mixed, logs,
    wqkv, wout, bias, sems, stat,
):
    @pl.when(pl.program_id(0) == 0)
    def _():
        load_attention_weights((a0, a1), wqkv, wout, bias, sems)

    meta = (core, slen, llen, scount, lcount)
    attention_heads_forward(start, count, short_blocks, meta, x, (wqkv, bias), qkv, mixed, logs, stat)


def attention_finish_kernel(
    start, count, short_blocks, core, slen, llen, scount, lcount, x, a2, a3, mixed_near, a0, a1, vec, *rest,
):
    qkv, mixed, logs, normed, scale_rows, wqkv, wout, bias, near_out, sems, stat = rest[-11:]

    @pl.when(pl.program_id(0) == 0)
    def _():
        width = near_out.shape[0] // 2
        near = [
            pltpu.make_async_copy(
                piece.at[pl.ds(3 * width, width)], near_out.at[pl.ds(j * width, width)], sems.at[10 + j]
            )
            for j, piece in enumerate((a0, a1))
        ]
        for copy in near:
            copy.start()
        load_attention_weights((a2, a3), wqkv, wout, bias, sems)
        for copy in near:
            copy.wait()

    meta = (core, slen, llen, scount, lcount)
    attention_heads_forward(start, count, short_blocks, meta, x, (wqkv, bias), qkv, mixed, logs, stat)
    hidden = x[...].astype(F32) + vec[0:1]
    hidden = hidden + nn(mixed_near[...], near_out[...]) + nn(mixed[...], wout[...])
    rows, scale = norm_rows(hidden)
    normed[...] = rows.astype(BF16)
    scale_rows[...] = jnp.broadcast_to(scale, scale_rows.shape)


def down_groups(side, downs):
    half = downs[0].shape[0] // 2
    spans = [pl.ds(pl.multiple_of(at * half, 16), half) for at in (side[0], 1 - side[0])]
    return [downs[0][...], downs[1][...]] + [downs[2 + j][span] for span in spans for j in range(2)]


def ffn_forward_kernel(short_blocks, core, slen, llen, scount, lcount, side, normed, cotangent, *rest):
    ups, downs, biases = rest[0:6], rest[6:10], rest[10:14]
    vec, layer_out, layer_rows, grad_low, slope, down_mine, down_partner, sums, active, down_sum, vec_sum = rest[14:]
    meta = (core, slen, llen, scount, lcount)
    block = pl.program_id(0)
    half = ups[2].shape[1]

    @pl.when(block == 0)
    def _():
        down_sum[...] = jnp.zeros_like(down_sum)
        vec_sum[...] = jnp.zeros_like(vec_sum)

    first = normed[...].astype(F32) * vec[1:2] + vec[2:3]
    first_low = first.astype(BF16)
    total = first + vec[3:4]
    at = 0
    for j, (up, down) in enumerate(zip(ups, down_groups(side, downs))):
        size = up.shape[1]
        if j < 2:
            bias = biases[j][0:1]
        else:
            bias = biases[2 + j % 2][9 + j // 4 : 10 + j // 4, 0:half]
        inner = nn(first_low, up[...]) + bias.astype(F32)
        chance = 0.5 * (1.0 + lax.erf(inner * 0.7071067811865476))
        units = (inner * chance).astype(BF16)
        slope[:, at : at + size] = (
            chance + inner * jnp.exp(-0.5 * inner * inner) * 0.3989422804014327
        ).astype(BF16)
        if j < 2:
            active[j] = units
        total = total + nn(units, down)
        at += size
    rows, scale = norm_rows(total)
    result = (rows * vec[4:5] + vec[5:6]).astype(BF16)
    layer_out[...] = result
    layer_rows[...] = result
    position = lax.broadcasted_iota(jnp.int32, (ROWS, 1), 0)
    slot = position // SHORT_LEN
    short_limit = jnp.zeros((ROWS, 1), jnp.int32)
    for n in range(SLOTS):
        short_limit = jnp.where(slot == n, short_valid(meta, jnp.minimum(block, short_blocks - 1), n), short_limit)
    long_limit = long_valid(meta, jnp.maximum(block, short_blocks), short_blocks)
    is_short = block < short_blocks
    alive = jnp.where(is_short, position % SHORT_LEN, position) < jnp.where(
        is_short, short_limit, long_limit
    )
    upstream = jnp.where(alive, cotangent[...].astype(F32), 0.0)
    grad = norm_back(upstream, rows, scale, vec[4:5])
    low = grad.astype(BF16)
    grad_low[...] = low
    vec_sum[0] += fold_rows(upstream * rows)
    vec_sum[1] += fold_rows(upstream)
    vec_sum[2] += fold_rows(grad)
    for j in range(2):
        down_sum[j] += tn(active[j], low)

    @pl.when(block == pl.num_programs(0) - 1)
    def _():
        down_mine[...] = down_sum[0].astype(BF16)
        down_partner[...] = down_sum[1].astype(BF16)
        sums[...] = jnp.zeros_like(sums)
        for n in range(3):
            sums[n : n + 1] = total_rows(vec_sum[n])


def ffn_backward_kernel(side, grad_low, slope, normed, stat, mixed, sums_two, *rest):
    ups, downs = rest[0:6], rest[6:10]
    vec, hidden_low, mine, partner, up_sum, out_sum, vec_sum, kept = rest[10:]
    block = pl.program_id(0)
    units = up_sum.shape[1]
    width = mixed.shape[1] // 2

    @pl.when(block == 0)
    def _():
        up_sum[...] = jnp.zeros_like(up_sum)
        out_sum[...] = jnp.zeros_like(out_sum)
        vec_sum[...] = jnp.zeros_like(vec_sum)

    low = grad_low[...]
    rows = normed[...].astype(F32)
    first_low = (rows * vec[1:2] + vec[2:3]).astype(BF16)
    total = low.astype(F32)
    at = 0
    for j, (up, down) in enumerate(zip(ups, down_groups(side, downs))):
        size = up.shape[1]
        inner = nt(low, down) * slope[:, at : at + size].astype(F32)
        inner_low = inner.astype(BF16)
        total = total + nt(inner_low, up[...])
        if j < 2:
            vec_sum[j] += fold_rows(inner)
            kept[j] = inner_low
        at += size
    for j in range(2):
        up_sum[j] += tn(first_low, kept[j])
    grad = norm_back(total, rows, stat[:, 0:1], vec[1:2])
    vec_sum[2] += fold_rows(total * rows)
    vec_sum[3] += fold_rows(total)
    vec_sum[4] += fold_rows(grad)
    grad_attn = grad.astype(BF16)
    hidden_low[...] = grad_attn
    out_sum[...] += tn(mixed[...], grad_attn)

    @pl.when(block == pl.num_programs(0) - 1)
    def _():
        index = lax.broadcasted_iota(jnp.int32, (16, 1), 0)
        shared = [sums_two[n : n + 1] for n in range(3)] + [total_rows(vec_sum[n]) for n in range(2, 5)]
        for j, out in enumerate((mine, partner)):
            out[0:units] = up_sum[j].astype(BF16)
            out[units : units + width] = out_sum[j * width : (j + 1) * width].astype(BF16)
            out[units + width :] = jnp.zeros((out.shape[0] - units - width, out.shape[1]), BF16)
            rows_out = jnp.zeros((16, out.shape[1]), F32)
            for n, row in enumerate(shared + [total_rows(vec_sum[j])]):
                rows_out = jnp.where(index == n, row, rows_out)
            out[units + width : units + width + 16] = rows_out.astype(BF16)


def attention_heads_backward(start, short_blocks, meta, logs, qkv, mixed, mixed_grad, low_qkv, delta):
    block = pl.program_id(0) + start
    half = mixed.shape[1]
    own = (mixed_grad[...].astype(F32) * mixed[...].astype(F32)).astype(BF16)
    head = lax.broadcasted_iota(jnp.int32, (8, half), 1) // HEAD_DIM
    pick = jnp.where(head == lax.broadcasted_iota(jnp.int32, (8, half), 0), 1.0, 0.0)
    delta[...] = nt(pick.astype(BF16), own)

    index = lax.broadcasted_iota(jnp.int32, (8, 1), 0)

    def tiles(pair, size, valids):
        column = pl.multiple_of(pair * PAIR, PAIR)
        spans = [pl.ds(n * size, size) for n in range(len(valids))]

        def rows(ref, span):
            picked = [total_rows(jnp.where(index == 2 * pair + e, ref[:, span], 0.0)) for e in range(2)]
            return jnp.concatenate(picked, axis=1)

        q = [stacked(qkv[t, pl.ds(column, PAIR)] * jnp.asarray(0.125, BF16)) for t in spans]
        g = [stacked(mixed_grad[t, pl.ds(column, PAIR)]) for t in spans]
        k = [qkv[t, pl.ds(half + column, PAIR)] for t in spans]
        scores = [nt(b, a) for a, b in zip(q, k)]
        grads = [nt(qkv[t, pl.ds(2 * half + column, PAIR)], a) for t, a in zip(spans, g)]
        place = lax.broadcasted_iota(jnp.int32, (size, 1), 0)
        probs = [
            jnp.where(place < valid, jnp.exp(v - rows(logs, t)), 0.0)
            for v, t, valid in zip(scores, spans, valids)
        ]
        scores = [(p * (v - rows(delta, t))).astype(BF16) for p, v, t in zip(probs, grads, spans)]
        dq = [tn(v, b) for v, b in zip(scores, k)]
        dk = [nn(v, a) for v, a in zip(scores, q)]
        dv = [nn(p.astype(BF16), a) for p, a in zip(probs, g)]
        for t, a, b, c in zip(spans, dq, dk, dv):
            low_qkv[t, pl.ds(column, PAIR)] = (unstacked(a) * 0.125).astype(BF16)
            low_qkv[t, pl.ds(half + column, PAIR)] = b.astype(BF16)
            low_qkv[t, pl.ds(2 * half + column, PAIR)] = c.astype(BF16)

    if start < short_blocks:
        valids = [short_valid(meta, block, slot) for slot in range(SLOTS)]
        size = SHORT_LEN
    else:
        valids = [long_valid(meta, block, short_blocks)]
        size = LONG_LEN

    def body(pair, carry):
        tiles(pair, size, valids)
        return carry

    lax.fori_loop(0, half // PAIR, body, 0)


def attention_backward_kernel(
    start, short_blocks, core, slen, llen, scount, lcount, hidden_low, stat, qkv, mixed, x,
    a0, a1, *rest,
):
    if start:
        sums_in, vec_in, low_qkv, mine, partner = rest[:5]
    else:
        low_qkv, qkv_out, vec_out = rest[:3]
    wqkv, wout, bias, sems, mixed_grad, delta, qkv_sum, vec_sum = rest[-8:]
    meta = (core, slen, llen, scount, lcount)
    block = pl.program_id(0)
    half = mixed.shape[1]
    width = half // 2

    @pl.when(block == 0)
    def _():
        load_attention_weights((a0, a1), wqkv, wout, bias, sems)
        if start:
            qkv_sum[...] = sums_in[...]
            vec_sum[...] = vec_in[...]
        else:
            qkv_sum[...] = jnp.zeros_like(qkv_sum)
            vec_sum[...] = jnp.zeros_like(vec_sum)

    mixed_grad[...] = nt(hidden_low[...], wout[...]).astype(BF16)
    attention_heads_backward(start, short_blocks, meta, stat, qkv, mixed, mixed_grad, low_qkv, delta)
    vec_sum[0] += fold_rows(low_qkv[:, 0:half].astype(F32))
    vec_sum[1] += fold_rows(low_qkv[:, 2 * half : 3 * half].astype(F32))
    for k in range(3):
        qkv_sum[k] += tn(low_qkv[:, k * half : (k + 1) * half], x[...])

    @pl.when(block == pl.num_programs(0) - 1)
    def _():
        if not start:
            qkv_out[...] = qkv_sum[...]
            vec_out[...] = vec_sum[...]
        else:
            index = lax.broadcasted_iota(jnp.int32, (16, 1), 0)
            heads = [total_rows(vec_sum[n]) for n in range(2)]
            for j, out in enumerate((mine, partner)):
                for k in range(3):
                    out[k * width : (k + 1) * width] = qkv_sum[k, j * width : (j + 1) * width].astype(BF16)
                out[3 * width :] = jnp.zeros((out.shape[0] - 3 * width, out.shape[1]), BF16)
                rows_out = jnp.zeros((16, half), F32)
                for n, row in enumerate(heads):
                    row = pltpu.roll(row, half - width, 1) if j else row
                    rows_out = jnp.where(index == n, row, rows_out)
                out[3 * width : 3 * width + 16, 0:half] = rows_out.astype(BF16)


def attention_input_kernel(
    start, short_blocks, core, slen, llen, scount, lcount, hidden_low, stat, qkv, mixed, low_near,
    a2, a3, a0, a1, *rest,
):
    input_rows, input_grad = rest[-10:-8]
    wqkv, wout, bias, near_qkv, sems, low_qkv, mixed_grad, delta = rest[-8:]
    meta = (core, slen, llen, scount, lcount)

    @pl.when(pl.program_id(0) == 0)
    def _():
        width = near_qkv.shape[0] // 6
        near = [
            pltpu.make_async_copy(
                piece.at[pl.ds(k * width, width)],
                near_qkv.at[pl.ds((2 * k + j) * width, width)],
                sems.at[10 + 2 * k + j],
            )
            for k in range(3)
            for j, piece in enumerate((a0, a1))
        ]
        for copy in near:
            copy.start()
        load_attention_weights((a2, a3), wqkv, wout, bias, sems)
        for copy in near:
            copy.wait()

    low = hidden_low[...]
    mixed_grad[...] = nt(low, wout[...]).astype(BF16)
    attention_heads_backward(start, short_blocks, meta, stat, qkv, mixed, mixed_grad, low_qkv, delta)
    total = low.astype(F32) + nn(low_near[...], near_qkv[...]) + nn(low_qkv[...], wqkv[...])
    input_rows[...] = total.astype(BF16)
    input_grad[...] = total


def const_spec(shape):
    return pl.BlockSpec(
        shape, lambda *_: (0,) * len(shape), pipeline_mode=pl.Buffered(1)
    )


def any_spec():
    return pl.BlockSpec(memory_space=pl.ANY)


def own_spec(width, start=0):
    return pl.BlockSpec((ROWS, width), lambda i, *_: (i + start, 0))


def whole_call(body, name, which, operands, shapes, scratch=(), keep=False, limit=24):
    moved = sum(v.size * v.dtype.itemsize for v in list(operands) + list(shapes))
    vmem = pl.BlockSpec(memory_space=pltpu.VMEM)
    if not keep:
        operands = [pltpu.with_memory_space_constraint(v, pltpu.VMEM) for v in operands]
        shapes = [pltpu.VMEM(v.shape, v.dtype) for v in shapes]
    return pl.pallas_call(
        body,
        name=name,
        in_specs=[pl.BlockSpec(memory_space=pltpu.SMEM)] + [vmem] * len(operands),
        out_specs=[vmem] * len(shapes),
        out_shape=shapes,
        scratch_shapes=list(scratch),
        compiler_params=pltpu.CompilerParams(vmem_limit_bytes=limit * 1024 * 1024),
        cost_estimate=pl.CostEstimate(flops=0, bytes_accessed=moved, transcendentals=0),
    )(which, *operands)


def spread(body, name, grid, in_specs, out_specs, out_shape, scratch=(), prefetch=0, flops=0, moved=0, exps=0, alias=None):
    return pl.pallas_call(
        body,
        name=name,
        grid_spec=pltpu.PrefetchScalarGridSpec(
            num_scalar_prefetch=prefetch,
            grid=grid,
            in_specs=in_specs,
            out_specs=out_specs,
            scratch_shapes=list(scratch),
        ),
        out_shape=out_shape,
        input_output_aliases=alias or {},
        compiler_params=pltpu.CompilerParams(
            dimension_semantics=("arbitrary",), vmem_limit_bytes=VMEM_LIMIT
        ),
        cost_estimate=pl.CostEstimate(flops=flops, bytes_accessed=moved, transcendentals=exps),
    )


def per_device(
    tokens,
    cotangent,
    short_len,
    long_len,
    short_count,
    long_count,
    query_weight,
    query_bias,
    key_weight,
    value_weight,
    value_bias,
    output_weight,
    output_bias,
    first_gain,
    first_shift,
    up_weight,
    up_bias,
    down_weight,
    down_bias,
    second_gain,
    second_shift,
):
    d = tokens.shape[1]
    width = query_weight.shape[1]
    units = up_weight.shape[1]
    half = 2 * width
    piece_rows = 4 * width + 16
    short_blocks = short_len.shape[0] * SHORT_LEN // (2 * ROWS)
    long_blocks = long_len.shape[0] * LONG_LEN // (2 * ROWS)
    blocks = short_blocks + long_blocks
    rows = blocks * ROWS
    core = lax.axis_index("tensor") % 2
    side = lax.axis_index("dp") % 2
    core_id = core.astype(jnp.int32).reshape(1)
    meta = (core_id, short_len, long_len, short_count, long_count)
    sds = jax.ShapeDtypeStruct

    def swap(values, bit, axis="tensor"):
        size = lax.axis_size(axis)
        return lax.ppermute(values, axis, [(i, i ^ bit) for i in range(size)])

    def after(value, *others):
        return lax.optimization_barrier((value,) + others)[0]

    def global_spec(start=0, flip=0):
        def index(i, core, *_):
            i = i + start
            first = core[0] if flip == 0 else 1 - core[0]
            return (2 * i + jnp.where(i < short_blocks, first, 1 - first), 0)

        return pl.BlockSpec((ROWS, d), index)

    vec_spec = const_spec((8, d))
    row_spec = own_spec(d)

    side_id = side.astype(jnp.int32).reshape(1)
    line_id = (lax.axis_index("dp") // 2).astype(jnp.int32).reshape(1)
    vectors = [query_bias, value_bias, up_bias, output_bias, first_gain, first_shift,
               down_bias, second_gain, second_shift]
    a0, vec = whole_call(
        pack_kernel, "pack", side_id,
        [query_weight.T, key_weight.T, value_weight.T, output_weight, *vectors],
        [sds((piece_rows, d), BF16), sds((8, d), F32)], [pltpu.VMEM((8, d), F32)], True, 61,
    )
    up_split = lax.dynamic_slice_in_dim(up_weight, side * (units // 2), units // 2, 1)
    def boundary(lead, *values):
        out = lax.optimization_barrier((lead,) + values)
        return out[0], list(out[1:])

    a1 = swap(a0, 1)
    a2 = swap(a0, 2)

    weight_scratch = [
        pltpu.VMEM((3 * half, d), BF16),
        pltpu.VMEM((half, d), BF16),
        pltpu.VMEM((32, d), BF16),
    ]
    sems = pltpu.SemaphoreType.DMA((16,))
    stat_scratch = pltpu.VMEM((ROWS, 128), F32)

    def log_spec(start=0):
        return pl.BlockSpec((8, ROWS), lambda i, *_: (i + start, 0))

    head_shapes = [sds((rows, 3 * half), BF16), sds((rows, half), BF16), sds((8 * blocks, ROWS), F32)]
    head_flops = 2 * rows * d * 3 * half + 4 * rows * 320 * half
    qkv_near, mixed_near, stat_near = spread(
        functools.partial(attention_forward_kernel, 0, blocks, short_blocks), "attention_near", (blocks,),
        [global_spec()] + [any_spec()] * 2, [own_spec(3 * half), own_spec(half), log_spec()], head_shapes,
        weight_scratch + [sems, stat_scratch], 5,
        head_flops, rows * d * 8, rows * 320 * 6,
    )(*meta, tokens, a0, a1)

    stat_near, (a2,) = boundary(stat_near, a2)
    a3 = swap(a2, 1)
    a3, (u2, d2, up_near) = boundary(a3, up_split, down_weight, up_weight)
    u2 = swap(u2, 2)
    d2 = swap(d2, 2)
    u1 = swap(up_near, 1)

    def far_forward(start, count, extra, alias):
        return spread(
            functools.partial(attention_finish_kernel, start, count, short_blocks), "attention_far", (count,),
            [global_spec(start)] + [any_spec()] * 2 + [own_spec(half, start)] + [any_spec()] * 2 + [vec_spec]
            + [any_spec()] * len(extra),
            [own_spec(3 * half, start), own_spec(half, start), log_spec(start), own_spec(d, start), own_spec(128, start)],
            head_shapes + [sds((rows, d), BF16), sds((rows, 128), F32)],
            weight_scratch + [pltpu.VMEM((half, d), BF16), sems, stat_scratch], 5,
            (head_flops + 2 * rows * d * d) * count // blocks, count * ROWS * d * 10, count * ROWS * 320 * 6, alias,
        )(*meta, tokens, a2, a3, mixed_near, a0, a1, vec, *extra)

    far = list(far_forward(0, short_blocks, [], None))
    far[3], (u2, u1, down_near) = boundary(far[3], u2, u1, down_weight)
    u4 = swap(u2, 1, "dp")
    u3, d1 = swap(u2, 1), swap(down_near, 1)
    qkv_far, mixed_far, stat_far, normed, scale_one = far_forward(
        short_blocks, long_blocks, far, {12 + n: n for n in range(5)}
    )
    normed, (u4, u3, d2, d1) = boundary(normed, u4, u3, d2, d1)
    u5, d3 = swap(u4, 1), swap(d2, 1)
    ups = (up_weight, u1, u2, u3, u4, u5)
    downs = (down_weight, d1, d2, d3)
    bias_spec = pl.BlockSpec((16, d), lambda *_: (4 * width // 16, 0), pipeline_mode=pl.Buffered(1))
    up_specs = [const_spec(v.shape) for v in ups]
    down_specs = [const_spec(v.shape) for v in downs]
    whole_out, out_rows, grad_low, slope, down_mine, down_partner, sums_two = spread(
        functools.partial(ffn_forward_kernel, short_blocks), "ffn_forward", (blocks,),
        [row_spec, global_spec()] + up_specs + down_specs + [bias_spec] * 4 + [vec_spec],
        [global_spec(), row_spec, row_spec, own_spec(4 * units)] + [const_spec((units, d))] * 2 + [vec_spec],
        [sds((2 * rows, d), BF16), sds((rows, d), BF16), sds((rows, d), BF16), sds((rows, 4 * units), BF16)]
        + [sds((units, d), BF16)] * 2 + [sds((8, d), F32)],
        [pltpu.VMEM((2, ROWS, units), BF16), pltpu.VMEM((2, units, d), F32), pltpu.VMEM((3, 8, d), F32)],
        6, 2 * rows * d * 10 * units, rows * d * 20, rows * 8 * units,
    )(*meta, side_id, normed, cotangent, *ups, *downs, a0, a1, a2, a3, vec)

    custom = lax.axis_size("dp") == 8

    line_steps = (
        [(0, 1), (3, 2)],
        [(1, 2), (2, 1)],
        [(1, 0), (2, 3)],
    )

    def along_line(values, stage):
        pairs = [(2 * i + n, 2 * j + n) for i, j in line_steps[stage] for n in range(2)]
        return lax.ppermute(values, "dp", pairs)

    class Reduction:
        def __init__(self, mine, partner, central):
            self.mine, self.size, self.central = mine, mine.shape[0], central
            self.moved = [swap(partner, 1)]
            self.stage = 0

        def part(self, count):
            return sds((self.size // count, d), BF16)

        def step(self):
            got = self.moved
            stage, self.stage = self.stage, self.stage + 1
            if not custom:
                if stage == 0:
                    total = (self.mine.astype(F32) + got[0].astype(F32)).astype(BF16)
                    self.moved = [lax.psum(total, "dp")]
                return self.moved[0]
            if stage == 0:
                self.keep, send = whole_call(
                    route_halves_kernel, "halves", side_id, [self.mine, got[0]], [self.part(2)] * 2
                )
                sent, self.moved = [send], [swap(send, 1, "dp")]
            elif self.central and stage < 4:
                (self.keep,) = whole_call(add_kernel, "add", line_id, [self.keep, got[0]], [self.part(2)])
                sent, self.moved = [self.keep], [along_line(self.keep, stage - 1)]
            elif self.central and stage == 4:
                (self.keep,) = whole_call(choose_kernel, "choose", line_id, [self.keep, got[0]], [self.part(2)])
                sent, self.moved = [self.keep], [swap(self.keep, 1, "dp")]
            elif stage == 1:
                self.keep, *sent = whole_call(
                    route_quarters_kernel, "quarters", line_id, [self.keep, got[0]], [self.part(8)] * 4
                )
                self.moved = [swap(v, 2 * (k + 1), "dp") for k, v in enumerate(sent)]
            elif stage == 2:
                (self.keep,) = whole_call(add_kernel, "add", line_id, [self.keep, *got], [self.part(8)])
                sent = [self.keep]
                self.moved = [swap(self.keep, 2 * k, "dp") for k in (1, 2, 3)]
            elif stage == 3:
                (self.keep,) = whole_call(
                    join_kernel, "join_quarters", line_id, [self.keep, *got], [self.part(2)]
                )
                sent, self.moved = [self.keep], [swap(self.keep, 1, "dp")]
            return sent[0]

        def finish(self, *sizes):
            shapes = [sds((n, d), F32) for n in sizes]
            if not custom:
                total = self.moved[0].astype(F32)
                cuts = [sum(sizes[:n]) for n in range(len(sizes))]
                return [total[at : at + n] for at, n in zip(cuts, sizes)]
            operands = [self.keep, self.moved[0]]
            return whole_call(
                finish_kernel, "finish", side_id, operands, shapes, [pltpu.VMEM((self.size, d), F32)], True
            )

    def settle(lead, reductions, *extra):
        lead, values = boundary(lead, *[v for r in reductions for v in r.moved], *extra)
        for r in reductions:
            count = len(r.moved)
            r.moved, values = values[:count], values[count:]
        return (lead, *values)

    grad_low, down_mine, down_partner = lax.optimization_barrier((grad_low, down_mine, down_partner))
    down_reduce = Reduction(down_mine, down_partner, True)
    tie = down_reduce.step()
    grad_low = after(grad_low, tie)
    moved_out = swap(after(out_rows, tie), 1)

    pack_rows = units + width + 64
    hidden_low, mine, partner = spread(
        ffn_backward_kernel, "ffn_backward", (blocks,),
        [row_spec, own_spec(4 * units), row_spec, own_spec(128), own_spec(half), vec_spec]
        + up_specs + down_specs + [vec_spec],
        [row_spec] + [const_spec((pack_rows, d))] * 2,
        [sds((rows, d), BF16)] + [sds((pack_rows, d), BF16)] * 2,
        [pltpu.VMEM((2, d, units), F32), pltpu.VMEM((half, d), F32), pltpu.VMEM((5, 8, d), F32),
         pltpu.VMEM((2, ROWS, units), BF16)],
        1, 2 * rows * d * 10 * units, rows * d * 16, 0,
    )(side_id, grad_low, slope, normed, scale_one, mixed_near, sums_two, *ups, *downs, vec)
    hidden_low, mine, partner, moved_out = settle(hidden_low, [down_reduce], mine, partner, moved_out)
    tie = down_reduce.step()
    partner = after(partner, tie)
    up_reduce = Reduction(mine, partner, True)
    tie = up_reduce.step()
    hidden_low = after(hidden_low, tie)

    qkv_rows = 3 * width + 64
    sums = [sds((3, half, d), F32), sds((2, 8, half), F32)]
    sum_specs = [const_spec(v.shape) for v in sums]

    def near_backward(start, count, extra, extra_specs, outs, out_specs, alias):
        return spread(
            functools.partial(attention_backward_kernel, start, short_blocks), "attention_near_backward", (count,),
            [own_spec(d, start), log_spec(start), own_spec(3 * half, start), own_spec(half, start), global_spec(start)]
            + [any_spec()] * 2 + extra_specs,
            [own_spec(3 * half)] + out_specs,
            [sds((count * ROWS, 3 * half), BF16)] + outs,
            weight_scratch + [sems, pltpu.VMEM((ROWS, half), BF16), pltpu.VMEM((8, ROWS), F32),
                              pltpu.VMEM((3, half, d), F32), pltpu.VMEM((2, 8, half), F32)],
            5, count * ROWS * (10 * d * half + 3200 * half), count * ROWS * d * 16, count * ROWS * 320 * 6,
        )(*meta, hidden_low, stat_near, qkv_near, mixed_near, tokens, a0, a1, *extra)

    low_short, *sums_short = near_backward(0, short_blocks, [], [], sums, sum_specs, None)
    (low_short,) = settle(low_short, [down_reduce, up_reduce])
    tie = down_reduce.step()
    tie_two = up_reduce.step()
    sums_short[1] = after(sums_short[1], tie, tie_two)
    low_long, mine, partner = near_backward(
        short_blocks, long_blocks, sums_short, sum_specs,
        [sds((qkv_rows, d), BF16)] * 2, [const_spec((qkv_rows, d))] * 2, None,
    )
    low_long, mine, partner = settle(low_long, [down_reduce, up_reduce], mine, partner)
    ties = [down_reduce.step(), up_reduce.step()]
    qkv_reduce = Reduction(mine, after(partner, *ties), False)
    ties += [qkv_reduce.step()]

    def far_backward(start, count, low_near, extra, alias):
        return spread(
            functools.partial(attention_input_kernel, start, short_blocks), "attention_far_backward", (count,),
            [own_spec(d, start), log_spec(start), own_spec(3 * half, start), own_spec(half, start), own_spec(3 * half)]
            + [any_spec()] * (4 + len(extra)),
            [row_spec, global_spec(start)], [sds((count * ROWS, d), BF16), sds((2 * rows, d), F32)],
            weight_scratch + [pltpu.VMEM((3 * half, d), BF16), sems, pltpu.VMEM((ROWS, 3 * half), BF16),
                              pltpu.VMEM((ROWS, half), BF16), pltpu.VMEM((8, ROWS), F32)],
            5, count * ROWS * (14 * d * half + 3200 * half), count * ROWS * d * 16, count * ROWS * 320 * 6, alias,
        )(*meta, hidden_low, stat_far, qkv_far, mixed_far, low_near, a2, a3, a0, a1, *extra)

    low_short = after(low_short, *ties)
    rows_short, whole_in = far_backward(0, short_blocks, low_short, [], None)
    (rows_short,) = settle(rows_short, [down_reduce, up_reduce, qkv_reduce])
    moved_short = swap(rows_short, 1)
    ties = [qkv_reduce.step(), up_reduce.step()]
    down_reduce.moved[0] = after(down_reduce.moved[0], moved_short)
    ties += [down_reduce.step()]
    low_long = after(low_long, *ties)
    rows_long, whole_in = far_backward(short_blocks, long_blocks, low_long, [whole_in], {14: 1})
    rows_long, moved_short = settle(rows_long, [down_reduce, up_reduce, qkv_reduce], moved_short)
    tie = qkv_reduce.step()
    tie = after(tie, up_reduce.step())
    down_reduce.moved[0] = after(down_reduce.moved[0], tie)
    (grad_down,) = down_reduce.finish(units)
    moved_long = swap(after(rows_long, tie), 1)

    def place(whole, other, start, count):
        return spread(
            place_kernel, "place", (count,), [own_spec(d), any_spec()], global_spec(start, 1),
            sds(whole.shape, whole.dtype), (), 1, 0, other.size * 6, 0, {2: 0},
        )(core_id, other, whole)

    layer_output = place(whole_out, after(moved_out, tie), 0, blocks)
    input_grad = place(whole_in, after(moved_short, tie), 0, short_blocks)
    layer_output, input_grad, moved_long = settle(layer_output, [qkv_reduce], input_grad, moved_long)
    tie = qkv_reduce.step()
    input_grad = place(input_grad, after(moved_long, tie), short_blocks, long_blocks)
    up_reduce.moved[0] = after(up_reduce.moved[0], tie)
    grad_up, grad_out, small = up_reduce.finish(units, width, 16)
    grad_up, input_grad = settle(grad_up, [qkv_reduce], input_grad)
    grad_query, grad_key, grad_value, heads = qkv_reduce.finish(width, width, width, 16)
    return (
        layer_output,
        input_grad,
        grad_query.T,
        heads[0, :width],
        grad_key.T,
        grad_value.T,
        heads[1, :width],
        grad_out,
        small[5],
        small[3],
        small[4],
        grad_up,
        small[6],
        grad_down,
        small[2],
        small[0],
        small[1],
    )

def solution(mesh):
    return jax.shard_map(
        per_device,
        mesh=mesh,
        in_specs=(
            P("dp", None),
            P("dp", None),
            P("dp"),
            P("dp"),
            P("dp"),
            P("dp"),
            P(None, "tensor"),
            P("tensor"),
            P(None, "tensor"),
            P(None, "tensor"),
            P("tensor"),
            P("tensor", None),
            P(),
            P(),
            P(),
            P(None, "tensor"),
            P("tensor"),
            P("tensor", None),
            P(),
            P(),
            P(),
        ),
        out_specs=(
            P("dp", None),
            P("dp", None),
            P(None, "tensor"),
            P("tensor"),
            P(None, "tensor"),
            P(None, "tensor"),
            P("tensor"),
            P("tensor", None),
            P(),
            P(),
            P(),
            P(None, "tensor"),
            P("tensor"),
            P("tensor", None),
            P(),
            P(),
            P(),
        ),
        check_vma=False,
    )
```

```python
import functools

import jax
import jax.numpy as jnp
from jax import lax
from jax.experimental import pallas as pl
from jax.experimental.pallas import tpu as pltpu
from jax.sharding import PartitionSpec as P

HEAD_DIM = 64
SHORT_LEN = 128
LONG_LEN = 512
ROWS = 512
SLOTS = ROWS // SHORT_LEN
PAIR = 2 * HEAD_DIM
MASKED = -30000.0
F32 = jnp.float32
BF16 = jnp.bfloat16
VMEM_LIMIT = 60 * 1024 * 1024


def nn(left, right):
    return lax.dot_general(left, right, (((1,), (0,)), ((), ())), preferred_element_type=F32)


def nt(left, right):
    return lax.dot_general(left, right, (((1,), (1,)), ((), ())), preferred_element_type=F32)


def tn(left, right):
    return lax.dot_general(left, right, (((0,), (0,)), ((), ())), preferred_element_type=F32)


def fold_rows(values):
    return jnp.sum(values.reshape(-1, 8, values.shape[-1]), axis=0)


def total_rows(values):
    return jnp.sum(values, axis=0, keepdims=True)


def half_mask(which):
    lanes = lax.broadcasted_iota(jnp.int32, (1, PAIR), 1)
    return (lanes >= HEAD_DIM) if which else (lanes < HEAD_DIM)


def short_valid(meta, block, slot):
    index = SLOTS * (2 * block + meta[0][0]) + slot
    return jnp.where(index < meta[3][0], meta[1][index], 0)


def long_valid(meta, block, short_blocks):
    index = 2 * (block - short_blocks) + 1 - meta[0][0]
    return jnp.where(index < meta[4][0], meta[2][index], 0)


def norm_rows(values):
    centre = values - jnp.mean(values, axis=-1, keepdims=True)
    scale = lax.rsqrt(jnp.mean(centre * centre, axis=-1, keepdims=True) + 1e-12)
    return centre * scale, scale


def norm_back(incoming, normed, scale, gain):
    grad = incoming * gain
    inner = grad - jnp.mean(grad, axis=-1, keepdims=True)
    inner = inner - normed * jnp.mean(grad * normed, axis=-1, keepdims=True)
    return scale * inner


def load_attention_weights(pieces, wqkv, wout, bias, sems):
    width = wqkv.shape[0] // 6
    copies = []
    for j, piece in enumerate(pieces):
        for k in range(3):
            copies.append(
                (piece.at[pl.ds(k * width, width)], wqkv.at[pl.ds((2 * k + j) * width, width)])
            )
        copies.append((piece.at[pl.ds(3 * width, width)], wout.at[pl.ds(j * width, width)]))
        copies.append((piece.at[pl.ds(4 * width, 16)], bias.at[pl.ds(16 * j, 16)]))
    started = [pltpu.make_async_copy(s, d, sems.at[n]) for n, (s, d) in enumerate(copies)]
    for copy in started:
        copy.start()
    for copy in started:
        copy.wait()


def flat_row(ref):
    return ref[...].astype(F32).reshape(1, ref.shape[0])


def pack_kernel(at, wq, wk, wv, wo, qb, vb, ub, ob, g1, s1, db, g2, s2, piece, vec, wide):
    width = wq.shape[0]
    d = piece.shape[1]
    piece[0:width] = wq[...]
    piece[width : 2 * width] = wk[...]
    piece[2 * width : 3 * width] = wv[...]
    piece[3 * width : 4 * width] = wo[...]
    index = lax.broadcasted_iota(jnp.int32, (16, 1), 0)
    wide[...] = jnp.zeros_like(wide)
    wide[0:1, 0:width] = flat_row(qb)
    wide[1:2, 0:width] = flat_row(vb)
    row_q, row_v, row_u = wide[0:1], wide[1:2], flat_row(ub)
    lead = jnp.where(lax.broadcasted_iota(jnp.int32, (1, d), 1) < d // 2, row_u, 0.0)
    trail = pltpu.roll(row_u - lead, d // 2, 1)
    mine = jnp.where(at[0] == 0, lead, trail)
    far = jnp.where(at[0] == 0, trail, lead)
    rows = [row_u, row_q, pltpu.roll(row_q, width, 1), row_v, pltpu.roll(row_v, width, 1)]
    block = jnp.zeros((16, d), F32)
    for n, row in enumerate(rows + [None] * 4 + [mine, far]):
        if row is not None:
            block = jnp.where(index == n, row, block)
    piece[4 * width : 4 * width + 16] = block.astype(BF16)
    for n, row in enumerate((ob, g1, s1, db, g2, s2)):
        vec[n : n + 1] = flat_row(row)
    vec[6:8] = jnp.zeros((2, d), F32)


def place_kernel(core, other, whole, out):
    out[...] = other[...].astype(out.dtype)


def route_halves_kernel(at, mine, partner, keep, send):
    half = keep.shape[0]
    for out, which in ((keep, at[0]), (send, 1 - at[0])):
        span = pl.ds(pl.multiple_of(which * half, 16), half)
        out[...] = (mine[span].astype(F32) + partner[span].astype(F32)).astype(BF16)


def route_quarters_kernel(at, keep, other, *outs):
    size = outs[0].shape[0]
    for k, out in enumerate(outs):
        span = pl.ds(pl.multiple_of((at[0] ^ k) * size, 16), size)
        out[...] = (keep[span].astype(F32) + other[span].astype(F32)).astype(BF16)


def add_kernel(at, *refs):
    total = refs[0][...].astype(F32)
    for ref in refs[1:-1]:
        total = total + ref[...].astype(F32)
    refs[-1][...] = total.astype(BF16)


def choose_kernel(at, own, other, out):
    central = jnp.logical_or(at[0] == 1, at[0] == 2)

    @pl.when(central)
    def _():
        out[...] = own[...]

    @pl.when(jnp.logical_not(central))
    def _():
        out[...] = other[...]


def join_kernel(at, *refs):
    out = refs[-1]
    size = refs[0].shape[0]
    for k, ref in enumerate(refs[:-1]):
        out[pl.ds(pl.multiple_of((at[0] ^ k) * size, 16), size)] = ref[...].astype(out.dtype)


def finish_kernel(at, own, other, *refs):
    outs, whole = refs[:-1], refs[-1]
    join_kernel(at, own, other, whole)
    start = 0
    for out in outs:
        out[...] = whole[start : start + out.shape[0]]
        start += out.shape[0]


def stacked(values):
    zero = jnp.zeros_like(values)
    return jnp.concatenate([jnp.where(half_mask(e), values, zero) for e in range(2)], axis=0)


def unstacked(values):
    size = values.shape[0] // 2
    return jnp.where(half_mask(0), values[:size], values[size:])


def attention_heads_forward(start, count, short_blocks, meta, x, weights, qkv, mixed, logs, stat):
    wqkv, bias, head_bias = weights
    block = pl.program_id(0) + start
    half = mixed.shape[1]

    @pl.when(pl.program_id(0) == 0)
    def _():
        small = bias[...].astype(F32)
        head_bias[0] = (small[1:2] + small[18:19])[:, 0:half]
        head_bias[1] = jnp.zeros((1, half), F32)
        head_bias[2] = (small[3:4] + small[20:21])[:, 0:half]

    def project(k, carry):
        span = pl.ds(pl.multiple_of(k * half, half), half)
        qkv[:, span] = (nt(x[...], wqkv[span]) + head_bias[k]).astype(BF16)
        return carry

    lax.fori_loop(0, 3, project, 0)
    stat[...] = jnp.zeros_like(stat)
    lanes = lax.broadcasted_iota(jnp.int32, (1, 128), 1)

    def tiles(pair, spans):
        column = pl.multiple_of(pair * PAIR, PAIR)
        q, scores = [], []
        for query_at, queries, key_at, keys, valid in spans:
            part = qkv[query_at : query_at + queries, pl.ds(column, PAIR)] * jnp.asarray(0.125, BF16)
            key_part = qkv[key_at : key_at + keys, pl.ds(half + column, PAIR)]
            scores.append(nt(stacked(part), key_part))
        live = [lax.broadcasted_iota(jnp.int32, (1, t[3]), 1) < t[4] for t in spans]
        scores = [jnp.where(a, v, MASKED) for a, v in zip(live, scores)]
        top = [jnp.max(v, axis=-1, keepdims=True) for v in scores]
        weights = [jnp.exp(v - m) for v, m in zip(scores, top)]
        total = [jnp.sum(v, axis=-1, keepdims=True) for v in weights]
        out = [
            nn(v.astype(BF16), qkv[t[2] : t[2] + t[3], pl.ds(2 * half + column, PAIR)])
            for v, t in zip(weights, spans)
        ]
        for (query_at, queries, *_), m, n, v in zip(spans, top, total, out):
            log = m + jnp.log(n)
            rows = stat[query_at : query_at + queries]
            rows = jnp.where(lanes == 2 * pair, log[:queries], rows)
            stat[query_at : query_at + queries] = jnp.where(lanes == 2 * pair + 1, log[queries:], rows)
            mixed[query_at : query_at + queries, pl.ds(column, PAIR)] = unstacked(v * (1.0 / n)).astype(BF16)

    def short_path():
        spans = [
            (slot * SHORT_LEN, SHORT_LEN, slot * SHORT_LEN, SHORT_LEN, short_valid(meta, block, slot))
            for slot in range(SLOTS)
        ]

        def body(pair, carry):
            tiles(pair, spans)
            return carry

        lax.fori_loop(0, half // PAIR, body, 0)

    def long_path():
        valid = long_valid(meta, block, short_blocks)
        spans = [(part * 256, 256, 0, LONG_LEN, valid) for part in range(2)]

        def body(pair, carry):
            tiles(pair, spans)
            return carry

        lax.fori_loop(0, half // PAIR, body, 0)

    if start < short_blocks:
        pl.when(block < short_blocks)(short_path)
    if start + count > short_blocks:
        pl.when(block >= short_blocks)(long_path)
    logs[...] = stat[...].T[0:8]


def attention_forward_kernel(
    start, count, short_blocks, core, slen, llen, scount, lcount, x, a0, a1, qkv, mixed, logs,
    wqkv, wout, bias, sems, stat, head_bias,
):
    @pl.when(pl.program_id(0) == 0)
    def _():
        load_attention_weights((a0, a1), wqkv, wout, bias, sems)

    meta = (core, slen, llen, scount, lcount)
    attention_heads_forward(start, count, short_blocks, meta, x, (wqkv, bias, head_bias), qkv, mixed, logs, stat)


def attention_finish_kernel(
    start, count, short_blocks, core, slen, llen, scount, lcount, x, a2, a3, mixed_near, a0, a1, vec, *rest,
):
    qkv, mixed, logs, normed, scale_rows, wqkv, wout, bias, near_out, sems, stat, head_bias = rest[-12:]

    @pl.when(pl.program_id(0) == 0)
    def _():
        width = near_out.shape[0] // 2
        near = [
            pltpu.make_async_copy(
                piece.at[pl.ds(3 * width, width)], near_out.at[pl.ds(j * width, width)], sems.at[10 + j]
            )
            for j, piece in enumerate((a0, a1))
        ]
        for copy in near:
            copy.start()
        load_attention_weights((a2, a3), wqkv, wout, bias, sems)
        for copy in near:
            copy.wait()

    meta = (core, slen, llen, scount, lcount)
    attention_heads_forward(start, count, short_blocks, meta, x, (wqkv, bias, head_bias), qkv, mixed, logs, stat)
    hidden = x[...].astype(F32) + vec[0:1]
    hidden = hidden + nn(mixed_near[...], near_out[...]) + nn(mixed[...], wout[...])
    rows, scale = norm_rows(hidden)
    normed[...] = rows.astype(BF16)
    scale_rows[...] = jnp.broadcast_to(scale, scale_rows.shape)


def weight_copies(side, ups, downs, up_all, down_all, sems):
    half = ups[2].shape[1]
    spans = [pl.ds(pl.multiple_of(at * half, 16), half) for at in (side[0], 1 - side[0])]
    copies = []
    for j in range(2):
        copies.append([(ups[j], up_all.at[j]), (downs[j], down_all.at[j])])
    for j in range(2):
        pairs = []
        for n in range(2):
            part = pl.ds(n * half, half)
            pairs.append((ups[2 + 2 * n + j], up_all.at[2 + j, :, part]))
            pairs.append((downs[2 + j].at[spans[n]], down_all.at[2 + j, part]))
        copies.append(pairs)
    return [
        [pltpu.make_async_copy(s, d, sems.at[4 * j + n]) for n, (s, d) in enumerate(pairs)]
        for j, pairs in enumerate(copies)
    ]


def start_weights(copies):
    for pairs in copies:
        for copy in pairs:
            copy.start()


def wait_weights(copies, step):
    for at in range(2):

        @pl.when(jnp.logical_and(pl.program_id(0) == 0, step == at))
        def _():
            for pairs in copies[2 * at : 2 * at + 2]:
                for copy in pairs:
                    copy.wait()


def ffn_forward_kernel(short_blocks, core, slen, llen, scount, lcount, side, normed, cotangent, *rest):
    ups, downs, biases = rest[0:6], rest[6:10], rest[10:14]
    vec, layer_out, layer_rows, grad_low, slope, down_mine, down_partner, sums = rest[14:22]
    active, down_sum, vec_sum, up_all, down_all, bias_all, total, sems = rest[22:]
    meta = (core, slen, llen, scount, lcount)
    block = pl.program_id(0)
    units = up_all.shape[2]
    half = units // 2
    copies = weight_copies(side, ups, downs, up_all, down_all, sems)

    @pl.when(block == 0)
    def _():
        start_weights(copies)
        down_sum[...] = jnp.zeros_like(down_sum)
        vec_sum[...] = jnp.zeros_like(vec_sum)
        for j in range(2):
            bias_all[j] = biases[j][0:1].astype(F32)
            for n in range(2):
                bias_all[2 + j, :, n * half : (n + 1) * half] = biases[2 + j][9 + n : 10 + n, 0:half].astype(F32)

    first = normed[...].astype(F32) * vec[1:2] + vec[2:3]
    first_low = first.astype(BF16)
    total[...] = first + vec[3:4]

    def groups(step, carry):
        wait_weights(copies, step)
        for e in range(2):
            j = 2 * step + e
            inner = nn(first_low, up_all[j]) + bias_all[j]
            chance = 0.5 * (1.0 + lax.erf(inner * 0.7071067811865476))
            low_units = (inner * chance).astype(BF16)
            slope[:, pl.ds(pl.multiple_of(j * units, units), units)] = (
                chance + inner * jnp.exp(-0.5 * inner * inner) * 0.3989422804014327
            ).astype(BF16)
            active[j] = low_units
            total[...] += nn(low_units, down_all[j])
        return carry

    lax.fori_loop(0, 2, groups, 0)
    rows, scale = norm_rows(total[...])
    result = (rows * vec[4:5] + vec[5:6]).astype(BF16)
    layer_out[...] = result
    layer_rows[...] = result
    position = lax.broadcasted_iota(jnp.int32, (ROWS, 1), 0)
    slot = position // SHORT_LEN
    short_limit = jnp.zeros((ROWS, 1), jnp.int32)
    for n in range(SLOTS):
        short_limit = jnp.where(slot == n, short_valid(meta, jnp.minimum(block, short_blocks - 1), n), short_limit)
    long_limit = long_valid(meta, jnp.maximum(block, short_blocks), short_blocks)
    is_short = block < short_blocks
    alive = jnp.where(is_short, position % SHORT_LEN, position) < jnp.where(
        is_short, short_limit, long_limit
    )
    upstream = jnp.where(alive, cotangent[...].astype(F32), 0.0)
    grad = norm_back(upstream, rows, scale, vec[4:5])
    low = grad.astype(BF16)
    grad_low[...] = low
    vec_sum[0] += fold_rows(upstream * rows)
    vec_sum[1] += fold_rows(upstream)
    vec_sum[2] += fold_rows(grad)
    for j in range(2):
        down_sum[j] += tn(active[j], low)

    @pl.when(block == pl.num_programs(0) - 1)
    def _():
        down_mine[...] = down_sum[0].astype(BF16)
        down_partner[...] = down_sum[1].astype(BF16)
        sums[...] = jnp.zeros_like(sums)
        for n in range(3):
            sums[n : n + 1] = total_rows(vec_sum[n])


def ffn_backward_kernel(side, grad_low, slope, normed, stat, mixed, sums_two, *rest):
    ups, downs = rest[0:6], rest[6:10]
    vec, hidden_low, mine, partner = rest[10:14]
    up_sum, out_sum, vec_sum, kept, up_all, down_all, total, sems = rest[14:]
    block = pl.program_id(0)
    units = up_sum.shape[2]
    width = mixed.shape[1] // 2
    copies = weight_copies(side, ups, downs, up_all, down_all, sems)

    @pl.when(block == 0)
    def _():
        start_weights(copies)
        up_sum[...] = jnp.zeros_like(up_sum)
        out_sum[...] = jnp.zeros_like(out_sum)
        vec_sum[...] = jnp.zeros_like(vec_sum)

    low = grad_low[...]
    total[...] = low.astype(F32)

    def groups(step, carry):
        wait_weights(copies, step)
        for e in range(2):
            j = 2 * step + e
            inner = nt(low, down_all[j]) * slope[:, pl.ds(pl.multiple_of(j * units, units), units)].astype(F32)
            inner_low = inner.astype(BF16)
            total[...] += nt(inner_low, up_all[j])
            vec_sum[j] += fold_rows(inner)
            kept[j] = inner_low
        return carry

    lax.fori_loop(0, 2, groups, 0)
    rows = normed[...].astype(F32)
    first_low = (rows * vec[1:2] + vec[2:3]).astype(BF16)
    for j in range(2):
        up_sum[j] += tn(first_low, kept[j])
    incoming = total[...]
    grad = norm_back(incoming, rows, stat[:, 0:1], vec[1:2])
    vec_sum[4] += fold_rows(incoming * rows)
    vec_sum[5] += fold_rows(incoming)
    vec_sum[6] += fold_rows(grad)
    grad_attn = grad.astype(BF16)
    hidden_low[...] = grad_attn
    out_sum[...] += tn(mixed[...], grad_attn)

    @pl.when(block == pl.num_programs(0) - 1)
    def _():
        index = lax.broadcasted_iota(jnp.int32, (16, 1), 0)
        shared = [sums_two[n : n + 1] for n in range(3)] + [total_rows(vec_sum[n]) for n in range(4, 7)]
        for j, out in enumerate((mine, partner)):
            out[0:units] = up_sum[j].astype(BF16)
            out[units : units + width] = out_sum[j * width : (j + 1) * width].astype(BF16)
            out[units + width :] = jnp.zeros((out.shape[0] - units - width, out.shape[1]), BF16)
            rows_out = jnp.zeros((16, out.shape[1]), F32)
            for n, row in enumerate(shared + [total_rows(vec_sum[j])]):
                rows_out = jnp.where(index == n, row, rows_out)
            out[units + width : units + width + 16] = rows_out.astype(BF16)


def attention_heads_backward(start, short_blocks, meta, logs, qkv, mixed, mixed_grad, low_qkv, delta):
    block = pl.program_id(0) + start
    half = mixed.shape[1]
    own = (mixed_grad[...].astype(F32) * mixed[...].astype(F32)).astype(BF16)
    head = lax.broadcasted_iota(jnp.int32, (8, half), 1) // HEAD_DIM
    pick = jnp.where(head == lax.broadcasted_iota(jnp.int32, (8, half), 0), 1.0, 0.0)
    delta[...] = nt(pick.astype(BF16), own)

    index = lax.broadcasted_iota(jnp.int32, (8, 1), 0)

    def tiles(pair, size, valids):
        column = pl.multiple_of(pair * PAIR, PAIR)
        spans = [pl.ds(n * size, size) for n in range(len(valids))]

        def rows(ref, span):
            picked = [total_rows(jnp.where(index == 2 * pair + e, ref[:, span], 0.0)) for e in range(2)]
            return jnp.concatenate(picked, axis=1)

        q = [stacked(qkv[t, pl.ds(column, PAIR)] * jnp.asarray(0.125, BF16)) for t in spans]
        g = [stacked(mixed_grad[t, pl.ds(column, PAIR)]) for t in spans]
        k = [qkv[t, pl.ds(half + column, PAIR)] for t in spans]
        scores = [nt(b, a) for a, b in zip(q, k)]
        grads = [nt(qkv[t, pl.ds(2 * half + column, PAIR)], a) for t, a in zip(spans, g)]
        place = lax.broadcasted_iota(jnp.int32, (size, 1), 0)
        probs = [
            jnp.where(place < valid, jnp.exp(v - rows(logs, t)), 0.0)
            for v, t, valid in zip(scores, spans, valids)
        ]
        scores = [(p * (v - rows(delta, t))).astype(BF16) for p, v, t in zip(probs, grads, spans)]
        dq = [tn(v, b) for v, b in zip(scores, k)]
        dk = [nn(v, a) for v, a in zip(scores, q)]
        dv = [nn(p.astype(BF16), a) for p, a in zip(probs, g)]
        for t, a, b, c in zip(spans, dq, dk, dv):
            low_qkv[t, pl.ds(column, PAIR)] = (unstacked(a) * 0.125).astype(BF16)
            low_qkv[t, pl.ds(half + column, PAIR)] = b.astype(BF16)
            low_qkv[t, pl.ds(2 * half + column, PAIR)] = c.astype(BF16)

    if start < short_blocks:
        valids = [short_valid(meta, block, slot) for slot in range(SLOTS)]
        size = SHORT_LEN
    else:
        valids = [long_valid(meta, block, short_blocks)]
        size = LONG_LEN

    def body(pair, carry):
        tiles(pair, size, valids)
        return carry

    lax.fori_loop(0, half // PAIR, body, 0)


def attention_backward_kernel(
    start, short_blocks, core, slen, llen, scount, lcount, hidden_low, stat, qkv, mixed, x,
    a0, a1, *rest,
):
    if start:
        sums_in, vec_in, low_qkv, mine, partner = rest[:5]
    else:
        low_qkv, qkv_out, vec_out = rest[:3]
    wqkv, wout, bias, sems, mixed_grad, delta, qkv_sum, vec_sum = rest[-8:]
    meta = (core, slen, llen, scount, lcount)
    block = pl.program_id(0)
    half = mixed.shape[1]
    width = half // 2

    @pl.when(block == 0)
    def _():
        load_attention_weights((a0, a1), wqkv, wout, bias, sems)
        if start:
            qkv_sum[...] = sums_in[...]
            vec_sum[...] = vec_in[...]
        else:
            qkv_sum[...] = jnp.zeros_like(qkv_sum)
            vec_sum[...] = jnp.zeros_like(vec_sum)

    mixed_grad[...] = nt(hidden_low[...], wout[...]).astype(BF16)
    attention_heads_backward(start, short_blocks, meta, stat, qkv, mixed, mixed_grad, low_qkv, delta)
    vec_sum[0] += fold_rows(low_qkv[:, 0:half].astype(F32))
    vec_sum[1] += fold_rows(low_qkv[:, 2 * half : 3 * half].astype(F32))

    for k in range(3):
        qkv_sum[k] += tn(low_qkv[:, k * half : (k + 1) * half], x[...])

    @pl.when(block == pl.num_programs(0) - 1)
    def _():
        if not start:
            qkv_out[...] = qkv_sum[...]
            vec_out[...] = vec_sum[...]
        else:
            index = lax.broadcasted_iota(jnp.int32, (16, 1), 0)
            heads = [total_rows(vec_sum[n]) for n in range(2)]
            for j, out in enumerate((mine, partner)):
                for k in range(3):
                    out[k * width : (k + 1) * width] = qkv_sum[k, j * width : (j + 1) * width].astype(BF16)
                out[3 * width :] = jnp.zeros((out.shape[0] - 3 * width, out.shape[1]), BF16)
                rows_out = jnp.zeros((16, half), F32)
                for n, row in enumerate(heads):
                    row = pltpu.roll(row, half - width, 1) if j else row
                    rows_out = jnp.where(index == n, row, rows_out)
                out[3 * width : 3 * width + 16, 0:half] = rows_out.astype(BF16)


def attention_input_kernel(
    start, short_blocks, core, slen, llen, scount, lcount, hidden_low, stat, qkv, mixed, low_near,
    a2, a3, a0, a1, *rest,
):
    input_rows, input_grad = rest[-10:-8]
    wqkv, wout, bias, near_qkv, sems, low_qkv, mixed_grad, delta = rest[-8:]
    meta = (core, slen, llen, scount, lcount)

    @pl.when(pl.program_id(0) == 0)
    def _():
        width = near_qkv.shape[0] // 6
        near = [
            pltpu.make_async_copy(
                piece.at[pl.ds(k * width, width)],
                near_qkv.at[pl.ds((2 * k + j) * width, width)],
                sems.at[10 + 2 * k + j],
            )
            for k in range(3)
            for j, piece in enumerate((a0, a1))
        ]
        for copy in near:
            copy.start()
        load_attention_weights((a2, a3), wqkv, wout, bias, sems)
        for copy in near:
            copy.wait()

    low = hidden_low[...]
    mixed_grad[...] = nt(low, wout[...]).astype(BF16)
    attention_heads_backward(start, short_blocks, meta, stat, qkv, mixed, mixed_grad, low_qkv, delta)
    total = low.astype(F32) + nn(low_near[...], near_qkv[...]) + nn(low_qkv[...], wqkv[...])
    input_rows[...] = total.astype(BF16)
    input_grad[...] = total


def const_spec(shape):
    return pl.BlockSpec(
        shape, lambda *_: (0,) * len(shape), pipeline_mode=pl.Buffered(1)
    )


def any_spec():
    return pl.BlockSpec(memory_space=pl.ANY)


def own_spec(width, start=0):
    return pl.BlockSpec((ROWS, width), lambda i, *_: (i + start, 0))


def whole_call(body, name, which, operands, shapes, scratch=(), keep=False, limit=24):
    moved = sum(v.size * v.dtype.itemsize for v in list(operands) + list(shapes))
    vmem = pl.BlockSpec(memory_space=pltpu.VMEM)
    if not keep:
        operands = [pltpu.with_memory_space_constraint(v, pltpu.VMEM) for v in operands]
        shapes = [pltpu.VMEM(v.shape, v.dtype) for v in shapes]
    return pl.pallas_call(
        body,
        name=name,
        in_specs=[pl.BlockSpec(memory_space=pltpu.SMEM)] + [vmem] * len(operands),
        out_specs=[vmem] * len(shapes),
        out_shape=shapes,
        scratch_shapes=list(scratch),
        compiler_params=pltpu.CompilerParams(vmem_limit_bytes=limit * 1024 * 1024),
        cost_estimate=pl.CostEstimate(flops=0, bytes_accessed=moved, transcendentals=0),
    )(which, *operands)


def spread(body, name, grid, in_specs, out_specs, out_shape, scratch=(), prefetch=0, flops=0, moved=0, exps=0, alias=None):
    return pl.pallas_call(
        body,
        name=name,
        grid_spec=pltpu.PrefetchScalarGridSpec(
            num_scalar_prefetch=prefetch,
            grid=grid,
            in_specs=in_specs,
            out_specs=out_specs,
            scratch_shapes=list(scratch),
        ),
        out_shape=out_shape,
        input_output_aliases=alias or {},
        compiler_params=pltpu.CompilerParams(
            dimension_semantics=("arbitrary",), vmem_limit_bytes=VMEM_LIMIT
        ),
        cost_estimate=pl.CostEstimate(flops=flops, bytes_accessed=moved, transcendentals=exps),
    )


def per_device(
    tokens,
    cotangent,
    short_len,
    long_len,
    short_count,
    long_count,
    query_weight,
    query_bias,
    key_weight,
    value_weight,
    value_bias,
    output_weight,
    output_bias,
    first_gain,
    first_shift,
    up_weight,
    up_bias,
    down_weight,
    down_bias,
    second_gain,
    second_shift,
):
    d = tokens.shape[1]
    width = query_weight.shape[1]
    units = up_weight.shape[1]
    half = 2 * width
    piece_rows = 4 * width + 16
    short_blocks = short_len.shape[0] * SHORT_LEN // (2 * ROWS)
    long_blocks = long_len.shape[0] * LONG_LEN // (2 * ROWS)
    blocks = short_blocks + long_blocks
    rows = blocks * ROWS
    core = lax.axis_index("tensor") % 2
    side = lax.axis_index("dp") % 2
    core_id = core.astype(jnp.int32).reshape(1)
    meta = (core_id, short_len, long_len, short_count, long_count)
    sds = jax.ShapeDtypeStruct

    def swap(values, bit, axis="tensor"):
        size = lax.axis_size(axis)
        return lax.ppermute(values, axis, [(i, i ^ bit) for i in range(size)])

    def after(value, *others):
        return lax.optimization_barrier((value,) + others)[0]

    def global_spec(start=0, flip=0):
        def index(i, core, *_):
            i = i + start
            first = core[0] if flip == 0 else 1 - core[0]
            return (2 * i + jnp.where(i < short_blocks, first, 1 - first), 0)

        return pl.BlockSpec((ROWS, d), index)

    vec_spec = const_spec((8, d))
    row_spec = own_spec(d)

    side_id = side.astype(jnp.int32).reshape(1)
    line_id = (lax.axis_index("dp") // 2).astype(jnp.int32).reshape(1)
    vectors = [query_bias, value_bias, up_bias, output_bias, first_gain, first_shift,
               down_bias, second_gain, second_shift]
    a0, vec = whole_call(
        pack_kernel, "pack", side_id,
        [query_weight.T, key_weight.T, value_weight.T, output_weight, *vectors],
        [sds((piece_rows, d), BF16), sds((8, d), F32)], [pltpu.VMEM((8, d), F32)], True, 61,
    )
    up_split = lax.dynamic_slice_in_dim(up_weight, side * (units // 2), units // 2, 1)
    def boundary(lead, *values):
        out = lax.optimization_barrier((lead,) + values)
        return out[0], list(out[1:])

    a1 = after(swap(a0, 1), up_split)
    a2 = swap(a0, 2)

    weight_scratch = [
        pltpu.VMEM((3 * half, d), BF16),
        pltpu.VMEM((half, d), BF16),
        pltpu.VMEM((32, d), BF16),
    ]
    sems = pltpu.SemaphoreType.DMA((16,))
    stat_scratch = pltpu.VMEM((ROWS, 128), F32)

    def log_spec(start=0):
        return pl.BlockSpec((8, ROWS), lambda i, *_: (i + start, 0))

    head_shapes = [sds((rows, 3 * half), BF16), sds((rows, half), BF16), sds((8 * blocks, ROWS), F32)]
    head_flops = 2 * rows * d * 3 * half + 4 * rows * 320 * half
    qkv_near, mixed_near, stat_near = spread(
        functools.partial(attention_forward_kernel, 0, blocks, short_blocks), "attention_near", (blocks,),
        [global_spec()] + [any_spec()] * 2, [own_spec(3 * half), own_spec(half), log_spec()], head_shapes,
        weight_scratch + [sems, stat_scratch, pltpu.VMEM((3, 1, half), F32)], 5,
        head_flops, rows * d * 8, rows * 320 * 6,
    )(*meta, tokens, a0, a1)

    stat_near, (a2,) = boundary(stat_near, a2)
    u2 = swap(after(up_split, a2), 2)
    d2 = swap(after(down_weight, a2), 2)
    a3 = swap(a2, 1)
    u1 = swap(after(up_weight, a3), 1)

    def far_forward(start, count, extra, alias):
        return spread(
            functools.partial(attention_finish_kernel, start, count, short_blocks), "attention_far", (count,),
            [global_spec(start)] + [any_spec()] * 2 + [own_spec(half, start)] + [any_spec()] * 2 + [vec_spec]
            + [any_spec()] * len(extra),
            [own_spec(3 * half, start), own_spec(half, start), log_spec(start), own_spec(d, start), own_spec(128, start)],
            head_shapes + [sds((rows, d), BF16), sds((rows, 128), F32)],
            weight_scratch + [pltpu.VMEM((half, d), BF16), sems, stat_scratch, pltpu.VMEM((3, 1, half), F32)], 5,
            (head_flops + 2 * rows * d * d) * count // blocks, count * ROWS * d * 10, count * ROWS * 320 * 6, alias,
        )(*meta, tokens, a2, a3, mixed_near, a0, a1, vec, *extra)

    far = list(far_forward(0, short_blocks, [], None))
    far[3], (u2, u1, down_near) = boundary(far[3], u2, u1, down_weight)
    u4 = swap(u2, 1, "dp")
    u3, d1 = swap(u2, 1), swap(down_near, 1)
    qkv_far, mixed_far, stat_far, normed, scale_one = far_forward(
        short_blocks, long_blocks, far, {12 + n: n for n in range(5)}
    )
    normed, (u4, u3, d2, d1) = boundary(normed, u4, u3, d2, d1)
    u5, d3 = swap(u4, 1), swap(d2, 1)
    ups = (up_weight, u1, u2, u3, u4, u5)
    downs = (down_weight, d1, d2, d3)
    bias_spec = pl.BlockSpec((16, d), lambda *_: (4 * width // 16, 0), pipeline_mode=pl.Buffered(1))
    up_specs = [any_spec()] * len(ups)
    down_specs = [any_spec()] * len(downs)
    ffn_scratch = [
        pltpu.VMEM((4, d, units), BF16),
        pltpu.VMEM((4, units, d), BF16),
    ]
    ffn_sems = pltpu.SemaphoreType.DMA((16,))
    whole_out, out_rows, grad_low, slope, down_mine, down_partner, sums_two = spread(
        functools.partial(ffn_forward_kernel, short_blocks), "ffn_forward", (blocks,),
        [row_spec, global_spec()] + up_specs + down_specs + [bias_spec] * 4 + [vec_spec],
        [global_spec(), row_spec, row_spec, own_spec(4 * units)] + [const_spec((units, d))] * 2 + [vec_spec],
        [sds((2 * rows, d), BF16), sds((rows, d), BF16), sds((rows, d), BF16), sds((rows, 4 * units), BF16)]
        + [sds((units, d), BF16)] * 2 + [sds((8, d), F32)],
        [pltpu.VMEM((4, ROWS, units), BF16), pltpu.VMEM((2, units, d), F32), pltpu.VMEM((3, 8, d), F32)]
        + ffn_scratch + [pltpu.VMEM((4, 1, units), F32), pltpu.VMEM((ROWS, d), F32), ffn_sems],
        6, 2 * rows * d * 10 * units, rows * d * 20, rows * 8 * units,
    )(*meta, side_id, normed, cotangent, *ups, *downs, a0, a1, a2, a3, vec)

    custom = lax.axis_size("dp") == 8

    line_steps = (
        [(0, 1), (3, 2)],
        [(1, 2), (2, 1)],
        [(1, 0), (2, 3)],
    )

    def along_line(values, stage):
        pairs = [(2 * i + n, 2 * j + n) for i, j in line_steps[stage] for n in range(2)]
        return lax.ppermute(values, "dp", pairs)

    class Reduction:
        def __init__(self, mine, partner, central):
            self.mine, self.size, self.central = mine, mine.shape[0], central
            self.moved = [swap(partner, 1)]
            self.stage = 0

        def part(self, count):
            return sds((self.size // count, d), BF16)

        def step(self):
            got = self.moved
            stage, self.stage = self.stage, self.stage + 1
            if not custom:
                if stage == 0:
                    total = (self.mine.astype(F32) + got[0].astype(F32)).astype(BF16)
                    self.moved = [lax.psum(total, "dp")]
                return self.moved[0]
            if stage == 0:
                self.keep, send = whole_call(
                    route_halves_kernel, "halves", side_id, [self.mine, got[0]], [self.part(2)] * 2
                )
                sent, self.moved = [send], [swap(send, 1, "dp")]
            elif self.central and stage < 4:
                (self.keep,) = whole_call(add_kernel, "add", line_id, [self.keep, got[0]], [self.part(2)])
                sent, self.moved = [self.keep], [along_line(self.keep, stage - 1)]
            elif self.central and stage == 4:
                (self.keep,) = whole_call(choose_kernel, "choose", line_id, [self.keep, got[0]], [self.part(2)])
                sent, self.moved = [self.keep], [swap(self.keep, 1, "dp")]
            elif stage == 1:
                self.keep, *sent = whole_call(
                    route_quarters_kernel, "quarters", line_id, [self.keep, got[0]], [self.part(8)] * 4
                )
                self.moved = [swap(v, 2 * (k + 1), "dp") for k, v in enumerate(sent)]
            elif stage == 2:
                (self.keep,) = whole_call(add_kernel, "add", line_id, [self.keep, *got], [self.part(8)])
                sent = [self.keep]
                self.moved = [swap(self.keep, 2 * k, "dp") for k in (1, 2, 3)]
            elif stage == 3:
                (self.keep,) = whole_call(
                    join_kernel, "join_quarters", line_id, [self.keep, *got], [self.part(2)]
                )
                sent, self.moved = [self.keep], [swap(self.keep, 1, "dp")]
            return sent[0]

        def finish(self, *sizes):
            shapes = [sds((n, d), F32) for n in sizes]
            if not custom:
                total = self.moved[0].astype(F32)
                cuts = [sum(sizes[:n]) for n in range(len(sizes))]
                return [total[at : at + n] for at, n in zip(cuts, sizes)]
            operands = [self.keep, self.moved[0]]
            return whole_call(
                finish_kernel, "finish", side_id, operands, shapes, [pltpu.VMEM((self.size, d), F32)], True
            )

    def settle(lead, reductions, *extra):
        lead, values = boundary(lead, *[v for r in reductions for v in r.moved], *extra)
        for r in reductions:
            count = len(r.moved)
            r.moved, values = values[:count], values[count:]
        return (lead, *values)

    grad_low, down_mine, down_partner = lax.optimization_barrier((grad_low, down_mine, down_partner))
    down_reduce = Reduction(down_mine, down_partner, True)
    tie = down_reduce.step()
    grad_low = after(grad_low, tie)
    moved_out = swap(after(out_rows, tie), 1)

    pack_rows = units + width + 64
    hidden_low, mine, partner = spread(
        ffn_backward_kernel, "ffn_backward", (blocks,),
        [row_spec, own_spec(4 * units), row_spec, own_spec(128), own_spec(half), vec_spec]
        + up_specs + down_specs + [vec_spec],
        [row_spec] + [const_spec((pack_rows, d))] * 2,
        [sds((rows, d), BF16)] + [sds((pack_rows, d), BF16)] * 2,
        [pltpu.VMEM((2, d, units), F32), pltpu.VMEM((half, d), F32), pltpu.VMEM((7, 8, d), F32),
         pltpu.VMEM((4, ROWS, units), BF16)] + ffn_scratch + [pltpu.VMEM((ROWS, d), F32), ffn_sems],
        1, 2 * rows * d * 10 * units, rows * d * 16, 0,
    )(side_id, grad_low, slope, normed, scale_one, mixed_near, sums_two, *ups, *downs, vec)
    hidden_low, mine, partner, moved_out = settle(hidden_low, [down_reduce], mine, partner, moved_out)
    tie = down_reduce.step()
    partner = after(partner, tie)
    up_reduce = Reduction(mine, partner, True)
    tie = up_reduce.step()
    hidden_low = after(hidden_low, tie)

    qkv_rows = 3 * width + 64
    sums = [sds((3, half, d), F32), sds((2, 8, half), F32)]
    sum_specs = [const_spec(v.shape) for v in sums]

    def near_backward(start, count, extra, extra_specs, outs, out_specs, alias):
        return spread(
            functools.partial(attention_backward_kernel, start, short_blocks), "attention_near_backward", (count,),
            [own_spec(d, start), log_spec(start), own_spec(3 * half, start), own_spec(half, start), global_spec(start)]
            + [any_spec()] * 2 + extra_specs,
            [own_spec(3 * half)] + out_specs,
            [sds((count * ROWS, 3 * half), BF16)] + outs,
            weight_scratch + [sems, pltpu.VMEM((ROWS, half), BF16), pltpu.VMEM((8, ROWS), F32),
                              pltpu.VMEM((3, half, d), F32), pltpu.VMEM((2, 8, half), F32)],
            5, count * ROWS * (10 * d * half + 3200 * half), count * ROWS * d * 16, count * ROWS * 320 * 6,
        )(*meta, hidden_low, stat_near, qkv_near, mixed_near, tokens, a0, a1, *extra)

    low_short, *sums_short = near_backward(0, short_blocks, [], [], sums, sum_specs, None)
    (low_short,) = settle(low_short, [down_reduce, up_reduce])
    tie = down_reduce.step()
    tie_two = up_reduce.step()
    sums_short[1] = after(sums_short[1], tie, tie_two)
    low_long, mine, partner = near_backward(
        short_blocks, long_blocks, sums_short, sum_specs,
        [sds((qkv_rows, d), BF16)] * 2, [const_spec((qkv_rows, d))] * 2, None,
    )
    low_long, mine, partner = settle(low_long, [down_reduce, up_reduce], mine, partner)
    ties = [down_reduce.step(), up_reduce.step()]
    qkv_reduce = Reduction(mine, after(partner, *ties), False)
    ties += [qkv_reduce.step()]

    def far_backward(start, count, low_near, extra, alias):
        return spread(
            functools.partial(attention_input_kernel, start, short_blocks), "attention_far_backward", (count,),
            [own_spec(d, start), log_spec(start), own_spec(3 * half, start), own_spec(half, start), own_spec(3 * half)]
            + [any_spec()] * (4 + len(extra)),
            [own_spec(d, start), global_spec(start)], [sds((rows, d), BF16), sds((2 * rows, d), F32)],
            weight_scratch + [pltpu.VMEM((3 * half, d), BF16), sems, pltpu.VMEM((ROWS, 3 * half), BF16),
                              pltpu.VMEM((ROWS, half), BF16), pltpu.VMEM((8, ROWS), F32)],
            5, count * ROWS * (14 * d * half + 3200 * half), count * ROWS * d * 16, count * ROWS * 320 * 6, alias,
        )(*meta, hidden_low, stat_far, qkv_far, mixed_far, low_near, a2, a3, a0, a1, *extra)

    low_short = after(low_short, *ties)
    rows_short, whole_in = far_backward(0, short_blocks, low_short, [], None)
    (rows_short,) = settle(rows_short, [down_reduce, up_reduce, qkv_reduce])
    ties = [qkv_reduce.step(), up_reduce.step(), down_reduce.step()]
    low_long = after(low_long, *ties)
    rows_all, whole_in = far_backward(
        short_blocks, long_blocks, low_long, [rows_short, whole_in], {14: 0, 15: 1}
    )
    (rows_all,) = settle(rows_all, [down_reduce, up_reduce, qkv_reduce])
    tie = qkv_reduce.step()
    tie = after(tie, up_reduce.step())
    down_reduce.moved[0] = after(down_reduce.moved[0], tie)
    (grad_down,) = down_reduce.finish(units)
    moved_rows = swap(after(rows_all, tie), 1)

    def place(whole, other, start, count):
        return spread(
            place_kernel, "place", (count,), [own_spec(d), any_spec()], global_spec(start, 1),
            sds(whole.shape, whole.dtype), (), 1, 0, other.size * 6, 0, {2: 0},
        )(core_id, other, whole)

    layer_output = place(whole_out, after(moved_out, tie), 0, blocks)
    layer_output, moved_rows = settle(layer_output, [qkv_reduce], moved_rows)
    tie = qkv_reduce.step()
    input_grad = place(whole_in, after(moved_rows, tie), 0, blocks)
    up_reduce.moved[0] = after(up_reduce.moved[0], tie)
    grad_up, grad_out, small = up_reduce.finish(units, width, 16)
    grad_up, input_grad = settle(grad_up, [qkv_reduce], input_grad)
    grad_query, grad_key, grad_value, heads = qkv_reduce.finish(width, width, width, 16)
    return (
        layer_output,
        input_grad,
        grad_query.T,
        heads[0, :width],
        grad_key.T,
        grad_value.T,
        heads[1, :width],
        grad_out,
        small[5],
        small[3],
        small[4],
        grad_up,
        small[6],
        grad_down,
        small[2],
        small[0],
        small[1],
    )

def solution(mesh):
    return jax.shard_map(
        per_device,
        mesh=mesh,
        in_specs=(
            P("dp", None),
            P("dp", None),
            P("dp"),
            P("dp"),
            P("dp"),
            P("dp"),
            P(None, "tensor"),
            P("tensor"),
            P(None, "tensor"),
            P(None, "tensor"),
            P("tensor"),
            P("tensor", None),
            P(),
            P(),
            P(),
            P(None, "tensor"),
            P("tensor"),
            P("tensor", None),
            P(),
            P(),
            P(),
        ),
        out_specs=(
            P("dp", None),
            P("dp", None),
            P(None, "tensor"),
            P("tensor"),
            P(None, "tensor"),
            P(None, "tensor"),
            P("tensor"),
            P("tensor", None),
            P(),
            P(),
            P(),
            P(None, "tensor"),
            P("tensor"),
            P("tensor", None),
            P(),
            P(),
            P(),
        ),
        check_vma=False,
    )
```

```python
import functools

import jax
import jax.numpy as jnp
from jax import lax
from jax.experimental import pallas as pl
from jax.experimental.pallas import tpu as pltpu
from jax.sharding import PartitionSpec as P

HEAD_DIM = 64
SHORT_LEN = 128
LONG_LEN = 512
ROWS = 512
SLOTS = ROWS // SHORT_LEN
PAIR = 2 * HEAD_DIM
MASKED = -30000.0
F32 = jnp.float32
BF16 = jnp.bfloat16
VMEM_LIMIT = 60 * 1024 * 1024


def nn(left, right):
    return lax.dot_general(left, right, (((1,), (0,)), ((), ())), preferred_element_type=F32)


def nt(left, right):
    return lax.dot_general(left, right, (((1,), (1,)), ((), ())), preferred_element_type=F32)


def tn(left, right):
    return lax.dot_general(left, right, (((0,), (0,)), ((), ())), preferred_element_type=F32)


def fold_rows(values):
    return jnp.sum(values.reshape(-1, 8, values.shape[-1]), axis=0)


def total_rows(values):
    return jnp.sum(values, axis=0, keepdims=True)


def by_rows(size, body):
    def step(n, carry):
        body(pl.ds(pl.multiple_of(n * 64, 64), 64))
        return carry

    lax.fori_loop(0, size // 64, step, 0)


def clear(ref):
    def body(span):
        for j in range(ref.shape[0]):
            ref[j, span] = jnp.zeros((64, ref.shape[2]), ref.dtype)

    by_rows(ref.shape[1], body)


def copy_rows(source, target, at=0):
    def body(span):
        target[pl.ds(pl.multiple_of(at + span.start, 16), 64)] = source[span].astype(target.dtype)

    if source.shape[0] % 64:
        target[pl.ds(at, source.shape[0])] = source[...].astype(target.dtype)
    else:
        by_rows(source.shape[0], body)


def half_mask(which):
    lanes = lax.broadcasted_iota(jnp.int32, (1, PAIR), 1)
    return (lanes >= HEAD_DIM) if which else (lanes < HEAD_DIM)


def short_valid(meta, block, slot):
    index = SLOTS * (2 * block + meta[0][0]) + slot
    return jnp.where(index < meta[3][0], meta[1][index], 0)


def long_valid(meta, block, short_blocks):
    index = 2 * (block - short_blocks) + 1 - meta[0][0]
    return jnp.where(index < meta[4][0], meta[2][index], 0)


def norm_rows(values):
    centre = values - jnp.mean(values, axis=-1, keepdims=True)
    scale = lax.rsqrt(jnp.mean(centre * centre, axis=-1, keepdims=True) + 1e-12)
    return centre * scale, scale


def norm_back(incoming, normed, scale, gain):
    grad = incoming * gain
    inner = grad - jnp.mean(grad, axis=-1, keepdims=True)
    inner = inner - normed * jnp.mean(grad * normed, axis=-1, keepdims=True)
    return scale * inner


def load_attention_weights(pieces, wqkv, wout, bias, sems):
    width = wqkv.shape[0] // 6
    copies = []
    for j, piece in enumerate(pieces):
        for k in range(3):
            copies.append(
                (piece.at[pl.ds(k * width, width)], wqkv.at[pl.ds((2 * k + j) * width, width)])
            )
        copies.append((piece.at[pl.ds(3 * width, width)], wout.at[pl.ds(j * width, width)]))
        copies.append((piece.at[pl.ds(4 * width, 16)], bias.at[pl.ds(16 * j, 16)]))
    started = [pltpu.make_async_copy(s, d, sems.at[n]) for n, (s, d) in enumerate(copies)]
    for copy in started:
        copy.start()
    for copy in started:
        copy.wait()


def flat_row(ref):
    return ref[...].astype(F32).reshape(1, ref.shape[0])


def pack_kernel(at, wq, wk, wv, wo, qb, vb, ub, ob, g1, s1, db, g2, s2, piece, vec, wide):
    width = wq.shape[0]
    d = piece.shape[1]
    piece[0:width] = wq[...]
    piece[width : 2 * width] = wk[...]
    piece[2 * width : 3 * width] = wv[...]
    piece[3 * width : 4 * width] = wo[...]
    index = lax.broadcasted_iota(jnp.int32, (16, 1), 0)
    wide[...] = jnp.zeros_like(wide)
    wide[0:1, 0:width] = flat_row(qb)
    wide[1:2, 0:width] = flat_row(vb)
    row_q, row_v, row_u = wide[0:1], wide[1:2], flat_row(ub)
    lead = jnp.where(lax.broadcasted_iota(jnp.int32, (1, d), 1) < d // 2, row_u, 0.0)
    trail = pltpu.roll(row_u - lead, d // 2, 1)
    mine = jnp.where(at[0] == 0, lead, trail)
    far = jnp.where(at[0] == 0, trail, lead)
    rows = [row_u, row_q, pltpu.roll(row_q, width, 1), row_v, pltpu.roll(row_v, width, 1)]
    block = jnp.zeros((16, d), F32)
    for n, row in enumerate(rows + [None] * 4 + [mine, far]):
        if row is not None:
            block = jnp.where(index == n, row, block)
    piece[4 * width : 4 * width + 16] = block.astype(BF16)
    for n, row in enumerate((ob, g1, s1, db, g2, s2)):
        vec[n : n + 1] = flat_row(row)
    vec[6:8] = jnp.zeros((2, d), F32)


def place_kernel(core, other, whole, out):
    out[...] = other[...].astype(out.dtype)


def route_halves_kernel(at, mine, partner, keep, send):
    half = keep.shape[0]
    for out, which in ((keep, at[0]), (send, 1 - at[0])):
        base = which * half

        def body(span):
            rows = pl.ds(pl.multiple_of(base + span.start, 16), 64)
            out[span] = (mine[rows].astype(F32) + partner[rows].astype(F32)).astype(BF16)

        by_rows(half, body)


def route_quarters_kernel(at, keep, other, *outs):
    size = outs[0].shape[0]
    for k, out in enumerate(outs):
        span = pl.ds(pl.multiple_of((at[0] ^ k) * size, 16), size)
        out[...] = (keep[span].astype(F32) + other[span].astype(F32)).astype(BF16)


def add_kernel(at, *refs):
    def body(span):
        refs[-1][span] = sum(ref[span].astype(F32) for ref in refs[:-1]).astype(BF16)

    size = refs[-1].shape[0]
    if size % 64:
        body(pl.ds(0, size))
    else:
        by_rows(size, body)


def choose_kernel(at, own, other, out):
    central = jnp.logical_or(at[0] == 1, at[0] == 2)

    @pl.when(central)
    def _():
        out[...] = own[...]

    @pl.when(jnp.logical_not(central))
    def _():
        out[...] = other[...]


def join_kernel(at, *refs):
    out = refs[-1]
    size = refs[0].shape[0]
    for k, ref in enumerate(refs[:-1]):
        copy_rows(ref, out, pl.multiple_of((at[0] ^ k) * size, 16))


def finish_kernel(at, own, other, *refs):
    outs, whole = refs[:-1], refs[-1]
    join_kernel(at, own, other, whole)
    start = 0
    for out in outs:
        copy_rows(whole.at[pl.ds(start, out.shape[0])], out)
        start += out.shape[0]


def stacked(values):
    zero = jnp.zeros_like(values)
    return jnp.concatenate([jnp.where(half_mask(e), values, zero) for e in range(2)], axis=0)


def unstacked(values):
    size = values.shape[0] // 2
    return jnp.where(half_mask(0), values[:size], values[size:])


def attention_heads_forward(start, count, short_blocks, meta, x, weights, qkv, mixed, logs, stat):
    wqkv, bias, head_bias = weights
    block = pl.program_id(0) + start
    half = mixed.shape[1]

    @pl.when(pl.program_id(0) == 0)
    def _():
        small = bias[...].astype(F32)
        head_bias[0] = (small[1:2] + small[18:19])[:, 0:half]
        head_bias[1] = jnp.zeros((1, half), F32)
        head_bias[2] = (small[3:4] + small[20:21])[:, 0:half]

    def project(k, carry):
        span = pl.ds(pl.multiple_of(k * half, half), half)
        qkv[:, span] = (nt(x[...], wqkv[span]) + head_bias[k]).astype(BF16)
        return carry

    lax.fori_loop(0, 3, project, 0)
    stat[...] = jnp.zeros_like(stat)
    lanes = lax.broadcasted_iota(jnp.int32, (1, 128), 1)

    def tiles(pair, spans):
        column = pl.multiple_of(pair * PAIR, PAIR)
        q, scores = [], []
        for query_at, queries, key_at, keys, valid in spans:
            part = qkv[query_at : query_at + queries, pl.ds(column, PAIR)] * jnp.asarray(0.125, BF16)
            key_part = qkv[key_at : key_at + keys, pl.ds(half + column, PAIR)]
            scores.append(nt(stacked(part), key_part))
        live = [lax.broadcasted_iota(jnp.int32, (1, t[3]), 1) < t[4] for t in spans]
        scores = [jnp.where(a, v, MASKED) for a, v in zip(live, scores)]
        top = [jnp.max(v, axis=-1, keepdims=True) for v in scores]
        weights = [jnp.exp(v - m) for v, m in zip(scores, top)]
        total = [jnp.sum(v, axis=-1, keepdims=True) for v in weights]
        out = [
            nn(v.astype(BF16), qkv[t[2] : t[2] + t[3], pl.ds(2 * half + column, PAIR)])
            for v, t in zip(weights, spans)
        ]
        for (query_at, queries, *_), m, n, v in zip(spans, top, total, out):
            log = m + jnp.log(n)
            rows = stat[query_at : query_at + queries]
            rows = jnp.where(lanes == 2 * pair, log[:queries], rows)
            stat[query_at : query_at + queries] = jnp.where(lanes == 2 * pair + 1, log[queries:], rows)
            mixed[query_at : query_at + queries, pl.ds(column, PAIR)] = unstacked(v * (1.0 / n)).astype(BF16)

    def short_path():
        spans = [
            (slot * SHORT_LEN, SHORT_LEN, slot * SHORT_LEN, SHORT_LEN, short_valid(meta, block, slot))
            for slot in range(SLOTS)
        ]

        def body(pair, carry):
            tiles(pair, spans)
            return carry

        lax.fori_loop(0, half // PAIR, body, 0)

    def long_path():
        valid = long_valid(meta, block, short_blocks)
        spans = [(part * 256, 256, 0, LONG_LEN, valid) for part in range(2)]

        def body(pair, carry):
            tiles(pair, spans)
            return carry

        lax.fori_loop(0, half // PAIR, body, 0)

    if start < short_blocks:
        pl.when(block < short_blocks)(short_path)
    if start + count > short_blocks:
        pl.when(block >= short_blocks)(long_path)
    logs[...] = stat[...].T[0:8]


def attention_forward_kernel(
    start, count, short_blocks, core, slen, llen, scount, lcount, x, a0, a1, qkv, mixed, logs,
    wqkv, wout, bias, sems, stat, head_bias,
):
    @pl.when(pl.program_id(0) == 0)
    def _():
        load_attention_weights((a0, a1), wqkv, wout, bias, sems)

    meta = (core, slen, llen, scount, lcount)
    attention_heads_forward(start, count, short_blocks, meta, x, (wqkv, bias, head_bias), qkv, mixed, logs, stat)


def attention_finish_kernel(
    start, count, short_blocks, core, slen, llen, scount, lcount, x, a2, a3, mixed_near, a0, a1, vec, *rest,
):
    qkv, mixed, logs, normed, scale_rows, wqkv, wout, bias, near_out, sems, stat, head_bias = rest[-12:]

    @pl.when(pl.program_id(0) == 0)
    def _():
        width = near_out.shape[0] // 2
        near = [
            pltpu.make_async_copy(
                piece.at[pl.ds(3 * width, width)], near_out.at[pl.ds(j * width, width)], sems.at[10 + j]
            )
            for j, piece in enumerate((a0, a1))
        ]
        for copy in near:
            copy.start()
        load_attention_weights((a2, a3), wqkv, wout, bias, sems)
        for copy in near:
            copy.wait()

    meta = (core, slen, llen, scount, lcount)
    attention_heads_forward(start, count, short_blocks, meta, x, (wqkv, bias, head_bias), qkv, mixed, logs, stat)
    hidden = x[...].astype(F32) + vec[0:1]
    hidden = hidden + nn(mixed_near[...], near_out[...]) + nn(mixed[...], wout[...])
    rows, scale = norm_rows(hidden)
    normed[...] = rows.astype(BF16)
    scale_rows[...] = jnp.broadcast_to(scale, scale_rows.shape)


def weight_copies(side, ups, downs, up_all, down_all, sems):
    half = ups[2].shape[1]
    spans = [pl.ds(pl.multiple_of(at * half, 16), half) for at in (side[0], 1 - side[0])]
    copies = []
    for j in range(2):
        copies.append([(ups[j], up_all.at[j]), (downs[j], down_all.at[j])])
    for j in range(2):
        pairs = []
        for n in range(2):
            part = pl.ds(n * half, half)
            pairs.append((ups[2 + 2 * n + j], up_all.at[2 + j, :, part]))
            pairs.append((downs[2 + j].at[spans[n]], down_all.at[2 + j, part]))
        copies.append(pairs)
    return [
        [pltpu.make_async_copy(s, d, sems.at[4 * j + n]) for n, (s, d) in enumerate(pairs)]
        for j, pairs in enumerate(copies)
    ]


def start_weights(copies):
    for pairs in copies:
        for copy in pairs:
            copy.start()


def wait_weights(copies, step):
    for at in range(2):

        @pl.when(jnp.logical_and(pl.program_id(0) == 0, step == at))
        def _():
            for pairs in copies[2 * at : 2 * at + 2]:
                for copy in pairs:
                    copy.wait()


def ffn_forward_kernel(short_blocks, core, slen, llen, scount, lcount, side, normed, cotangent, *rest):
    ups, downs, biases = rest[0:6], rest[6:10], rest[10:14]
    vec, layer_out, layer_rows, grad_low, slope, down_mine, down_partner, sums = rest[14:22]
    active, down_sum, vec_sum, up_all, down_all, bias_all, total, sems = rest[22:]
    meta = (core, slen, llen, scount, lcount)
    block = pl.program_id(0)
    units = up_all.shape[2]
    half = units // 2
    copies = weight_copies(side, ups, downs, up_all, down_all, sems)

    @pl.when(block == 0)
    def _():
        start_weights(copies)
        clear(down_sum)
        vec_sum[...] = jnp.zeros_like(vec_sum)
        for j in range(2):
            bias_all[j] = biases[j][0:1].astype(F32)
            for n in range(2):
                bias_all[2 + j, :, n * half : (n + 1) * half] = biases[2 + j][9 + n : 10 + n, 0:half].astype(F32)

    first = normed[...].astype(F32) * vec[1:2] + vec[2:3]
    first_low = first.astype(BF16)
    total[...] = first + vec[3:4]

    def groups(step, carry):
        wait_weights(copies, step)
        for e in range(2):
            j = 2 * step + e
            inner = nn(first_low, up_all[j]) + bias_all[j]
            chance = 0.5 * (1.0 + lax.erf(inner * 0.7071067811865476))
            low_units = (inner * chance).astype(BF16)
            slope[:, pl.ds(pl.multiple_of(j * units, units), units)] = (
                chance + inner * jnp.exp(-0.5 * inner * inner) * 0.3989422804014327
            ).astype(BF16)
            active[j] = low_units
            total[...] += nn(low_units, down_all[j])
        return carry

    lax.fori_loop(0, 2, groups, 0)
    rows, scale = norm_rows(total[...])
    result = (rows * vec[4:5] + vec[5:6]).astype(BF16)
    layer_out[...] = result
    layer_rows[...] = result
    position = lax.broadcasted_iota(jnp.int32, (ROWS, 1), 0)
    slot = position // SHORT_LEN
    short_limit = jnp.zeros((ROWS, 1), jnp.int32)
    for n in range(SLOTS):
        short_limit = jnp.where(slot == n, short_valid(meta, jnp.minimum(block, short_blocks - 1), n), short_limit)
    long_limit = long_valid(meta, jnp.maximum(block, short_blocks), short_blocks)
    is_short = block < short_blocks
    alive = jnp.where(is_short, position % SHORT_LEN, position) < jnp.where(
        is_short, short_limit, long_limit
    )
    upstream = jnp.where(alive, cotangent[...].astype(F32), 0.0)
    grad = norm_back(upstream, rows, scale, vec[4:5])
    low = grad.astype(BF16)
    grad_low[...] = low
    vec_sum[0] += fold_rows(upstream * rows)
    vec_sum[1] += fold_rows(upstream)
    vec_sum[2] += fold_rows(grad)
    for j in range(2):
        down_sum[j] += tn(active[j], low)

    @pl.when(block == pl.num_programs(0) - 1)
    def _():
        copy_rows(down_sum.at[0], down_mine)
        copy_rows(down_sum.at[1], down_partner)
        sums[...] = jnp.zeros_like(sums)
        for n in range(3):
            sums[n : n + 1] = total_rows(vec_sum[n])


def ffn_backward_kernel(side, grad_low, slope, normed, stat, mixed, sums_two, *rest):
    ups, downs = rest[0:6], rest[6:10]
    vec, hidden_low, mine, partner = rest[10:14]
    up_sum, out_sum, vec_sum, kept, up_all, down_all, total, sems = rest[14:]
    block = pl.program_id(0)
    units = up_sum.shape[2]
    width = mixed.shape[1] // 2
    copies = weight_copies(side, ups, downs, up_all, down_all, sems)

    @pl.when(block == 0)
    def _():
        start_weights(copies)
        clear(up_sum)
        out_sum[...] = jnp.zeros_like(out_sum)
        vec_sum[...] = jnp.zeros_like(vec_sum)

    low = grad_low[...]
    total[...] = low.astype(F32)

    def groups(step, carry):
        wait_weights(copies, step)
        for e in range(2):
            j = 2 * step + e
            inner = nt(low, down_all[j]) * slope[:, pl.ds(pl.multiple_of(j * units, units), units)].astype(F32)
            inner_low = inner.astype(BF16)
            total[...] += nt(inner_low, up_all[j])
            vec_sum[j] += fold_rows(inner)
            kept[j] = inner_low
        return carry

    lax.fori_loop(0, 2, groups, 0)
    rows = normed[...].astype(F32)
    first_low = (rows * vec[1:2] + vec[2:3]).astype(BF16)
    for j in range(2):
        up_sum[j] += tn(first_low, kept[j])
    incoming = total[...]
    grad = norm_back(incoming, rows, stat[:, 0:1], vec[1:2])
    vec_sum[4] += fold_rows(incoming * rows)
    vec_sum[5] += fold_rows(incoming)
    vec_sum[6] += fold_rows(grad)
    grad_attn = grad.astype(BF16)
    hidden_low[...] = grad_attn
    out_sum[...] += tn(mixed[...], grad_attn)

    @pl.when(block == pl.num_programs(0) - 1)
    def _():
        index = lax.broadcasted_iota(jnp.int32, (16, 1), 0)
        shared = [sums_two[n : n + 1] for n in range(3)] + [total_rows(vec_sum[n]) for n in range(4, 7)]
        for j, out in enumerate((mine, partner)):
            copy_rows(up_sum.at[j], out)
            copy_rows(out_sum.at[pl.ds(j * width, width)], out, units)
            out[units + width :] = jnp.zeros((out.shape[0] - units - width, out.shape[1]), BF16)
            rows_out = jnp.zeros((16, out.shape[1]), F32)
            for n, row in enumerate(shared + [total_rows(vec_sum[j])]):
                rows_out = jnp.where(index == n, row, rows_out)
            out[units + width : units + width + 16] = rows_out.astype(BF16)


def attention_heads_backward(start, short_blocks, meta, logs, qkv, mixed, mixed_grad, low_qkv, delta):
    block = pl.program_id(0) + start
    half = mixed.shape[1]
    own = (mixed_grad[...].astype(F32) * mixed[...].astype(F32)).astype(BF16)
    head = lax.broadcasted_iota(jnp.int32, (8, half), 1) // HEAD_DIM
    pick = jnp.where(head == lax.broadcasted_iota(jnp.int32, (8, half), 0), 1.0, 0.0)
    delta[...] = nt(pick.astype(BF16), own)

    index = lax.broadcasted_iota(jnp.int32, (8, 1), 0)

    def tiles(pair, size, valids):
        column = pl.multiple_of(pair * PAIR, PAIR)
        spans = [pl.ds(n * size, size) for n in range(len(valids))]

        def rows(ref, span):
            picked = [total_rows(jnp.where(index == 2 * pair + e, ref[:, span], 0.0)) for e in range(2)]
            return jnp.concatenate(picked, axis=1)

        q = [stacked(qkv[t, pl.ds(column, PAIR)] * jnp.asarray(0.125, BF16)) for t in spans]
        g = [stacked(mixed_grad[t, pl.ds(column, PAIR)]) for t in spans]
        k = [qkv[t, pl.ds(half + column, PAIR)] for t in spans]
        scores = [nt(b, a) for a, b in zip(q, k)]
        grads = [nt(qkv[t, pl.ds(2 * half + column, PAIR)], a) for t, a in zip(spans, g)]
        place = lax.broadcasted_iota(jnp.int32, (size, 1), 0)
        probs = [
            jnp.where(place < valid, jnp.exp(v - rows(logs, t)), 0.0)
            for v, t, valid in zip(scores, spans, valids)
        ]
        scores = [(p * (v - rows(delta, t))).astype(BF16) for p, v, t in zip(probs, grads, spans)]
        dq = [tn(v, b) for v, b in zip(scores, k)]
        dk = [nn(v, a) for v, a in zip(scores, q)]
        dv = [nn(p.astype(BF16), a) for p, a in zip(probs, g)]
        for t, a, b, c in zip(spans, dq, dk, dv):
            low_qkv[t, pl.ds(column, PAIR)] = (unstacked(a) * 0.125).astype(BF16)
            low_qkv[t, pl.ds(half + column, PAIR)] = b.astype(BF16)
            low_qkv[t, pl.ds(2 * half + column, PAIR)] = c.astype(BF16)

    if start < short_blocks:
        valids = [short_valid(meta, block, slot) for slot in range(SLOTS)]
        size = SHORT_LEN
    else:
        valids = [long_valid(meta, block, short_blocks)]
        size = LONG_LEN

    def body(pair, carry):
        tiles(pair, size, valids)
        return carry

    lax.fori_loop(0, half // PAIR, body, 0)


def attention_backward_kernel(
    start, short_blocks, core, slen, llen, scount, lcount, hidden_low, stat, qkv, mixed, x,
    a0, a1, *rest,
):
    if start:
        sums_in, vec_in, low_qkv, mine, partner = rest[:5]
    else:
        low_qkv, qkv_out, vec_out = rest[:3]
    wqkv, wout, bias, sems, mixed_grad, delta, qkv_sum, vec_sum = rest[-8:]
    meta = (core, slen, llen, scount, lcount)
    block = pl.program_id(0)
    half = mixed.shape[1]
    width = half // 2

    @pl.when(block == 0)
    def _():
        load_attention_weights((a0, a1), wqkv, wout, bias, sems)
        if start:
            qkv_sum[...] = sums_in[...]
            vec_sum[...] = vec_in[...]
        else:
            clear(qkv_sum)
            vec_sum[...] = jnp.zeros_like(vec_sum)

    mixed_grad[...] = nt(hidden_low[...], wout[...]).astype(BF16)
    attention_heads_backward(start, short_blocks, meta, stat, qkv, mixed, mixed_grad, low_qkv, delta)
    vec_sum[0] += fold_rows(low_qkv[:, 0:half].astype(F32))
    vec_sum[1] += fold_rows(low_qkv[:, 2 * half : 3 * half].astype(F32))

    for k in range(3):
        qkv_sum[k] += tn(low_qkv[:, k * half : (k + 1) * half], x[...])

    @pl.when(block == pl.num_programs(0) - 1)
    def _():
        if not start:
            qkv_out[...] = qkv_sum[...]
            vec_out[...] = vec_sum[...]
        else:
            index = lax.broadcasted_iota(jnp.int32, (16, 1), 0)
            heads = [total_rows(vec_sum[n]) for n in range(2)]
            for j, out in enumerate((mine, partner)):
                for k in range(3):
                    out[k * width : (k + 1) * width] = qkv_sum[k, j * width : (j + 1) * width].astype(BF16)
                out[3 * width :] = jnp.zeros((out.shape[0] - 3 * width, out.shape[1]), BF16)
                rows_out = jnp.zeros((16, half), F32)
                for n, row in enumerate(heads):
                    row = pltpu.roll(row, half - width, 1) if j else row
                    rows_out = jnp.where(index == n, row, rows_out)
                out[3 * width : 3 * width + 16, 0:half] = rows_out.astype(BF16)


def attention_input_kernel(
    start, short_blocks, core, slen, llen, scount, lcount, hidden_low, stat, qkv, mixed, low_near,
    a2, a3, a0, a1, *rest,
):
    input_rows, input_grad = rest[-10:-8]
    wqkv, wout, bias, near_qkv, sems, low_qkv, mixed_grad, delta = rest[-8:]
    meta = (core, slen, llen, scount, lcount)

    @pl.when(pl.program_id(0) == 0)
    def _():
        width = near_qkv.shape[0] // 6
        near = [
            pltpu.make_async_copy(
                piece.at[pl.ds(k * width, width)],
                near_qkv.at[pl.ds((2 * k + j) * width, width)],
                sems.at[10 + 2 * k + j],
            )
            for k in range(3)
            for j, piece in enumerate((a0, a1))
        ]
        for copy in near:
            copy.start()
        load_attention_weights((a2, a3), wqkv, wout, bias, sems)
        for copy in near:
            copy.wait()

    low = hidden_low[...]
    mixed_grad[...] = nt(low, wout[...]).astype(BF16)
    attention_heads_backward(start, short_blocks, meta, stat, qkv, mixed, mixed_grad, low_qkv, delta)
    total = low.astype(F32) + nn(low_near[...], near_qkv[...]) + nn(low_qkv[...], wqkv[...])
    input_rows[...] = total.astype(BF16)
    input_grad[...] = total


def const_spec(shape):
    return pl.BlockSpec(
        shape, lambda *_: (0,) * len(shape), pipeline_mode=pl.Buffered(1)
    )


def any_spec():
    return pl.BlockSpec(memory_space=pl.ANY)


def own_spec(width, start=0):
    return pl.BlockSpec((ROWS, width), lambda i, *_: (i + start, 0))


def whole_call(body, name, which, operands, shapes, scratch=(), keep=False, limit=24):
    moved = sum(v.size * v.dtype.itemsize for v in list(operands) + list(shapes))
    vmem = pl.BlockSpec(memory_space=pltpu.VMEM)
    if not keep:
        operands = [pltpu.with_memory_space_constraint(v, pltpu.VMEM) for v in operands]
        shapes = [pltpu.VMEM(v.shape, v.dtype) for v in shapes]
    return pl.pallas_call(
        body,
        name=name,
        in_specs=[pl.BlockSpec(memory_space=pltpu.SMEM)] + [vmem] * len(operands),
        out_specs=[vmem] * len(shapes),
        out_shape=shapes,
        scratch_shapes=list(scratch),
        compiler_params=pltpu.CompilerParams(vmem_limit_bytes=limit * 1024 * 1024),
        cost_estimate=pl.CostEstimate(flops=0, bytes_accessed=moved, transcendentals=0),
    )(which, *operands)


def spread(body, name, grid, in_specs, out_specs, out_shape, scratch=(), prefetch=0, flops=0, moved=0, exps=0, alias=None):
    return pl.pallas_call(
        body,
        name=name,
        grid_spec=pltpu.PrefetchScalarGridSpec(
            num_scalar_prefetch=prefetch,
            grid=grid,
            in_specs=in_specs,
            out_specs=out_specs,
            scratch_shapes=list(scratch),
        ),
        out_shape=out_shape,
        input_output_aliases=alias or {},
        compiler_params=pltpu.CompilerParams(
            dimension_semantics=("arbitrary",), vmem_limit_bytes=VMEM_LIMIT
        ),
        cost_estimate=pl.CostEstimate(flops=flops, bytes_accessed=moved, transcendentals=exps),
    )


def per_device(
    tokens,
    cotangent,
    short_len,
    long_len,
    short_count,
    long_count,
    query_weight,
    query_bias,
    key_weight,
    value_weight,
    value_bias,
    output_weight,
    output_bias,
    first_gain,
    first_shift,
    up_weight,
    up_bias,
    down_weight,
    down_bias,
    second_gain,
    second_shift,
):
    d = tokens.shape[1]
    width = query_weight.shape[1]
    units = up_weight.shape[1]
    half = 2 * width
    piece_rows = 4 * width + 16
    short_blocks = short_len.shape[0] * SHORT_LEN // (2 * ROWS)
    long_blocks = long_len.shape[0] * LONG_LEN // (2 * ROWS)
    blocks = short_blocks + long_blocks
    rows = blocks * ROWS
    core = lax.axis_index("tensor") % 2
    side = lax.axis_index("dp") % 2
    core_id = core.astype(jnp.int32).reshape(1)
    meta = (core_id, short_len, long_len, short_count, long_count)
    sds = jax.ShapeDtypeStruct

    def swap(values, bit, axis="tensor"):
        size = lax.axis_size(axis)
        return lax.ppermute(values, axis, [(i, i ^ bit) for i in range(size)])

    def after(value, *others):
        return lax.optimization_barrier((value,) + others)[0]

    def global_spec(start=0, flip=0):
        def index(i, core, *_):
            i = i + start
            first = core[0] if flip == 0 else 1 - core[0]
            return (2 * i + jnp.where(i < short_blocks, first, 1 - first), 0)

        return pl.BlockSpec((ROWS, d), index)

    vec_spec = const_spec((8, d))
    row_spec = own_spec(d)

    side_id = side.astype(jnp.int32).reshape(1)
    line_id = (lax.axis_index("dp") // 2).astype(jnp.int32).reshape(1)
    vectors = [query_bias, value_bias, up_bias, output_bias, first_gain, first_shift,
               down_bias, second_gain, second_shift]
    a0, vec = whole_call(
        pack_kernel, "pack", side_id,
        [query_weight.T, key_weight.T, value_weight.T, output_weight, *vectors],
        [sds((piece_rows, d), BF16), sds((8, d), F32)], [pltpu.VMEM((8, d), F32)], True, 61,
    )
    up_split = lax.dynamic_slice_in_dim(up_weight, side * (units // 2), units // 2, 1)
    def boundary(lead, *values):
        out = lax.optimization_barrier((lead,) + values)
        return out[0], list(out[1:])

    a1 = after(swap(a0, 1), up_split)
    a2 = swap(a0, 2)

    weight_scratch = [
        pltpu.VMEM((3 * half, d), BF16),
        pltpu.VMEM((half, d), BF16),
        pltpu.VMEM((32, d), BF16),
    ]
    sems = pltpu.SemaphoreType.DMA((16,))
    stat_scratch = pltpu.VMEM((ROWS, 128), F32)

    def log_spec(start=0):
        return pl.BlockSpec((8, ROWS), lambda i, *_: (i + start, 0))

    head_shapes = [sds((rows, 3 * half), BF16), sds((rows, half), BF16), sds((8 * blocks, ROWS), F32)]
    head_flops = 2 * rows * d * 3 * half + 4 * rows * 320 * half
    qkv_near, mixed_near, stat_near = spread(
        functools.partial(attention_forward_kernel, 0, blocks, short_blocks), "attention_near", (blocks,),
        [global_spec()] + [any_spec()] * 2, [own_spec(3 * half), own_spec(half), log_spec()], head_shapes,
        weight_scratch + [sems, stat_scratch, pltpu.VMEM((3, 1, half), F32)], 5,
        head_flops, rows * d * 8, rows * 320 * 6,
    )(*meta, tokens, a0, a1)

    stat_near, (a2,) = boundary(stat_near, a2)
    u2 = swap(after(up_split, a2), 2)
    d2 = swap(after(down_weight, a2), 2)
    a3 = swap(a2, 1)
    u1 = swap(after(up_weight, a3), 1)

    def far_forward(start, count, extra, alias):
        return spread(
            functools.partial(attention_finish_kernel, start, count, short_blocks), "attention_far", (count,),
            [global_spec(start)] + [any_spec()] * 2 + [own_spec(half, start)] + [any_spec()] * 2 + [vec_spec]
            + [any_spec()] * len(extra),
            [own_spec(3 * half, start), own_spec(half, start), log_spec(start), own_spec(d, start), own_spec(128, start)],
            head_shapes + [sds((rows, d), BF16), sds((rows, 128), F32)],
            weight_scratch + [pltpu.VMEM((half, d), BF16), sems, stat_scratch, pltpu.VMEM((3, 1, half), F32)], 5,
            (head_flops + 2 * rows * d * d) * count // blocks, count * ROWS * d * 10, count * ROWS * 320 * 6, alias,
        )(*meta, tokens, a2, a3, mixed_near, a0, a1, vec, *extra)

    far = list(far_forward(0, short_blocks, [], None))
    far[3], (u2, u1, down_near) = boundary(far[3], u2, u1, down_weight)
    u4 = swap(u2, 1, "dp")
    u3, d1 = swap(u2, 1), swap(down_near, 1)
    qkv_far, mixed_far, stat_far, normed, scale_one = far_forward(
        short_blocks, long_blocks, far, {12 + n: n for n in range(5)}
    )
    normed, (u4, u3, d2, d1) = boundary(normed, u4, u3, d2, d1)
    u5, d3 = swap(u4, 1), swap(d2, 1)
    ups = (up_weight, u1, u2, u3, u4, u5)
    downs = (down_weight, d1, d2, d3)
    bias_spec = pl.BlockSpec((16, d), lambda *_: (4 * width // 16, 0), pipeline_mode=pl.Buffered(1))
    up_specs = [any_spec()] * len(ups)
    down_specs = [any_spec()] * len(downs)
    ffn_scratch = [
        pltpu.VMEM((4, d, units), BF16),
        pltpu.VMEM((4, units, d), BF16),
    ]
    ffn_sems = pltpu.SemaphoreType.DMA((16,))
    whole_out, out_rows, grad_low, slope, down_mine, down_partner, sums_two = spread(
        functools.partial(ffn_forward_kernel, short_blocks), "ffn_forward", (blocks,),
        [row_spec, global_spec()] + up_specs + down_specs + [bias_spec] * 4 + [vec_spec],
        [global_spec(), row_spec, row_spec, own_spec(4 * units)] + [const_spec((units, d))] * 2 + [vec_spec],
        [sds((2 * rows, d), BF16), sds((rows, d), BF16), sds((rows, d), BF16), sds((rows, 4 * units), BF16)]
        + [sds((units, d), BF16)] * 2 + [sds((8, d), F32)],
        [pltpu.VMEM((4, ROWS, units), BF16), pltpu.VMEM((2, units, d), F32), pltpu.VMEM((3, 8, d), F32)]
        + ffn_scratch + [pltpu.VMEM((4, 1, units), F32), pltpu.VMEM((ROWS, d), F32), ffn_sems],
        6, 2 * rows * d * 10 * units, rows * d * 20, rows * 8 * units,
    )(*meta, side_id, normed, cotangent, *ups, *downs, a0, a1, a2, a3, vec)

    custom = lax.axis_size("dp") == 8

    line_steps = (
        [(0, 1), (3, 2)],
        [(1, 2), (2, 1)],
        [(1, 0), (2, 3)],
    )

    def along_line(values, stage):
        pairs = [(2 * i + n, 2 * j + n) for i, j in line_steps[stage] for n in range(2)]
        return lax.ppermute(values, "dp", pairs)

    class Reduction:
        def __init__(self, mine, partner, central):
            self.mine, self.size, self.central = mine, mine.shape[0], central
            self.moved = [swap(partner, 1)]
            self.stage = 0

        def part(self, count):
            return sds((self.size // count, d), BF16)

        def step(self):
            got = self.moved
            stage, self.stage = self.stage, self.stage + 1
            if not custom:
                if stage == 0:
                    total = (self.mine.astype(F32) + got[0].astype(F32)).astype(BF16)
                    self.moved = [lax.psum(total, "dp")]
                return self.moved[0]
            if stage == 0:
                self.keep, send = whole_call(
                    route_halves_kernel, "halves", side_id, [self.mine, got[0]], [self.part(2)] * 2
                )
                sent, self.moved = [send], [swap(send, 1, "dp")]
            elif self.central and stage < 4:
                (self.keep,) = whole_call(add_kernel, "add", line_id, [self.keep, got[0]], [self.part(2)])
                sent, self.moved = [self.keep], [along_line(self.keep, stage - 1)]
            elif self.central and stage == 4:
                (self.keep,) = whole_call(choose_kernel, "choose", line_id, [self.keep, got[0]], [self.part(2)])
                sent, self.moved = [self.keep], [swap(self.keep, 1, "dp")]
            elif stage == 1:
                self.keep, *sent = whole_call(
                    route_quarters_kernel, "quarters", line_id, [self.keep, got[0]], [self.part(8)] * 4
                )
                self.moved = [swap(v, 2 * (k + 1), "dp") for k, v in enumerate(sent)]
            elif stage == 2:
                (self.keep,) = whole_call(add_kernel, "add", line_id, [self.keep, *got], [self.part(8)])
                sent = [self.keep]
                self.moved = [swap(self.keep, 2 * k, "dp") for k in (1, 2, 3)]
            elif stage == 3:
                (self.keep,) = whole_call(
                    join_kernel, "join_quarters", line_id, [self.keep, *got], [self.part(2)]
                )
                sent, self.moved = [self.keep], [swap(self.keep, 1, "dp")]
            return sent[0]

        def finish(self, *sizes):
            shapes = [sds((n, d), F32) for n in sizes]
            if not custom:
                total = self.moved[0].astype(F32)
                cuts = [sum(sizes[:n]) for n in range(len(sizes))]
                return [total[at : at + n] for at, n in zip(cuts, sizes)]
            operands = [self.keep, self.moved[0]]
            return whole_call(
                finish_kernel, "finish", side_id, operands, shapes, [pltpu.VMEM((self.size, d), F32)], True
            )

    def settle(lead, reductions, *extra):
        lead, values = boundary(lead, *[v for r in reductions for v in r.moved], *extra)
        for r in reductions:
            count = len(r.moved)
            r.moved, values = values[:count], values[count:]
        return (lead, *values)

    grad_low, down_mine, down_partner = lax.optimization_barrier((grad_low, down_mine, down_partner))
    down_reduce = Reduction(down_mine, down_partner, True)
    tie = down_reduce.step()
    grad_low = after(grad_low, tie)
    moved_out = swap(after(out_rows, tie), 1)

    pack_rows = units + width + 64
    hidden_low, mine, partner = spread(
        ffn_backward_kernel, "ffn_backward", (blocks,),
        [row_spec, own_spec(4 * units), row_spec, own_spec(128), own_spec(half), vec_spec]
        + up_specs + down_specs + [vec_spec],
        [row_spec] + [const_spec((pack_rows, d))] * 2,
        [sds((rows, d), BF16)] + [sds((pack_rows, d), BF16)] * 2,
        [pltpu.VMEM((2, d, units), F32), pltpu.VMEM((half, d), F32), pltpu.VMEM((7, 8, d), F32),
         pltpu.VMEM((4, ROWS, units), BF16)] + ffn_scratch + [pltpu.VMEM((ROWS, d), F32), ffn_sems],
        1, 2 * rows * d * 10 * units, rows * d * 16, 0,
    )(side_id, grad_low, slope, normed, scale_one, mixed_near, sums_two, *ups, *downs, vec)
    hidden_low, mine, partner, moved_out = settle(hidden_low, [down_reduce], mine, partner, moved_out)
    tie = down_reduce.step()
    partner = after(partner, tie)
    up_reduce = Reduction(mine, partner, True)
    tie = up_reduce.step()
    hidden_low = after(hidden_low, tie)

    qkv_rows = 3 * width + 64
    sums = [sds((3, half, d), F32), sds((2, 8, half), F32)]
    sum_specs = [const_spec(v.shape) for v in sums]

    def near_backward(start, count, extra, extra_specs, outs, out_specs, alias):
        return spread(
            functools.partial(attention_backward_kernel, start, short_blocks), "attention_near_backward", (count,),
            [own_spec(d, start), log_spec(start), own_spec(3 * half, start), own_spec(half, start), global_spec(start)]
            + [any_spec()] * 2 + extra_specs,
            [own_spec(3 * half)] + out_specs,
            [sds((count * ROWS, 3 * half), BF16)] + outs,
            weight_scratch + [sems, pltpu.VMEM((ROWS, half), BF16), pltpu.VMEM((8, ROWS), F32),
                              pltpu.VMEM((3, half, d), F32), pltpu.VMEM((2, 8, half), F32)],
            5, count * ROWS * (10 * d * half + 3200 * half), count * ROWS * d * 16, count * ROWS * 320 * 6,
        )(*meta, hidden_low, stat_near, qkv_near, mixed_near, tokens, a0, a1, *extra)

    low_short, *sums_short = near_backward(0, short_blocks, [], [], sums, sum_specs, None)
    (low_short,) = settle(low_short, [down_reduce, up_reduce])
    tie = down_reduce.step()
    tie_two = up_reduce.step()
    sums_short[1] = after(sums_short[1], tie, tie_two)
    low_long, mine, partner = near_backward(
        short_blocks, long_blocks, sums_short, sum_specs,
        [sds((qkv_rows, d), BF16)] * 2, [const_spec((qkv_rows, d))] * 2, None,
    )
    low_long, mine, partner = settle(low_long, [down_reduce, up_reduce], mine, partner)
    ties = [down_reduce.step(), up_reduce.step()]
    qkv_reduce = Reduction(mine, after(partner, *ties), False)
    ties += [qkv_reduce.step()]

    def far_backward(start, count, low_near, extra, alias):
        return spread(
            functools.partial(attention_input_kernel, start, short_blocks), "attention_far_backward", (count,),
            [own_spec(d, start), log_spec(start), own_spec(3 * half, start), own_spec(half, start), own_spec(3 * half)]
            + [any_spec()] * (4 + len(extra)),
            [own_spec(d, start), global_spec(start)], [sds((rows, d), BF16), sds((2 * rows, d), F32)],
            weight_scratch + [pltpu.VMEM((3 * half, d), BF16), sems, pltpu.VMEM((ROWS, 3 * half), BF16),
                              pltpu.VMEM((ROWS, half), BF16), pltpu.VMEM((8, ROWS), F32)],
            5, count * ROWS * (14 * d * half + 3200 * half), count * ROWS * d * 16, count * ROWS * 320 * 6, alias,
        )(*meta, hidden_low, stat_far, qkv_far, mixed_far, low_near, a2, a3, a0, a1, *extra)

    low_short = after(low_short, *ties)
    rows_short, whole_in = far_backward(0, short_blocks, low_short, [], None)
    (rows_short,) = settle(rows_short, [down_reduce, up_reduce, qkv_reduce])
    ties = [qkv_reduce.step(), up_reduce.step(), down_reduce.step()]
    low_long = after(low_long, *ties)
    rows_all, whole_in = far_backward(
        short_blocks, long_blocks, low_long, [rows_short, whole_in], {14: 0, 15: 1}
    )
    (rows_all,) = settle(rows_all, [down_reduce, up_reduce, qkv_reduce])
    tie = qkv_reduce.step()
    tie = after(tie, up_reduce.step())
    down_reduce.moved[0] = after(down_reduce.moved[0], tie)
    (grad_down,) = down_reduce.finish(units)
    moved_rows = swap(after(rows_all, tie), 1)

    def place(whole, other, start, count):
        return spread(
            place_kernel, "place", (count,), [own_spec(d), any_spec()], global_spec(start, 1),
            sds(whole.shape, whole.dtype), (), 1, 0, other.size * 6, 0, {2: 0},
        )(core_id, other, whole)

    layer_output = place(whole_out, after(moved_out, tie), 0, blocks)
    layer_output, moved_rows = settle(layer_output, [qkv_reduce], moved_rows)
    tie = qkv_reduce.step()
    input_grad = place(whole_in, after(moved_rows, tie), 0, blocks)
    up_reduce.moved[0] = after(up_reduce.moved[0], tie)
    grad_up, grad_out, small = up_reduce.finish(units, width, 16)
    grad_up, input_grad = settle(grad_up, [qkv_reduce], input_grad)
    grad_query, grad_key, grad_value, heads = qkv_reduce.finish(width, width, width, 16)
    return (
        layer_output,
        input_grad,
        grad_query.T,
        heads[0, :width],
        grad_key.T,
        grad_value.T,
        heads[1, :width],
        grad_out,
        small[5],
        small[3],
        small[4],
        grad_up,
        small[6],
        grad_down,
        small[2],
        small[0],
        small[1],
    )

def solution(mesh):
    return jax.shard_map(
        per_device,
        mesh=mesh,
        in_specs=(
            P("dp", None),
            P("dp", None),
            P("dp"),
            P("dp"),
            P("dp"),
            P("dp"),
            P(None, "tensor"),
            P("tensor"),
            P(None, "tensor"),
            P(None, "tensor"),
            P("tensor"),
            P("tensor", None),
            P(),
            P(),
            P(),
            P(None, "tensor"),
            P("tensor"),
            P("tensor", None),
            P(),
            P(),
            P(),
        ),
        out_specs=(
            P("dp", None),
            P("dp", None),
            P(None, "tensor"),
            P("tensor"),
            P(None, "tensor"),
            P(None, "tensor"),
            P("tensor"),
            P("tensor", None),
            P(),
            P(),
            P(),
            P(None, "tensor"),
            P("tensor"),
            P("tensor", None),
            P(),
            P(),
            P(),
        ),
        check_vma=False,
    )
```

```python
import functools

import jax
import jax.numpy as jnp
from jax import lax
from jax.experimental import pallas as pl
from jax.experimental.pallas import tpu as pltpu
from jax.sharding import PartitionSpec as P

HEAD_DIM = 64
SHORT_LEN = 128
LONG_LEN = 512
ROWS = 512
SLOTS = ROWS // SHORT_LEN
PAIR = 2 * HEAD_DIM
MASKED = -30000.0
F32 = jnp.float32
BF16 = jnp.bfloat16
VMEM_LIMIT = 60 * 1024 * 1024


def nn(left, right):
    return lax.dot_general(left, right, (((1,), (0,)), ((), ())), preferred_element_type=F32)


def nt(left, right):
    return lax.dot_general(left, right, (((1,), (1,)), ((), ())), preferred_element_type=F32)


def tn(left, right):
    return lax.dot_general(left, right, (((0,), (0,)), ((), ())), preferred_element_type=F32)


def fold_rows(values):
    return jnp.sum(values.reshape(-1, 8, values.shape[-1]), axis=0)


def total_rows(values):
    return jnp.sum(values, axis=0, keepdims=True)


def by_rows(size, body):
    def step(n, carry):
        body(pl.ds(pl.multiple_of(n * 64, 64), 64))
        return carry

    lax.fori_loop(0, size // 64, step, 0)


def clear(ref):
    def body(span):
        for j in range(ref.shape[0]):
            ref[j, span] = jnp.zeros((64, ref.shape[2]), ref.dtype)

    by_rows(ref.shape[1], body)


def copy_rows(source, target, at=0):
    def body(span):
        target[pl.ds(pl.multiple_of(at + span.start, 16), 64)] = source[span].astype(target.dtype)

    if source.shape[0] % 64:
        target[pl.ds(at, source.shape[0])] = source[...].astype(target.dtype)
    else:
        by_rows(source.shape[0], body)


def half_mask(which):
    lanes = lax.broadcasted_iota(jnp.int32, (1, PAIR), 1)
    return (lanes >= HEAD_DIM) if which else (lanes < HEAD_DIM)


def short_valid(meta, block, slot):
    index = SLOTS * (2 * block + meta[0][0]) + slot
    return jnp.where(index < meta[3][0], meta[1][index], 0)


def long_valid(meta, block, short_blocks):
    index = 2 * (block - short_blocks) + 1 - meta[0][0]
    return jnp.where(index < meta[4][0], meta[2][index], 0)


def norm_rows(values):
    centre = values - jnp.mean(values, axis=-1, keepdims=True)
    scale = lax.rsqrt(jnp.mean(centre * centre, axis=-1, keepdims=True) + 1e-12)
    return centre * scale, scale


def norm_back(incoming, normed, scale, gain):
    grad = incoming * gain
    inner = grad - jnp.mean(grad, axis=-1, keepdims=True)
    inner = inner - normed * jnp.mean(grad * normed, axis=-1, keepdims=True)
    return scale * inner


def attention_copies(pieces, sems, wqkv=None, wout=None, bias=None):
    copies = []
    for j, piece in enumerate(pieces):
        width = (piece.shape[0] - 16) // 4
        pairs = []
        if wqkv is not None:
            for k in range(3):
                rows = pl.ds((2 * k + j) * width, width)
                pairs.append((k, piece.at[pl.ds(k * width, width)], wqkv.at[rows]))
        if wout is not None:
            pairs.append((3, piece.at[pl.ds(3 * width, width)], wout.at[pl.ds(j * width, width)]))
        if bias is not None:
            pairs.append((4, piece.at[pl.ds(4 * width, 16)], bias.at[pl.ds(16 * j, 16)]))
        copies += [pltpu.make_async_copy(s, d, sems.at[5 * j + n]) for n, s, d in pairs]
    return copies


def start_all(copies):
    for copy in copies:
        copy.start()


def wait_all(copies):
    for copy in copies:
        copy.wait()


def flat_row(ref):
    return ref[...].astype(F32).reshape(1, ref.shape[0])


def pack_kernel(at, wq, wk, wv, wo, qb, vb, ub, ob, g1, s1, db, g2, s2, piece, vec, wide):
    width = wq.shape[0]
    d = piece.shape[1]
    piece[0:width] = wq[...]
    piece[width : 2 * width] = wk[...]
    piece[2 * width : 3 * width] = wv[...]
    piece[3 * width : 4 * width] = wo[...]
    index = lax.broadcasted_iota(jnp.int32, (16, 1), 0)
    wide[...] = jnp.zeros_like(wide)
    wide[0:1, 0:width] = flat_row(qb)
    wide[1:2, 0:width] = flat_row(vb)
    row_q, row_v, row_u = wide[0:1], wide[1:2], flat_row(ub)
    lead = jnp.where(lax.broadcasted_iota(jnp.int32, (1, d), 1) < d // 2, row_u, 0.0)
    trail = pltpu.roll(row_u - lead, d // 2, 1)
    mine = jnp.where(at[0] == 0, lead, trail)
    far = jnp.where(at[0] == 0, trail, lead)
    rows = [row_u, row_q, pltpu.roll(row_q, width, 1), row_v, pltpu.roll(row_v, width, 1)]
    block = jnp.zeros((16, d), F32)
    for n, row in enumerate(rows + [None] * 4 + [mine, far]):
        if row is not None:
            block = jnp.where(index == n, row, block)
    piece[4 * width : 4 * width + 16] = block.astype(BF16)
    for n, row in enumerate((ob, g1, s1, db, g2, s2)):
        vec[n : n + 1] = flat_row(row)
    vec[6:8] = jnp.zeros((2, d), F32)


def place_kernel(core, other, whole, out):
    out[...] = other[...].astype(out.dtype)


def route_halves_kernel(at, mine, partner, keep, send):
    half = keep.shape[0]
    for out, which in ((keep, at[0]), (send, 1 - at[0])):
        base = which * half

        def body(span):
            rows = pl.ds(pl.multiple_of(base + span.start, 16), 64)
            out[span] = (mine[rows].astype(F32) + partner[rows].astype(F32)).astype(BF16)

        by_rows(half, body)


def route_quarters_kernel(at, keep, other, *outs):
    size = outs[0].shape[0]
    for k, out in enumerate(outs):
        span = pl.ds(pl.multiple_of((at[0] ^ k) * size, 16), size)
        out[...] = (keep[span].astype(F32) + other[span].astype(F32)).astype(BF16)


def add_kernel(at, *refs):
    def body(span):
        refs[-1][span] = sum(ref[span].astype(F32) for ref in refs[:-1]).astype(BF16)

    size = refs[-1].shape[0]
    if size % 64:
        body(pl.ds(0, size))
    else:
        by_rows(size, body)


def choose_kernel(at, own, other, out):
    central = jnp.logical_or(at[0] == 1, at[0] == 2)

    @pl.when(central)
    def _():
        out[...] = own[...]

    @pl.when(jnp.logical_not(central))
    def _():
        out[...] = other[...]


def join_kernel(at, *refs):
    out = refs[-1]
    size = refs[0].shape[0]
    for k, ref in enumerate(refs[:-1]):
        copy_rows(ref, out, pl.multiple_of((at[0] ^ k) * size, 16))


def finish_kernel(at, own, other, *refs):
    outs, whole = refs[:-1], refs[-1]
    join_kernel(at, own, other, whole)
    start = 0
    for out in outs:
        copy_rows(whole.at[pl.ds(start, out.shape[0])], out)
        start += out.shape[0]


def stacked(values):
    zero = jnp.zeros_like(values)
    return jnp.concatenate([jnp.where(half_mask(e), values, zero) for e in range(2)], axis=0)


def unstacked(values):
    size = values.shape[0] // 2
    return jnp.where(half_mask(0), values[:size], values[size:])


def attention_heads_forward(start, count, short_blocks, meta, x, weights, qkv, mixed, logs, stat):
    wqkv, bias, head_bias = weights
    block = pl.program_id(0) + start
    half = mixed.shape[1]

    @pl.when(pl.program_id(0) == 0)
    def _():
        small = bias[...].astype(F32)
        head_bias[0] = (small[1:2] + small[18:19])[:, 0:half]
        head_bias[1] = jnp.zeros((1, half), F32)
        head_bias[2] = (small[3:4] + small[20:21])[:, 0:half]

    def project(k, carry):
        span = pl.ds(pl.multiple_of(k * half, half), half)
        qkv[:, span] = (nt(x[...], wqkv[span]) + head_bias[k]).astype(BF16)
        return carry

    lax.fori_loop(0, 3, project, 0)
    stat[...] = jnp.zeros_like(stat)
    lanes = lax.broadcasted_iota(jnp.int32, (1, 128), 1)

    def tiles(pair, spans):
        column = pl.multiple_of(pair * PAIR, PAIR)
        q, scores = [], []
        for query_at, queries, key_at, keys, valid in spans:
            part = qkv[query_at : query_at + queries, pl.ds(column, PAIR)] * jnp.asarray(0.125, BF16)
            key_part = qkv[key_at : key_at + keys, pl.ds(half + column, PAIR)]
            scores.append(nt(stacked(part), key_part))
        live = [lax.broadcasted_iota(jnp.int32, (1, t[3]), 1) < t[4] for t in spans]
        scores = [jnp.where(a, v, MASKED) for a, v in zip(live, scores)]
        top = [jnp.max(v, axis=-1, keepdims=True) for v in scores]
        weights = [jnp.exp(v - m) for v, m in zip(scores, top)]
        total = [jnp.sum(v, axis=-1, keepdims=True) for v in weights]
        out = [
            nn(v.astype(BF16), qkv[t[2] : t[2] + t[3], pl.ds(2 * half + column, PAIR)])
            for v, t in zip(weights, spans)
        ]
        for (query_at, queries, *_), m, n, v in zip(spans, top, total, out):
            log = m + jnp.log(n)
            rows = stat[query_at : query_at + queries]
            rows = jnp.where(lanes == 2 * pair, log[:queries], rows)
            stat[query_at : query_at + queries] = jnp.where(lanes == 2 * pair + 1, log[queries:], rows)
            mixed[query_at : query_at + queries, pl.ds(column, PAIR)] = unstacked(v * (1.0 / n)).astype(BF16)

    def short_path():
        spans = [
            (slot * SHORT_LEN, SHORT_LEN, slot * SHORT_LEN, SHORT_LEN, short_valid(meta, block, slot))
            for slot in range(SLOTS)
        ]

        def body(pair, carry):
            tiles(pair, spans)
            return carry

        lax.fori_loop(0, half // PAIR, body, 0)

    def long_path():
        valid = long_valid(meta, block, short_blocks)
        spans = [(part * 256, 256, 0, LONG_LEN, valid) for part in range(2)]

        def body(pair, carry):
            tiles(pair, spans)
            return carry

        lax.fori_loop(0, half // PAIR, body, 0)

    if start < short_blocks:
        pl.when(block < short_blocks)(short_path)
    if start + count > short_blocks:
        pl.when(block >= short_blocks)(long_path)
    logs[...] = stat[...].T[0:8]


def attention_forward_kernel(
    start, count, short_blocks, core, slen, llen, scount, lcount, x, a0, a1, qkv, mixed, logs,
    wqkv, wout, bias, sems, stat, head_bias,
):
    copies = attention_copies((a0, a1), sems, wqkv=wqkv, bias=bias)

    @pl.when(pl.program_id(0) == 0)
    def _():
        start_all(copies)
        wait_all(copies)

    meta = (core, slen, llen, scount, lcount)
    attention_heads_forward(start, count, short_blocks, meta, x, (wqkv, bias, head_bias), qkv, mixed, logs, stat)


def attention_finish_kernel(
    start, count, short_blocks, core, slen, llen, scount, lcount, x, a2, a3, mixed_near, a0, a1, vec, *rest,
):
    qkv, mixed, logs, normed, scale_rows, wqkv, wout, bias, near_out, sems, stat, head_bias = rest[-12:]

    width = near_out.shape[0] // 2
    needed = attention_copies((a2, a3), sems, wqkv=wqkv, bias=bias)
    later = attention_copies((a2, a3), sems, wout=wout) + [
        pltpu.make_async_copy(
            piece.at[pl.ds(3 * width, width)], near_out.at[pl.ds(j * width, width)], sems.at[10 + j]
        )
        for j, piece in enumerate((a0, a1))
    ]

    @pl.when(pl.program_id(0) == 0)
    def _():
        start_all(needed + later)
        wait_all(needed)

    meta = (core, slen, llen, scount, lcount)
    attention_heads_forward(start, count, short_blocks, meta, x, (wqkv, bias, head_bias), qkv, mixed, logs, stat)

    @pl.when(pl.program_id(0) == 0)
    def _():
        wait_all(later)

    hidden = x[...].astype(F32) + vec[0:1]
    hidden = hidden + nn(mixed_near[...], near_out[...]) + nn(mixed[...], wout[...])
    rows, scale = norm_rows(hidden)
    normed[...] = rows.astype(BF16)
    scale_rows[...] = jnp.broadcast_to(scale, scale_rows.shape)


def weight_copies(side, ups, downs, up_all, down_all, sems):
    half = ups[2].shape[1]
    spans = [pl.ds(pl.multiple_of(at * half, 16), half) for at in (side[0], 1 - side[0])]
    copies = []
    for j in range(2):
        copies.append([(ups[j], up_all.at[j]), (downs[j], down_all.at[j])])
    for j in range(2):
        pairs = []
        for n in range(2):
            part = pl.ds(n * half, half)
            pairs.append((ups[2 + 2 * n + j], up_all.at[2 + j, :, part]))
            pairs.append((downs[2 + j].at[spans[n]], down_all.at[2 + j, part]))
        copies.append(pairs)
    return [
        [pltpu.make_async_copy(s, d, sems.at[4 * j + n]) for n, (s, d) in enumerate(pairs)]
        for j, pairs in enumerate(copies)
    ]


def start_weights(copies):
    for pairs in copies:
        for copy in pairs:
            copy.start()


def wait_weights(copies, step):
    for at in range(2):

        @pl.when(jnp.logical_and(pl.program_id(0) == 0, step == at))
        def _():
            for pairs in copies[2 * at : 2 * at + 2]:
                for copy in pairs:
                    copy.wait()


def ffn_forward_kernel(short_blocks, core, slen, llen, scount, lcount, side, normed, cotangent, *rest):
    ups, downs, biases = rest[0:6], rest[6:10], rest[10:14]
    vec, layer_out, layer_rows, grad_low, slope, down_mine, down_partner, sums = rest[14:22]
    active, down_sum, vec_sum, up_all, down_all, bias_all, total, sems = rest[22:]
    meta = (core, slen, llen, scount, lcount)
    block = pl.program_id(0)
    units = up_all.shape[2]
    half = units // 2
    copies = weight_copies(side, ups, downs, up_all, down_all, sems)

    @pl.when(block == 0)
    def _():
        start_weights(copies)
        clear(down_sum)
        vec_sum[...] = jnp.zeros_like(vec_sum)
        for j in range(2):
            bias_all[j] = biases[j][0:1].astype(F32)
            for n in range(2):
                bias_all[2 + j, :, n * half : (n + 1) * half] = biases[2 + j][9 + n : 10 + n, 0:half].astype(F32)

    first = normed[...].astype(F32) * vec[1:2] + vec[2:3]
    first_low = first.astype(BF16)
    total[...] = first + vec[3:4]

    def groups(step, carry):
        wait_weights(copies, step)
        for e in range(2):
            j = 2 * step + e
            inner = nn(first_low, up_all[j]) + bias_all[j]
            chance = 0.5 * (1.0 + lax.erf(inner * 0.7071067811865476))
            low_units = (inner * chance).astype(BF16)
            slope[:, pl.ds(pl.multiple_of(j * units, units), units)] = (
                chance + inner * jnp.exp(-0.5 * inner * inner) * 0.3989422804014327
            ).astype(BF16)
            active[j] = low_units
            total[...] += nn(low_units, down_all[j])
        return carry

    lax.fori_loop(0, 2, groups, 0)
    rows, scale = norm_rows(total[...])
    result = (rows * vec[4:5] + vec[5:6]).astype(BF16)
    layer_out[...] = result
    layer_rows[...] = result
    position = lax.broadcasted_iota(jnp.int32, (ROWS, 1), 0)
    slot = position // SHORT_LEN
    short_limit = jnp.zeros((ROWS, 1), jnp.int32)
    for n in range(SLOTS):
        short_limit = jnp.where(slot == n, short_valid(meta, jnp.minimum(block, short_blocks - 1), n), short_limit)
    long_limit = long_valid(meta, jnp.maximum(block, short_blocks), short_blocks)
    is_short = block < short_blocks
    alive = jnp.where(is_short, position % SHORT_LEN, position) < jnp.where(
        is_short, short_limit, long_limit
    )
    upstream = jnp.where(alive, cotangent[...].astype(F32), 0.0)
    grad = norm_back(upstream, rows, scale, vec[4:5])
    low = grad.astype(BF16)
    grad_low[...] = low
    vec_sum[0] += fold_rows(upstream * rows)
    vec_sum[1] += fold_rows(upstream)
    vec_sum[2] += fold_rows(grad)
    for j in range(2):
        down_sum[j] += tn(active[j], low)

    @pl.when(block == pl.num_programs(0) - 1)
    def _():
        copy_rows(down_sum.at[0], down_mine)
        copy_rows(down_sum.at[1], down_partner)
        sums[...] = jnp.zeros_like(sums)
        for n in range(3):
            sums[n : n + 1] = total_rows(vec_sum[n])


def ffn_backward_kernel(side, grad_low, slope, normed, stat, mixed, sums_two, *rest):
    ups, downs = rest[0:6], rest[6:10]
    vec, hidden_low, mine, partner = rest[10:14]
    up_sum, out_sum, vec_sum, kept, up_all, down_all, total, sems = rest[14:]
    block = pl.program_id(0)
    units = up_sum.shape[2]
    width = mixed.shape[1] // 2
    copies = weight_copies(side, ups, downs, up_all, down_all, sems)

    @pl.when(block == 0)
    def _():
        start_weights(copies)
        clear(up_sum)
        out_sum[...] = jnp.zeros_like(out_sum)
        vec_sum[...] = jnp.zeros_like(vec_sum)

    low = grad_low[...]
    total[...] = low.astype(F32)

    def groups(step, carry):
        wait_weights(copies, step)
        for e in range(2):
            j = 2 * step + e
            inner = nt(low, down_all[j]) * slope[:, pl.ds(pl.multiple_of(j * units, units), units)].astype(F32)
            inner_low = inner.astype(BF16)
            total[...] += nt(inner_low, up_all[j])
            vec_sum[j] += fold_rows(inner)
            kept[j] = inner_low
        return carry

    lax.fori_loop(0, 2, groups, 0)
    rows = normed[...].astype(F32)
    first_low = (rows * vec[1:2] + vec[2:3]).astype(BF16)
    for j in range(2):
        up_sum[j] += tn(first_low, kept[j])
    incoming = total[...]
    grad = norm_back(incoming, rows, stat[:, 0:1], vec[1:2])
    vec_sum[4] += fold_rows(incoming * rows)
    vec_sum[5] += fold_rows(incoming)
    vec_sum[6] += fold_rows(grad)
    grad_attn = grad.astype(BF16)
    hidden_low[...] = grad_attn
    out_sum[...] += tn(mixed[...], grad_attn)

    @pl.when(block == pl.num_programs(0) - 1)
    def _():
        index = lax.broadcasted_iota(jnp.int32, (16, 1), 0)
        shared = [sums_two[n : n + 1] for n in range(3)] + [total_rows(vec_sum[n]) for n in range(4, 7)]
        for j, out in enumerate((mine, partner)):
            copy_rows(up_sum.at[j], out)
            copy_rows(out_sum.at[pl.ds(j * width, width)], out, units)
            out[units + width :] = jnp.zeros((out.shape[0] - units - width, out.shape[1]), BF16)
            rows_out = jnp.zeros((16, out.shape[1]), F32)
            for n, row in enumerate(shared + [total_rows(vec_sum[j])]):
                rows_out = jnp.where(index == n, row, rows_out)
            out[units + width : units + width + 16] = rows_out.astype(BF16)


def attention_heads_backward(start, short_blocks, meta, logs, qkv, mixed, mixed_grad, low_qkv, delta):
    block = pl.program_id(0) + start
    half = mixed.shape[1]
    own = (mixed_grad[...].astype(F32) * mixed[...].astype(F32)).astype(BF16)
    head = lax.broadcasted_iota(jnp.int32, (8, half), 1) // HEAD_DIM
    pick = jnp.where(head == lax.broadcasted_iota(jnp.int32, (8, half), 0), 1.0, 0.0)
    delta[...] = nt(pick.astype(BF16), own)

    index = lax.broadcasted_iota(jnp.int32, (8, 1), 0)

    def tiles(pair, size, valids):
        column = pl.multiple_of(pair * PAIR, PAIR)
        spans = [pl.ds(n * size, size) for n in range(len(valids))]

        def rows(ref, span):
            picked = [total_rows(jnp.where(index == 2 * pair + e, ref[:, span], 0.0)) for e in range(2)]
            return jnp.concatenate(picked, axis=1)

        q = [stacked(qkv[t, pl.ds(column, PAIR)] * jnp.asarray(0.125, BF16)) for t in spans]
        g = [stacked(mixed_grad[t, pl.ds(column, PAIR)]) for t in spans]
        k = [qkv[t, pl.ds(half + column, PAIR)] for t in spans]
        scores = [nt(b, a) for a, b in zip(q, k)]
        grads = [nt(qkv[t, pl.ds(2 * half + column, PAIR)], a) for t, a in zip(spans, g)]
        place = lax.broadcasted_iota(jnp.int32, (size, 1), 0)
        probs = [
            jnp.where(place < valid, jnp.exp(v - rows(logs, t)), 0.0)
            for v, t, valid in zip(scores, spans, valids)
        ]
        scores = [(p * (v - rows(delta, t))).astype(BF16) for p, v, t in zip(probs, grads, spans)]
        dq = [tn(v, b) for v, b in zip(scores, k)]
        dk = [nn(v, a) for v, a in zip(scores, q)]
        dv = [nn(p.astype(BF16), a) for p, a in zip(probs, g)]
        for t, a, b, c in zip(spans, dq, dk, dv):
            low_qkv[t, pl.ds(column, PAIR)] = (unstacked(a) * 0.125).astype(BF16)
            low_qkv[t, pl.ds(half + column, PAIR)] = b.astype(BF16)
            low_qkv[t, pl.ds(2 * half + column, PAIR)] = c.astype(BF16)

    if start < short_blocks:
        valids = [short_valid(meta, block, slot) for slot in range(SLOTS)]
        size = SHORT_LEN
    else:
        valids = [long_valid(meta, block, short_blocks)]
        size = LONG_LEN

    def body(pair, carry):
        tiles(pair, size, valids)
        return carry

    lax.fori_loop(0, half // PAIR, body, 0)


def attention_backward_kernel(
    start, short_blocks, core, slen, llen, scount, lcount, hidden_low, stat, qkv, mixed, x,
    a0, a1, *rest,
):
    if start:
        sums_in, vec_in, low_qkv, mine, partner = rest[:5]
    else:
        low_qkv, qkv_out, vec_out = rest[:3]
    wqkv, wout, bias, sems, mixed_grad, delta, qkv_sum, vec_sum = rest[-8:]
    meta = (core, slen, llen, scount, lcount)
    block = pl.program_id(0)
    half = mixed.shape[1]
    width = half // 2

    copies = attention_copies((a0, a1), sems, wout=wout)

    @pl.when(block == 0)
    def _():
        start_all(copies)
        wait_all(copies)
        if start:
            qkv_sum[...] = sums_in[...]
            vec_sum[...] = vec_in[...]
        else:
            clear(qkv_sum)
            vec_sum[...] = jnp.zeros_like(vec_sum)

    mixed_grad[...] = nt(hidden_low[...], wout[...]).astype(BF16)
    attention_heads_backward(start, short_blocks, meta, stat, qkv, mixed, mixed_grad, low_qkv, delta)
    vec_sum[0] += fold_rows(low_qkv[:, 0:half].astype(F32))
    vec_sum[1] += fold_rows(low_qkv[:, 2 * half : 3 * half].astype(F32))

    for k in range(3):
        qkv_sum[k] += tn(low_qkv[:, k * half : (k + 1) * half], x[...])

    @pl.when(block == pl.num_programs(0) - 1)
    def _():
        if not start:
            qkv_out[...] = qkv_sum[...]
            vec_out[...] = vec_sum[...]
        else:
            index = lax.broadcasted_iota(jnp.int32, (16, 1), 0)
            heads = [total_rows(vec_sum[n]) for n in range(2)]
            for j, out in enumerate((mine, partner)):
                for k in range(3):
                    out[k * width : (k + 1) * width] = qkv_sum[k, j * width : (j + 1) * width].astype(BF16)
                out[3 * width :] = jnp.zeros((out.shape[0] - 3 * width, out.shape[1]), BF16)
                rows_out = jnp.zeros((16, half), F32)
                for n, row in enumerate(heads):
                    row = pltpu.roll(row, half - width, 1) if j else row
                    rows_out = jnp.where(index == n, row, rows_out)
                out[3 * width : 3 * width + 16, 0:half] = rows_out.astype(BF16)


def attention_input_kernel(
    start, short_blocks, core, slen, llen, scount, lcount, hidden_low, stat, qkv, mixed, low_near,
    a2, a3, a0, a1, *rest,
):
    input_rows, input_grad = rest[-10:-8]
    wqkv, wout, bias, near_qkv, sems, low_qkv, mixed_grad, delta = rest[-8:]
    meta = (core, slen, llen, scount, lcount)

    width = near_qkv.shape[0] // 6
    needed = attention_copies((a2, a3), sems, wout=wout)
    later = attention_copies((a2, a3), sems, wqkv=wqkv) + [
        pltpu.make_async_copy(
            piece.at[pl.ds(k * width, width)],
            near_qkv.at[pl.ds((2 * k + j) * width, width)],
            sems.at[10 + 2 * k + j],
        )
        for k in range(3)
        for j, piece in enumerate((a0, a1))
    ]

    @pl.when(pl.program_id(0) == 0)
    def _():
        start_all(needed + later)
        wait_all(needed)

    low = hidden_low[...]
    mixed_grad[...] = nt(low, wout[...]).astype(BF16)
    attention_heads_backward(start, short_blocks, meta, stat, qkv, mixed, mixed_grad, low_qkv, delta)

    @pl.when(pl.program_id(0) == 0)
    def _():
        wait_all(later)

    total = low.astype(F32) + nn(low_near[...], near_qkv[...]) + nn(low_qkv[...], wqkv[...])
    input_rows[...] = total.astype(BF16)
    input_grad[...] = total


def const_spec(shape):
    return pl.BlockSpec(
        shape, lambda *_: (0,) * len(shape), pipeline_mode=pl.Buffered(1)
    )


def any_spec():
    return pl.BlockSpec(memory_space=pl.ANY)


def own_spec(width, start=0):
    return pl.BlockSpec((ROWS, width), lambda i, *_: (i + start, 0))


def whole_call(body, name, which, operands, shapes, scratch=(), keep=False, limit=24):
    moved = sum(v.size * v.dtype.itemsize for v in list(operands) + list(shapes))
    vmem = pl.BlockSpec(memory_space=pltpu.VMEM)
    if not keep:
        operands = [pltpu.with_memory_space_constraint(v, pltpu.VMEM) for v in operands]
        shapes = [pltpu.VMEM(v.shape, v.dtype) for v in shapes]
    return pl.pallas_call(
        body,
        name=name,
        in_specs=[pl.BlockSpec(memory_space=pltpu.SMEM)] + [vmem] * len(operands),
        out_specs=[vmem] * len(shapes),
        out_shape=shapes,
        scratch_shapes=list(scratch),
        compiler_params=pltpu.CompilerParams(vmem_limit_bytes=limit * 1024 * 1024),
        cost_estimate=pl.CostEstimate(flops=0, bytes_accessed=moved, transcendentals=0),
    )(which, *operands)


def spread(body, name, grid, in_specs, out_specs, out_shape, scratch=(), prefetch=0, flops=0, moved=0, exps=0, alias=None):
    return pl.pallas_call(
        body,
        name=name,
        grid_spec=pltpu.PrefetchScalarGridSpec(
            num_scalar_prefetch=prefetch,
            grid=grid,
            in_specs=in_specs,
            out_specs=out_specs,
            scratch_shapes=list(scratch),
        ),
        out_shape=out_shape,
        input_output_aliases=alias or {},
        compiler_params=pltpu.CompilerParams(
            dimension_semantics=("arbitrary",), vmem_limit_bytes=VMEM_LIMIT
        ),
        cost_estimate=pl.CostEstimate(flops=flops, bytes_accessed=moved, transcendentals=exps),
    )


def per_device(
    tokens,
    cotangent,
    short_len,
    long_len,
    short_count,
    long_count,
    query_weight,
    query_bias,
    key_weight,
    value_weight,
    value_bias,
    output_weight,
    output_bias,
    first_gain,
    first_shift,
    up_weight,
    up_bias,
    down_weight,
    down_bias,
    second_gain,
    second_shift,
):
    d = tokens.shape[1]
    width = query_weight.shape[1]
    units = up_weight.shape[1]
    half = 2 * width
    piece_rows = 4 * width + 16
    short_blocks = short_len.shape[0] * SHORT_LEN // (2 * ROWS)
    long_blocks = long_len.shape[0] * LONG_LEN // (2 * ROWS)
    blocks = short_blocks + long_blocks
    rows = blocks * ROWS
    core = lax.axis_index("tensor") % 2
    side = lax.axis_index("dp") % 2
    core_id = core.astype(jnp.int32).reshape(1)
    meta = (core_id, short_len, long_len, short_count, long_count)
    sds = jax.ShapeDtypeStruct

    def swap(values, bit, axis="tensor"):
        size = lax.axis_size(axis)
        return lax.ppermute(values, axis, [(i, i ^ bit) for i in range(size)])

    def after(value, *others):
        return lax.optimization_barrier((value,) + others)[0]

    def global_spec(start=0, flip=0):
        def index(i, core, *_):
            i = i + start
            first = core[0] if flip == 0 else 1 - core[0]
            return (2 * i + jnp.where(i < short_blocks, first, 1 - first), 0)

        return pl.BlockSpec((ROWS, d), index)

    vec_spec = const_spec((8, d))
    row_spec = own_spec(d)

    side_id = side.astype(jnp.int32).reshape(1)
    line_id = (lax.axis_index("dp") // 2).astype(jnp.int32).reshape(1)
    vectors = [query_bias, value_bias, up_bias, output_bias, first_gain, first_shift,
               down_bias, second_gain, second_shift]
    a0, vec = whole_call(
        pack_kernel, "pack", side_id,
        [query_weight.T, key_weight.T, value_weight.T, output_weight, *vectors],
        [sds((piece_rows, d), BF16), sds((8, d), F32)], [pltpu.VMEM((8, d), F32)], True, 61,
    )
    up_split = lax.dynamic_slice_in_dim(up_weight, side * (units // 2), units // 2, 1)
    def boundary(lead, *values):
        out = lax.optimization_barrier((lead,) + values)
        return out[0], list(out[1:])

    a1 = after(swap(a0, 1), up_split)
    a2 = swap(a0, 2)

    weight_scratch = [
        pltpu.VMEM((3 * half, d), BF16),
        pltpu.VMEM((half, d), BF16),
        pltpu.VMEM((32, d), BF16),
    ]
    sems = pltpu.SemaphoreType.DMA((16,))
    stat_scratch = pltpu.VMEM((ROWS, 128), F32)

    def log_spec(start=0):
        return pl.BlockSpec((8, ROWS), lambda i, *_: (i + start, 0))

    head_shapes = [sds((rows, 3 * half), BF16), sds((rows, half), BF16), sds((8 * blocks, ROWS), F32)]
    head_flops = 2 * rows * d * 3 * half + 4 * rows * 320 * half
    qkv_near, mixed_near, stat_near = spread(
        functools.partial(attention_forward_kernel, 0, blocks, short_blocks), "attention_near", (blocks,),
        [global_spec()] + [any_spec()] * 2, [own_spec(3 * half), own_spec(half), log_spec()], head_shapes,
        weight_scratch + [sems, stat_scratch, pltpu.VMEM((3, 1, half), F32)], 5,
        head_flops, rows * d * 8, rows * 320 * 6,
    )(*meta, tokens, a0, a1)

    stat_near, (a2,) = boundary(stat_near, a2)
    u2 = swap(after(up_split, a2), 2)
    d2 = swap(after(down_weight, a2), 2)
    a3 = swap(a2, 1)
    u1 = swap(after(up_weight, a3), 1)

    def far_forward(start, count, extra, alias):
        return spread(
            functools.partial(attention_finish_kernel, start, count, short_blocks), "attention_far", (count,),
            [global_spec(start)] + [any_spec()] * 2 + [own_spec(half, start)] + [any_spec()] * 2 + [vec_spec]
            + [any_spec()] * len(extra),
            [own_spec(3 * half, start), own_spec(half, start), log_spec(start), own_spec(d, start), own_spec(128, start)],
            head_shapes + [sds((rows, d), BF16), sds((rows, 128), F32)],
            weight_scratch + [pltpu.VMEM((half, d), BF16), sems, stat_scratch, pltpu.VMEM((3, 1, half), F32)], 5,
            (head_flops + 2 * rows * d * d) * count // blocks, count * ROWS * d * 10, count * ROWS * 320 * 6, alias,
        )(*meta, tokens, a2, a3, mixed_near, a0, a1, vec, *extra)

    far = list(far_forward(0, short_blocks, [], None))
    far[3], (u2, u1, down_near) = boundary(far[3], u2, u1, down_weight)
    u4 = swap(u2, 1, "dp")
    u3, d1 = swap(u2, 1), swap(down_near, 1)
    qkv_far, mixed_far, stat_far, normed, scale_one = far_forward(
        short_blocks, long_blocks, far, {12 + n: n for n in range(5)}
    )
    normed, (u4, u3, d2, d1) = boundary(normed, u4, u3, d2, d1)
    u5, d3 = swap(u4, 1), swap(d2, 1)
    ups = (up_weight, u1, u2, u3, u4, u5)
    downs = (down_weight, d1, d2, d3)
    bias_spec = pl.BlockSpec((16, d), lambda *_: (4 * width // 16, 0), pipeline_mode=pl.Buffered(1))
    up_specs = [any_spec()] * len(ups)
    down_specs = [any_spec()] * len(downs)
    ffn_scratch = [
        pltpu.VMEM((4, d, units), BF16),
        pltpu.VMEM((4, units, d), BF16),
    ]
    ffn_sems = pltpu.SemaphoreType.DMA((16,))
    whole_out, out_rows, grad_low, slope, down_mine, down_partner, sums_two = spread(
        functools.partial(ffn_forward_kernel, short_blocks), "ffn_forward", (blocks,),
        [row_spec, global_spec()] + up_specs + down_specs + [bias_spec] * 4 + [vec_spec],
        [global_spec(), row_spec, row_spec, own_spec(4 * units)] + [const_spec((units, d))] * 2 + [vec_spec],
        [sds((2 * rows, d), BF16), sds((rows, d), BF16), sds((rows, d), BF16), sds((rows, 4 * units), BF16)]
        + [sds((units, d), BF16)] * 2 + [sds((8, d), F32)],
        [pltpu.VMEM((4, ROWS, units), BF16), pltpu.VMEM((2, units, d), F32), pltpu.VMEM((3, 8, d), F32)]
        + ffn_scratch + [pltpu.VMEM((4, 1, units), F32), pltpu.VMEM((ROWS, d), F32), ffn_sems],
        6, 2 * rows * d * 10 * units, rows * d * 20, rows * 8 * units,
    )(*meta, side_id, normed, cotangent, *ups, *downs, a0, a1, a2, a3, vec)

    custom = lax.axis_size("dp") == 8

    line_steps = (
        [(0, 1), (3, 2)],
        [(1, 2), (2, 1)],
        [(1, 0), (2, 3)],
    )

    def along_line(values, stage):
        pairs = [(2 * i + n, 2 * j + n) for i, j in line_steps[stage] for n in range(2)]
        return lax.ppermute(values, "dp", pairs)

    class Reduction:
        def __init__(self, mine, partner, central):
            self.mine, self.size, self.central = mine, mine.shape[0], central
            self.moved = [swap(partner, 1)]
            self.stage = 0

        def part(self, count):
            return sds((self.size // count, d), BF16)

        def step(self):
            got = self.moved
            stage, self.stage = self.stage, self.stage + 1
            if not custom:
                if stage == 0:
                    total = (self.mine.astype(F32) + got[0].astype(F32)).astype(BF16)
                    self.moved = [lax.psum(total, "dp")]
                return self.moved[0]
            if stage == 0:
                self.keep, send = whole_call(
                    route_halves_kernel, "halves", side_id, [self.mine, got[0]], [self.part(2)] * 2
                )
                sent, self.moved = [send], [swap(send, 1, "dp")]
            elif self.central and stage < 4:
                (self.keep,) = whole_call(add_kernel, "add", line_id, [self.keep, got[0]], [self.part(2)])
                sent, self.moved = [self.keep], [along_line(self.keep, stage - 1)]
            elif self.central and stage == 4:
                (self.keep,) = whole_call(choose_kernel, "choose", line_id, [self.keep, got[0]], [self.part(2)])
                sent, self.moved = [self.keep], [swap(self.keep, 1, "dp")]
            elif stage == 1:
                self.keep, *sent = whole_call(
                    route_quarters_kernel, "quarters", line_id, [self.keep, got[0]], [self.part(8)] * 4
                )
                self.moved = [swap(v, 2 * (k + 1), "dp") for k, v in enumerate(sent)]
            elif stage == 2:
                (self.keep,) = whole_call(add_kernel, "add", line_id, [self.keep, *got], [self.part(8)])
                sent = [self.keep]
                self.moved = [swap(self.keep, 2 * k, "dp") for k in (1, 2, 3)]
            elif stage == 3:
                (self.keep,) = whole_call(
                    join_kernel, "join_quarters", line_id, [self.keep, *got], [self.part(2)]
                )
                sent, self.moved = [self.keep], [swap(self.keep, 1, "dp")]
            return sent[0]

        def finish(self, *sizes):
            shapes = [sds((n, d), F32) for n in sizes]
            if not custom:
                total = self.moved[0].astype(F32)
                cuts = [sum(sizes[:n]) for n in range(len(sizes))]
                return [total[at : at + n] for at, n in zip(cuts, sizes)]
            operands = [self.keep, self.moved[0]]
            return whole_call(
                finish_kernel, "finish", side_id, operands, shapes, [pltpu.VMEM((self.size, d), F32)], True
            )

    def settle(lead, reductions, *extra):
        lead, values = boundary(lead, *[v for r in reductions for v in r.moved], *extra)
        for r in reductions:
            count = len(r.moved)
            r.moved, values = values[:count], values[count:]
        return (lead, *values)

    grad_low, down_mine, down_partner = lax.optimization_barrier((grad_low, down_mine, down_partner))
    down_reduce = Reduction(down_mine, down_partner, True)
    tie = down_reduce.step()
    grad_low = after(grad_low, tie)
    moved_out = swap(after(out_rows, tie), 1)

    pack_rows = units + width + 64
    hidden_low, mine, partner = spread(
        ffn_backward_kernel, "ffn_backward", (blocks,),
        [row_spec, own_spec(4 * units), row_spec, own_spec(128), own_spec(half), vec_spec]
        + up_specs + down_specs + [vec_spec],
        [row_spec] + [const_spec((pack_rows, d))] * 2,
        [sds((rows, d), BF16)] + [sds((pack_rows, d), BF16)] * 2,
        [pltpu.VMEM((2, d, units), F32), pltpu.VMEM((half, d), F32), pltpu.VMEM((7, 8, d), F32),
         pltpu.VMEM((4, ROWS, units), BF16)] + ffn_scratch + [pltpu.VMEM((ROWS, d), F32), ffn_sems],
        1, 2 * rows * d * 10 * units, rows * d * 16, 0,
    )(side_id, grad_low, slope, normed, scale_one, mixed_near, sums_two, *ups, *downs, vec)
    hidden_low, mine, partner, moved_out = settle(hidden_low, [down_reduce], mine, partner, moved_out)
    tie = down_reduce.step()
    partner = after(partner, tie)
    up_reduce = Reduction(mine, partner, True)
    tie = up_reduce.step()
    hidden_low = after(hidden_low, tie)

    qkv_rows = 3 * width + 64
    sums = [sds((3, half, d), F32), sds((2, 8, half), F32)]
    sum_specs = [const_spec(v.shape) for v in sums]

    def near_backward(start, count, extra, extra_specs, outs, out_specs, alias):
        return spread(
            functools.partial(attention_backward_kernel, start, short_blocks), "attention_near_backward", (count,),
            [own_spec(d, start), log_spec(start), own_spec(3 * half, start), own_spec(half, start), global_spec(start)]
            + [any_spec()] * 2 + extra_specs,
            [own_spec(3 * half)] + out_specs,
            [sds((count * ROWS, 3 * half), BF16)] + outs,
            weight_scratch + [sems, pltpu.VMEM((ROWS, half), BF16), pltpu.VMEM((8, ROWS), F32),
                              pltpu.VMEM((3, half, d), F32), pltpu.VMEM((2, 8, half), F32)],
            5, count * ROWS * (10 * d * half + 3200 * half), count * ROWS * d * 16, count * ROWS * 320 * 6,
        )(*meta, hidden_low, stat_near, qkv_near, mixed_near, tokens, a0, a1, *extra)

    low_short, *sums_short = near_backward(0, short_blocks, [], [], sums, sum_specs, None)
    (low_short,) = settle(low_short, [down_reduce, up_reduce])
    tie = down_reduce.step()
    tie_two = up_reduce.step()
    sums_short[1] = after(sums_short[1], tie, tie_two)
    low_long, mine, partner = near_backward(
        short_blocks, long_blocks, sums_short, sum_specs,
        [sds((qkv_rows, d), BF16)] * 2, [const_spec((qkv_rows, d))] * 2, None,
    )
    low_long, mine, partner = settle(low_long, [down_reduce, up_reduce], mine, partner)
    ties = [down_reduce.step(), up_reduce.step()]
    qkv_reduce = Reduction(mine, after(partner, *ties), False)
    ties += [qkv_reduce.step()]

    def far_backward(start, count, low_near, extra, alias):
        return spread(
            functools.partial(attention_input_kernel, start, short_blocks), "attention_far_backward", (count,),
            [own_spec(d, start), log_spec(start), own_spec(3 * half, start), own_spec(half, start), own_spec(3 * half)]
            + [any_spec()] * (4 + len(extra)),
            [own_spec(d, start), global_spec(start)], [sds((rows, d), BF16), sds((2 * rows, d), F32)],
            weight_scratch + [pltpu.VMEM((3 * half, d), BF16), sems, pltpu.VMEM((ROWS, 3 * half), BF16),
                              pltpu.VMEM((ROWS, half), BF16), pltpu.VMEM((8, ROWS), F32)],
            5, count * ROWS * (14 * d * half + 3200 * half), count * ROWS * d * 16, count * ROWS * 320 * 6, alias,
        )(*meta, hidden_low, stat_far, qkv_far, mixed_far, low_near, a2, a3, a0, a1, *extra)

    low_short = after(low_short, *ties)
    rows_short, whole_in = far_backward(0, short_blocks, low_short, [], None)
    (rows_short,) = settle(rows_short, [down_reduce, up_reduce, qkv_reduce])
    ties = [qkv_reduce.step(), up_reduce.step(), down_reduce.step()]
    low_long = after(low_long, *ties)
    rows_all, whole_in = far_backward(
        short_blocks, long_blocks, low_long, [rows_short, whole_in], {14: 0, 15: 1}
    )
    (rows_all,) = settle(rows_all, [down_reduce, up_reduce, qkv_reduce])
    tie = qkv_reduce.step()
    tie = after(tie, up_reduce.step())
    down_reduce.moved[0] = after(down_reduce.moved[0], tie)
    (grad_down,) = down_reduce.finish(units)
    moved_rows = swap(after(rows_all, tie), 1)

    def place(whole, other, start, count):
        return spread(
            place_kernel, "place", (count,), [own_spec(d), any_spec()], global_spec(start, 1),
            sds(whole.shape, whole.dtype), (), 1, 0, other.size * 6, 0, {2: 0},
        )(core_id, other, whole)

    layer_output = place(whole_out, after(moved_out, tie), 0, blocks)
    layer_output, moved_rows = settle(layer_output, [qkv_reduce], moved_rows)
    tie = qkv_reduce.step()
    input_grad = place(whole_in, after(moved_rows, tie), 0, blocks)
    up_reduce.moved[0] = after(up_reduce.moved[0], tie)
    grad_up, grad_out, small = up_reduce.finish(units, width, 16)
    grad_up, input_grad = settle(grad_up, [qkv_reduce], input_grad)
    grad_query, grad_key, grad_value, heads = qkv_reduce.finish(width, width, width, 16)
    return (
        layer_output,
        input_grad,
        grad_query.T,
        heads[0, :width],
        grad_key.T,
        grad_value.T,
        heads[1, :width],
        grad_out,
        small[5],
        small[3],
        small[4],
        grad_up,
        small[6],
        grad_down,
        small[2],
        small[0],
        small[1],
    )

def solution(mesh):
    return jax.shard_map(
        per_device,
        mesh=mesh,
        in_specs=(
            P("dp", None),
            P("dp", None),
            P("dp"),
            P("dp"),
            P("dp"),
            P("dp"),
            P(None, "tensor"),
            P("tensor"),
            P(None, "tensor"),
            P(None, "tensor"),
            P("tensor"),
            P("tensor", None),
            P(),
            P(),
            P(),
            P(None, "tensor"),
            P("tensor"),
            P("tensor", None),
            P(),
            P(),
            P(),
        ),
        out_specs=(
            P("dp", None),
            P("dp", None),
            P(None, "tensor"),
            P("tensor"),
            P(None, "tensor"),
            P(None, "tensor"),
            P("tensor"),
            P("tensor", None),
            P(),
            P(),
            P(),
            P(None, "tensor"),
            P("tensor"),
            P("tensor", None),
            P(),
            P(),
            P(),
        ),
        check_vma=False,
    )
```

```python
import functools

import jax
import jax.numpy as jnp
from jax import lax
from jax.experimental import pallas as pl
from jax.experimental.pallas import tpu as pltpu
from jax.sharding import PartitionSpec as P

HEAD_DIM = 64
SHORT_LEN = 128
LONG_LEN = 512
ROWS = 512
SLOTS = ROWS // SHORT_LEN
PAIR = 2 * HEAD_DIM
MASKED = -30000.0
F32 = jnp.float32
BF16 = jnp.bfloat16
VMEM_LIMIT = 60 * 1024 * 1024


def nn(left, right):
    return lax.dot_general(left, right, (((1,), (0,)), ((), ())), preferred_element_type=F32)


def nt(left, right):
    return lax.dot_general(left, right, (((1,), (1,)), ((), ())), preferred_element_type=F32)


def tn(left, right):
    return lax.dot_general(left, right, (((0,), (0,)), ((), ())), preferred_element_type=F32)


def fold_rows(values):
    return jnp.sum(values.reshape(-1, 8, values.shape[-1]), axis=0)


def total_rows(values):
    return jnp.sum(values, axis=0, keepdims=True)


def by_rows(size, body):
    def step(n, carry):
        body(pl.ds(pl.multiple_of(n * 64, 64), 64))
        return carry

    lax.fori_loop(0, size // 64, step, 0)


def clear(ref):
    def body(span):
        for j in range(ref.shape[0]):
            ref[j, span] = jnp.zeros((64, ref.shape[2]), ref.dtype)

    by_rows(ref.shape[1], body)


def copy_rows(source, target, at=0):
    def body(span):
        target[pl.ds(pl.multiple_of(at + span.start, 16), 64)] = source[span].astype(target.dtype)

    if source.shape[0] % 64:
        target[pl.ds(at, source.shape[0])] = source[...].astype(target.dtype)
    else:
        by_rows(source.shape[0], body)


def half_mask(which):
    lanes = lax.broadcasted_iota(jnp.int32, (1, PAIR), 1)
    return (lanes >= HEAD_DIM) if which else (lanes < HEAD_DIM)


def short_valid(meta, block, slot):
    index = SLOTS * (2 * block + meta[0][0]) + slot
    return jnp.where(index < meta[3][0], meta[1][index], 0)


def long_valid(meta, block, short_blocks):
    index = 2 * (block - short_blocks) + 1 - meta[0][0]
    return jnp.where(index < meta[4][0], meta[2][index], 0)


def norm_rows(values):
    centre = values - jnp.mean(values, axis=-1, keepdims=True)
    scale = lax.rsqrt(jnp.mean(centre * centre, axis=-1, keepdims=True) + 1e-12)
    return centre * scale, scale


def norm_back(incoming, normed, scale, gain):
    grad = incoming * gain
    inner = grad - jnp.mean(grad, axis=-1, keepdims=True)
    inner = inner - normed * jnp.mean(grad * normed, axis=-1, keepdims=True)
    return scale * inner


def attention_copies(pieces, sems, wqkv=None, wout=None, bias=None):
    copies = []
    for j, piece in enumerate(pieces):
        width = (piece.shape[0] - 16) // 4
        pairs = []
        if wqkv is not None:
            for k in range(3):
                rows = pl.ds((2 * k + j) * width, width)
                pairs.append((k, piece.at[pl.ds(k * width, width)], wqkv.at[rows]))
        if wout is not None:
            pairs.append((3, piece.at[pl.ds(3 * width, width)], wout.at[pl.ds(j * width, width)]))
        if bias is not None:
            pairs.append((4, piece.at[pl.ds(4 * width, 16)], bias.at[pl.ds(16 * j, 16)]))
        copies += [pltpu.make_async_copy(s, d, sems.at[5 * j + n]) for n, s, d in pairs]
    return copies


def start_all(copies):
    for copy in copies:
        copy.start()


def wait_all(copies):
    for copy in copies:
        copy.wait()


def flat_row(ref):
    return ref[...].astype(F32).reshape(1, ref.shape[0])


def pack_kernel(at, wq, wk, wv, wo, qb, vb, ub, ob, g1, s1, db, g2, s2, piece, vec, wide):
    width = wq.shape[0]
    d = piece.shape[1]
    piece[0:width] = wq[...]
    piece[width : 2 * width] = wk[...]
    piece[2 * width : 3 * width] = wv[...]
    piece[3 * width : 4 * width] = wo[...]
    index = lax.broadcasted_iota(jnp.int32, (16, 1), 0)
    wide[...] = jnp.zeros_like(wide)
    wide[0:1, 0:width] = flat_row(qb)
    wide[1:2, 0:width] = flat_row(vb)
    row_q, row_v, row_u = wide[0:1], wide[1:2], flat_row(ub)
    lead = jnp.where(lax.broadcasted_iota(jnp.int32, (1, d), 1) < d // 2, row_u, 0.0)
    trail = pltpu.roll(row_u - lead, d // 2, 1)
    mine = jnp.where(at[0] == 0, lead, trail)
    far = jnp.where(at[0] == 0, trail, lead)
    rows = [row_u, row_q, pltpu.roll(row_q, width, 1), row_v, pltpu.roll(row_v, width, 1)]
    block = jnp.zeros((16, d), F32)
    for n, row in enumerate(rows + [None] * 4 + [mine, far]):
        if row is not None:
            block = jnp.where(index == n, row, block)
    piece[4 * width : 4 * width + 16] = block.astype(BF16)
    for n, row in enumerate((ob, g1, s1, db, g2, s2)):
        vec[n : n + 1] = flat_row(row)
    vec[6:8] = jnp.zeros((2, d), F32)


def place_kernel(core, other, whole, out):
    out[...] = other[...].astype(out.dtype)


def route_halves_kernel(at, mine, partner, keep, send):
    half = keep.shape[0]
    for out, which in ((keep, at[0]), (send, 1 - at[0])):
        base = which * half

        def body(span):
            rows = pl.ds(pl.multiple_of(base + span.start, 16), 64)
            out[span] = (mine[rows].astype(F32) + partner[rows].astype(F32)).astype(BF16)

        by_rows(half, body)


def route_quarters_kernel(at, keep, other, *outs):
    size = outs[0].shape[0]
    for k, out in enumerate(outs):
        span = pl.ds(pl.multiple_of((at[0] ^ k) * size, 16), size)
        out[...] = (keep[span].astype(F32) + other[span].astype(F32)).astype(BF16)


def add_kernel(at, *refs):
    def body(span):
        refs[-1][span] = sum(ref[span].astype(F32) for ref in refs[:-1]).astype(BF16)

    size = refs[-1].shape[0]
    if size % 64:
        body(pl.ds(0, size))
    else:
        by_rows(size, body)


def choose_kernel(at, own, other, out):
    central = jnp.logical_or(at[0] == 1, at[0] == 2)

    @pl.when(central)
    def _():
        out[...] = own[...]

    @pl.when(jnp.logical_not(central))
    def _():
        out[...] = other[...]


def join_kernel(at, *refs):
    out = refs[-1]
    size = refs[0].shape[0]
    for k, ref in enumerate(refs[:-1]):
        copy_rows(ref, out, pl.multiple_of((at[0] ^ k) * size, 16))


def finish_kernel(at, own, other, *refs):
    outs, whole = refs[:-1], refs[-1]
    join_kernel(at, own, other, whole)
    start = 0
    for out in outs:
        copy_rows(whole.at[pl.ds(start, out.shape[0])], out)
        start += out.shape[0]


def stacked(values):
    zero = jnp.zeros_like(values)
    return jnp.concatenate([jnp.where(half_mask(e), values, zero) for e in range(2)], axis=0)


def unstacked(values):
    size = values.shape[0] // 2
    return jnp.where(half_mask(0), values[:size], values[size:])


def attention_heads_forward(start, count, short_blocks, meta, x, weights, qkv, mixed, logs, stat):
    wqkv, bias, head_bias = weights
    block = pl.program_id(0) + start
    half = mixed.shape[1]

    @pl.when(pl.program_id(0) == 0)
    def _():
        small = bias[...].astype(F32)
        head_bias[0] = (small[1:2] + small[18:19])[:, 0:half]
        head_bias[1] = jnp.zeros((1, half), F32)
        head_bias[2] = (small[3:4] + small[20:21])[:, 0:half]

    def project(k, carry):
        span = pl.ds(pl.multiple_of(k * half, half), half)
        qkv[:, span] = (nt(x[...], wqkv[span]) + head_bias[k]).astype(BF16)
        return carry

    lax.fori_loop(0, 3, project, 0)
    stat[...] = jnp.zeros_like(stat)
    lanes = lax.broadcasted_iota(jnp.int32, (1, 128), 1)

    def tiles(pair, spans):
        column = pl.multiple_of(pair * PAIR, PAIR)
        q, scores = [], []
        for query_at, queries, key_at, keys, valid in spans:
            part = qkv[query_at : query_at + queries, pl.ds(column, PAIR)] * jnp.asarray(0.125, BF16)
            key_part = qkv[key_at : key_at + keys, pl.ds(half + column, PAIR)]
            scores.append(nt(stacked(part), key_part))
        live = [lax.broadcasted_iota(jnp.int32, (1, t[3]), 1) < t[4] for t in spans]
        scores = [jnp.where(a, v, MASKED) for a, v in zip(live, scores)]
        top = [jnp.max(v, axis=-1, keepdims=True) for v in scores]
        weights = [jnp.exp(v - m) for v, m in zip(scores, top)]
        total = [jnp.sum(v, axis=-1, keepdims=True) for v in weights]
        out = [
            nn(v.astype(BF16), qkv[t[2] : t[2] + t[3], pl.ds(2 * half + column, PAIR)])
            for v, t in zip(weights, spans)
        ]
        for (query_at, queries, *_), m, n, v in zip(spans, top, total, out):
            log = m + jnp.log(n)
            rows = stat[query_at : query_at + queries]
            rows = jnp.where(lanes == 2 * pair, log[:queries], rows)
            stat[query_at : query_at + queries] = jnp.where(lanes == 2 * pair + 1, log[queries:], rows)
            mixed[query_at : query_at + queries, pl.ds(column, PAIR)] = unstacked(v * (1.0 / n)).astype(BF16)

    def short_path():
        spans = [
            (slot * SHORT_LEN, SHORT_LEN, slot * SHORT_LEN, SHORT_LEN, short_valid(meta, block, slot))
            for slot in range(SLOTS)
        ]

        def body(pair, carry):
            tiles(pair, spans)
            return carry

        lax.fori_loop(0, half // PAIR, body, 0)

    def long_path():
        valid = long_valid(meta, block, short_blocks)
        spans = [(part * 256, 256, 0, LONG_LEN, valid) for part in range(2)]

        def body(pair, carry):
            tiles(pair, spans)
            return carry

        lax.fori_loop(0, half // PAIR, body, 0)

    if start < short_blocks:
        pl.when(block < short_blocks)(short_path)
    if start + count > short_blocks:
        pl.when(block >= short_blocks)(long_path)
    logs[...] = stat[...].T[0:8]


def attention_forward_kernel(
    start, count, short_blocks, core, slen, llen, scount, lcount, x, a0, a1, qkv, mixed, logs,
    wqkv, wout, bias, sems, stat, head_bias,
):
    copies = attention_copies((a0, a1), sems, wqkv=wqkv, bias=bias)

    @pl.when(pl.program_id(0) == 0)
    def _():
        start_all(copies)
        wait_all(copies)

    meta = (core, slen, llen, scount, lcount)
    attention_heads_forward(start, count, short_blocks, meta, x, (wqkv, bias, head_bias), qkv, mixed, logs, stat)


def attention_finish_kernel(
    start, count, short_blocks, core, slen, llen, scount, lcount, x, a2, a3, mixed_near, a0, a1, vec, *rest,
):
    qkv, mixed, logs, normed, scale_rows, wqkv, wout, bias, near_out, sems, stat, head_bias = rest[-12:]

    width = near_out.shape[0] // 2
    needed = attention_copies((a2, a3), sems, wqkv=wqkv, bias=bias)
    later = attention_copies((a2, a3), sems, wout=wout) + [
        pltpu.make_async_copy(
            piece.at[pl.ds(3 * width, width)], near_out.at[pl.ds(j * width, width)], sems.at[10 + j]
        )
        for j, piece in enumerate((a0, a1))
    ]

    @pl.when(pl.program_id(0) == 0)
    def _():
        start_all(needed + later)
        wait_all(needed)

    meta = (core, slen, llen, scount, lcount)
    attention_heads_forward(start, count, short_blocks, meta, x, (wqkv, bias, head_bias), qkv, mixed, logs, stat)

    @pl.when(pl.program_id(0) == 0)
    def _():
        wait_all(later)

    hidden = x[...].astype(F32) + vec[0:1]
    hidden = hidden + nn(mixed_near[...], near_out[...]) + nn(mixed[...], wout[...])
    rows, scale = norm_rows(hidden)
    normed[...] = rows.astype(BF16)
    scale_rows[...] = jnp.broadcast_to(scale, scale_rows.shape)


def weight_copies(side, ups, downs, up_all, down_all, sems):
    half = ups[2].shape[1]
    spans = [pl.ds(pl.multiple_of(at * half, 16), half) for at in (side[0], 1 - side[0])]
    copies = []
    for j in range(2):
        copies.append([(ups[j], up_all.at[j]), (downs[j], down_all.at[j])])
    for j in range(2):
        pairs = []
        for n in range(2):
            part = pl.ds(n * half, half)
            pairs.append((ups[2 + 2 * n + j], up_all.at[2 + j, :, part]))
            pairs.append((downs[2 + j].at[spans[n]], down_all.at[2 + j, part]))
        copies.append(pairs)
    return [
        [pltpu.make_async_copy(s, d, sems.at[4 * j + n]) for n, (s, d) in enumerate(pairs)]
        for j, pairs in enumerate(copies)
    ]


def start_weights(copies):
    for pairs in copies:
        for copy in pairs:
            copy.start()


def wait_weights(copies, step):
    for at in range(2):

        @pl.when(jnp.logical_and(pl.program_id(0) == 0, step == at))
        def _():
            for pairs in copies[2 * at : 2 * at + 2]:
                for copy in pairs:
                    copy.wait()


def ffn_forward_kernel(short_blocks, core, slen, llen, scount, lcount, side, normed, cotangent, *rest):
    ups, downs, biases = rest[0:6], rest[6:10], rest[10:14]
    vec, layer_out, layer_rows, grad_low, slope, down_mine, down_partner, sums = rest[14:22]
    active, down_sum, vec_sum, up_all, down_all, bias_all, total, sems = rest[22:]
    meta = (core, slen, llen, scount, lcount)
    block = pl.program_id(0)
    units = up_all.shape[2]
    half = units // 2
    copies = weight_copies(side, ups, downs, up_all, down_all, sems)

    @pl.when(block == 0)
    def _():
        start_weights(copies)
        clear(down_sum)
        vec_sum[...] = jnp.zeros_like(vec_sum)
        for j in range(2):
            bias_all[j] = biases[j][0:1].astype(F32)
            for n in range(2):
                bias_all[2 + j, :, n * half : (n + 1) * half] = biases[2 + j][9 + n : 10 + n, 0:half].astype(F32)

    first = normed[...].astype(F32) * vec[1:2] + vec[2:3]
    first_low = first.astype(BF16)
    total[...] = first + vec[3:4]

    def groups(step, carry):
        wait_weights(copies, step)
        for e in range(2):
            j = 2 * step + e
            inner = nn(first_low, up_all[j]) + bias_all[j]
            chance = 0.5 * (1.0 + lax.erf(inner * 0.7071067811865476))
            low_units = (inner * chance).astype(BF16)
            slope[:, pl.ds(pl.multiple_of(j * units, units), units)] = (
                chance + inner * jnp.exp(-0.5 * inner * inner) * 0.3989422804014327
            ).astype(BF16)
            active[j] = low_units
            total[...] += nn(low_units, down_all[j])
        return carry

    lax.fori_loop(0, 2, groups, 0)
    rows, scale = norm_rows(total[...])
    result = (rows * vec[4:5] + vec[5:6]).astype(BF16)
    layer_out[...] = result
    layer_rows[...] = result
    position = lax.broadcasted_iota(jnp.int32, (ROWS, 1), 0)
    slot = position // SHORT_LEN
    short_limit = jnp.zeros((ROWS, 1), jnp.int32)
    for n in range(SLOTS):
        short_limit = jnp.where(slot == n, short_valid(meta, jnp.minimum(block, short_blocks - 1), n), short_limit)
    long_limit = long_valid(meta, jnp.maximum(block, short_blocks), short_blocks)
    is_short = block < short_blocks
    alive = jnp.where(is_short, position % SHORT_LEN, position) < jnp.where(
        is_short, short_limit, long_limit
    )
    upstream = jnp.where(alive, cotangent[...].astype(F32), 0.0)
    grad = norm_back(upstream, rows, scale, vec[4:5])
    low = grad.astype(BF16)
    grad_low[...] = low
    vec_sum[0] += fold_rows(upstream * rows)
    vec_sum[1] += fold_rows(upstream)
    vec_sum[2] += fold_rows(grad)
    for j in range(2):
        down_sum[j] += tn(active[j], low)

    @pl.when(block == pl.num_programs(0) - 1)
    def _():
        copy_rows(down_sum.at[0], down_mine)
        copy_rows(down_sum.at[1], down_partner)
        sums[...] = jnp.zeros_like(sums)
        for n in range(3):
            sums[n : n + 1] = total_rows(vec_sum[n])


def ffn_backward_kernel(side, grad_low, slope, normed, stat, mixed, sums_two, *rest):
    ups, downs = rest[0:6], rest[6:10]
    vec, hidden_low, mine, partner = rest[10:14]
    up_sum, out_sum, vec_sum, kept, up_all, down_all, total, sems = rest[14:]
    block = pl.program_id(0)
    units = up_sum.shape[2]
    width = mixed.shape[1] // 2
    copies = weight_copies(side, ups, downs, up_all, down_all, sems)

    @pl.when(block == 0)
    def _():
        start_weights(copies)
        clear(up_sum)
        out_sum[...] = jnp.zeros_like(out_sum)
        vec_sum[...] = jnp.zeros_like(vec_sum)

    low = grad_low[...]
    total[...] = low.astype(F32)

    def groups(step, carry):
        wait_weights(copies, step)
        for e in range(2):
            j = 2 * step + e
            inner = nt(low, down_all[j]) * slope[:, pl.ds(pl.multiple_of(j * units, units), units)].astype(F32)
            inner_low = inner.astype(BF16)
            total[...] += nt(inner_low, up_all[j])
            vec_sum[j] += fold_rows(inner)
            kept[j] = inner_low
        return carry

    lax.fori_loop(0, 2, groups, 0)
    rows = normed[...].astype(F32)
    first_low = (rows * vec[1:2] + vec[2:3]).astype(BF16)
    for j in range(2):
        up_sum[j] += tn(first_low, kept[j])
    incoming = total[...]
    grad = norm_back(incoming, rows, stat[:, 0:1], vec[1:2])
    vec_sum[4] += fold_rows(incoming * rows)
    vec_sum[5] += fold_rows(incoming)
    vec_sum[6] += fold_rows(grad)
    grad_attn = grad.astype(BF16)
    hidden_low[...] = grad_attn
    out_sum[...] += tn(mixed[...], grad_attn)

    @pl.when(block == pl.num_programs(0) - 1)
    def _():
        index = lax.broadcasted_iota(jnp.int32, (16, 1), 0)
        shared = [sums_two[n : n + 1] for n in range(3)] + [total_rows(vec_sum[n]) for n in range(4, 7)]
        for j, out in enumerate((mine, partner)):
            copy_rows(up_sum.at[j], out)
            copy_rows(out_sum.at[pl.ds(j * width, width)], out, units)
            out[units + width :] = jnp.zeros((out.shape[0] - units - width, out.shape[1]), BF16)
            rows_out = jnp.zeros((16, out.shape[1]), F32)
            for n, row in enumerate(shared + [total_rows(vec_sum[j])]):
                rows_out = jnp.where(index == n, row, rows_out)
            out[units + width : units + width + 16] = rows_out.astype(BF16)


def attention_heads_backward(start, short_blocks, meta, logs, qkv, mixed, mixed_grad, low_qkv, delta):
    block = pl.program_id(0) + start
    half = mixed.shape[1]
    own = (mixed_grad[...].astype(F32) * mixed[...].astype(F32)).astype(BF16)
    head = lax.broadcasted_iota(jnp.int32, (8, half), 1) // HEAD_DIM
    pick = jnp.where(head == lax.broadcasted_iota(jnp.int32, (8, half), 0), 1.0, 0.0)
    delta[...] = nt(pick.astype(BF16), own)

    index = lax.broadcasted_iota(jnp.int32, (8, 1), 0)

    def tiles(pair, size, valids):
        column = pl.multiple_of(pair * PAIR, PAIR)
        spans = [pl.ds(n * size, size) for n in range(len(valids))]

        def rows(ref, span):
            picked = [total_rows(jnp.where(index == 2 * pair + e, ref[:, span], 0.0)) for e in range(2)]
            return jnp.concatenate(picked, axis=1)

        q = [stacked(qkv[t, pl.ds(column, PAIR)] * jnp.asarray(0.125, BF16)) for t in spans]
        g = [stacked(mixed_grad[t, pl.ds(column, PAIR)]) for t in spans]
        k = [qkv[t, pl.ds(half + column, PAIR)] for t in spans]
        scores = [nt(b, a) for a, b in zip(q, k)]
        grads = [nt(qkv[t, pl.ds(2 * half + column, PAIR)], a) for t, a in zip(spans, g)]
        place = lax.broadcasted_iota(jnp.int32, (size, 1), 0)
        probs = [
            jnp.where(place < valid, jnp.exp(v - rows(logs, t)), 0.0)
            for v, t, valid in zip(scores, spans, valids)
        ]
        scores = [(p * (v - rows(delta, t))).astype(BF16) for p, v, t in zip(probs, grads, spans)]
        dq = [tn(v, b) for v, b in zip(scores, k)]
        dk = [nn(v, a) for v, a in zip(scores, q)]
        dv = [nn(p.astype(BF16), a) for p, a in zip(probs, g)]
        for t, a, b, c in zip(spans, dq, dk, dv):
            low_qkv[t, pl.ds(column, PAIR)] = (unstacked(a) * 0.125).astype(BF16)
            low_qkv[t, pl.ds(half + column, PAIR)] = b.astype(BF16)
            low_qkv[t, pl.ds(2 * half + column, PAIR)] = c.astype(BF16)

    if start < short_blocks:
        valids = [short_valid(meta, block, slot) for slot in range(SLOTS)]
        size = SHORT_LEN
    else:
        valids = [long_valid(meta, block, short_blocks)]
        size = LONG_LEN

    def body(pair, carry):
        tiles(pair, size, valids)
        return carry

    lax.fori_loop(0, half // PAIR, body, 0)


def attention_backward_kernel(
    start, short_blocks, core, slen, llen, scount, lcount, hidden_low, stat, qkv, mixed, x,
    a0, a1, *rest,
):
    if start:
        sums_in, vec_in, low_qkv, mine, partner = rest[:5]
    else:
        low_qkv, qkv_out, vec_out = rest[:3]
    wqkv, wout, bias, sems, mixed_grad, delta, qkv_sum, vec_sum = rest[-8:]
    meta = (core, slen, llen, scount, lcount)
    block = pl.program_id(0)
    half = mixed.shape[1]
    width = half // 2

    copies = attention_copies((a0, a1), sems, wout=wout)
    carried = pltpu.make_async_copy(sums_in, qkv_sum, sems.at[15]) if start else None

    @pl.when(block == 0)
    def _():
        start_all(copies)
        if start:
            carried.start()
        wait_all(copies)
        if start:
            vec_sum[...] = vec_in[...]
        else:
            clear(qkv_sum)
            vec_sum[...] = jnp.zeros_like(vec_sum)

    mixed_grad[...] = nt(hidden_low[...], wout[...]).astype(BF16)
    attention_heads_backward(start, short_blocks, meta, stat, qkv, mixed, mixed_grad, low_qkv, delta)
    vec_sum[0] += fold_rows(low_qkv[:, 0:half].astype(F32))
    vec_sum[1] += fold_rows(low_qkv[:, 2 * half : 3 * half].astype(F32))

    if start:

        @pl.when(block == 0)
        def _():
            carried.wait()

    for k in range(3):
        qkv_sum[k] += tn(low_qkv[:, k * half : (k + 1) * half], x[...])

    @pl.when(block == pl.num_programs(0) - 1)
    def _():
        if not start:
            leaving = pltpu.make_async_copy(qkv_sum, qkv_out, sems.at[15])
            leaving.start()
            leaving.wait()
            vec_out[...] = vec_sum[...]
        else:
            index = lax.broadcasted_iota(jnp.int32, (16, 1), 0)
            heads = [total_rows(vec_sum[n]) for n in range(2)]
            for j, out in enumerate((mine, partner)):
                for k in range(3):
                    out[k * width : (k + 1) * width] = qkv_sum[k, j * width : (j + 1) * width].astype(BF16)
                out[3 * width :] = jnp.zeros((out.shape[0] - 3 * width, out.shape[1]), BF16)
                rows_out = jnp.zeros((16, half), F32)
                for n, row in enumerate(heads):
                    row = pltpu.roll(row, half - width, 1) if j else row
                    rows_out = jnp.where(index == n, row, rows_out)
                out[3 * width : 3 * width + 16, 0:half] = rows_out.astype(BF16)


def attention_input_kernel(
    start, short_blocks, core, slen, llen, scount, lcount, hidden_low, stat, qkv, mixed, low_near,
    a2, a3, a0, a1, *rest,
):
    input_rows, input_grad = rest[-10:-8]
    wqkv, wout, bias, near_qkv, sems, low_qkv, mixed_grad, delta = rest[-8:]
    meta = (core, slen, llen, scount, lcount)

    width = near_qkv.shape[0] // 6
    needed = attention_copies((a2, a3), sems, wout=wout)
    later = attention_copies((a2, a3), sems, wqkv=wqkv) + [
        pltpu.make_async_copy(
            piece.at[pl.ds(k * width, width)],
            near_qkv.at[pl.ds((2 * k + j) * width, width)],
            sems.at[10 + 2 * k + j],
        )
        for k in range(3)
        for j, piece in enumerate((a0, a1))
    ]

    @pl.when(pl.program_id(0) == 0)
    def _():
        start_all(needed + later)
        wait_all(needed)

    low = hidden_low[...]
    mixed_grad[...] = nt(low, wout[...]).astype(BF16)
    attention_heads_backward(start, short_blocks, meta, stat, qkv, mixed, mixed_grad, low_qkv, delta)

    @pl.when(pl.program_id(0) == 0)
    def _():
        wait_all(later)

    total = low.astype(F32) + nn(low_near[...], near_qkv[...]) + nn(low_qkv[...], wqkv[...])
    input_rows[...] = total.astype(BF16)
    input_grad[...] = total


def const_spec(shape):
    return pl.BlockSpec(
        shape, lambda *_: (0,) * len(shape), pipeline_mode=pl.Buffered(1)
    )


def any_spec():
    return pl.BlockSpec(memory_space=pl.ANY)


def own_spec(width, start=0):
    return pl.BlockSpec((ROWS, width), lambda i, *_: (i + start, 0))


def whole_call(body, name, which, operands, shapes, scratch=(), keep=False, limit=24):
    moved = sum(v.size * v.dtype.itemsize for v in list(operands) + list(shapes))
    vmem = pl.BlockSpec(memory_space=pltpu.VMEM)
    if not keep:
        operands = [pltpu.with_memory_space_constraint(v, pltpu.VMEM) for v in operands]
        shapes = [pltpu.VMEM(v.shape, v.dtype) for v in shapes]
    return pl.pallas_call(
        body,
        name=name,
        in_specs=[pl.BlockSpec(memory_space=pltpu.SMEM)] + [vmem] * len(operands),
        out_specs=[vmem] * len(shapes),
        out_shape=shapes,
        scratch_shapes=list(scratch),
        compiler_params=pltpu.CompilerParams(vmem_limit_bytes=limit * 1024 * 1024),
        cost_estimate=pl.CostEstimate(flops=0, bytes_accessed=moved, transcendentals=0),
    )(which, *operands)


def spread(body, name, grid, in_specs, out_specs, out_shape, scratch=(), prefetch=0, flops=0, moved=0, exps=0, alias=None):
    return pl.pallas_call(
        body,
        name=name,
        grid_spec=pltpu.PrefetchScalarGridSpec(
            num_scalar_prefetch=prefetch,
            grid=grid,
            in_specs=in_specs,
            out_specs=out_specs,
            scratch_shapes=list(scratch),
        ),
        out_shape=out_shape,
        input_output_aliases=alias or {},
        compiler_params=pltpu.CompilerParams(
            dimension_semantics=("arbitrary",), vmem_limit_bytes=VMEM_LIMIT
        ),
        cost_estimate=pl.CostEstimate(flops=flops, bytes_accessed=moved, transcendentals=exps),
    )


def per_device(
    tokens,
    cotangent,
    short_len,
    long_len,
    short_count,
    long_count,
    query_weight,
    query_bias,
    key_weight,
    value_weight,
    value_bias,
    output_weight,
    output_bias,
    first_gain,
    first_shift,
    up_weight,
    up_bias,
    down_weight,
    down_bias,
    second_gain,
    second_shift,
):
    d = tokens.shape[1]
    width = query_weight.shape[1]
    units = up_weight.shape[1]
    half = 2 * width
    piece_rows = 4 * width + 16
    short_blocks = short_len.shape[0] * SHORT_LEN // (2 * ROWS)
    long_blocks = long_len.shape[0] * LONG_LEN // (2 * ROWS)
    blocks = short_blocks + long_blocks
    rows = blocks * ROWS
    core = lax.axis_index("tensor") % 2
    side = lax.axis_index("dp") % 2
    core_id = core.astype(jnp.int32).reshape(1)
    meta = (core_id, short_len, long_len, short_count, long_count)
    sds = jax.ShapeDtypeStruct

    def swap(values, bit, axis="tensor"):
        size = lax.axis_size(axis)
        return lax.ppermute(values, axis, [(i, i ^ bit) for i in range(size)])

    def after(value, *others):
        return lax.optimization_barrier((value,) + others)[0]

    def global_spec(start=0, flip=0):
        def index(i, core, *_):
            i = i + start
            first = core[0] if flip == 0 else 1 - core[0]
            return (2 * i + jnp.where(i < short_blocks, first, 1 - first), 0)

        return pl.BlockSpec((ROWS, d), index)

    vec_spec = const_spec((8, d))
    row_spec = own_spec(d)

    side_id = side.astype(jnp.int32).reshape(1)
    line_id = (lax.axis_index("dp") // 2).astype(jnp.int32).reshape(1)
    vectors = [query_bias, value_bias, up_bias, output_bias, first_gain, first_shift,
               down_bias, second_gain, second_shift]
    a0, vec = whole_call(
        pack_kernel, "pack", side_id,
        [query_weight.T, key_weight.T, value_weight.T, output_weight, *vectors],
        [sds((piece_rows, d), BF16), sds((8, d), F32)], [pltpu.VMEM((8, d), F32)], True, 61,
    )
    up_split = lax.dynamic_slice_in_dim(up_weight, side * (units // 2), units // 2, 1)
    def boundary(lead, *values):
        out = lax.optimization_barrier((lead,) + values)
        return out[0], list(out[1:])

    a1 = after(swap(a0, 1), up_split)
    a2 = swap(a0, 2)

    weight_scratch = [
        pltpu.VMEM((3 * half, d), BF16),
        pltpu.VMEM((half, d), BF16),
        pltpu.VMEM((32, d), BF16),
    ]
    sems = pltpu.SemaphoreType.DMA((16,))
    stat_scratch = pltpu.VMEM((ROWS, 128), F32)

    def log_spec(start=0):
        return pl.BlockSpec((8, ROWS), lambda i, *_: (i + start, 0))

    head_shapes = [sds((rows, 3 * half), BF16), sds((rows, half), BF16), sds((8 * blocks, ROWS), F32)]
    head_flops = 2 * rows * d * 3 * half + 4 * rows * 320 * half
    qkv_near, mixed_near, stat_near = spread(
        functools.partial(attention_forward_kernel, 0, blocks, short_blocks), "attention_near", (blocks,),
        [global_spec()] + [any_spec()] * 2, [own_spec(3 * half), own_spec(half), log_spec()], head_shapes,
        weight_scratch + [sems, stat_scratch, pltpu.VMEM((3, 1, half), F32)], 5,
        head_flops, rows * d * 8, rows * 320 * 6,
    )(*meta, tokens, a0, a1)

    stat_near, (a2,) = boundary(stat_near, a2)
    u2 = swap(after(up_split, a2), 2)
    d2 = swap(after(down_weight, a2), 2)
    a3 = swap(a2, 1)
    u1 = swap(after(up_weight, a3), 1)

    def far_forward(start, count, extra, alias):
        return spread(
            functools.partial(attention_finish_kernel, start, count, short_blocks), "attention_far", (count,),
            [global_spec(start)] + [any_spec()] * 2 + [own_spec(half, start)] + [any_spec()] * 2 + [vec_spec]
            + [any_spec()] * len(extra),
            [own_spec(3 * half, start), own_spec(half, start), log_spec(start), own_spec(d, start), own_spec(128, start)],
            head_shapes + [sds((rows, d), BF16), sds((rows, 128), F32)],
            weight_scratch + [pltpu.VMEM((half, d), BF16), sems, stat_scratch, pltpu.VMEM((3, 1, half), F32)], 5,
            (head_flops + 2 * rows * d * d) * count // blocks, count * ROWS * d * 10, count * ROWS * 320 * 6, alias,
        )(*meta, tokens, a2, a3, mixed_near, a0, a1, vec, *extra)

    far = list(far_forward(0, short_blocks, [], None))
    far[3], (u2, u1, down_near) = boundary(far[3], u2, u1, down_weight)
    u4 = swap(u2, 1, "dp")
    u3, d1 = swap(u2, 1), swap(down_near, 1)
    qkv_far, mixed_far, stat_far, normed, scale_one = far_forward(
        short_blocks, long_blocks, far, {12 + n: n for n in range(5)}
    )
    normed, (u4, u3, d2, d1) = boundary(normed, u4, u3, d2, d1)
    u5, d3 = swap(u4, 1), swap(d2, 1)
    ups = (up_weight, u1, u2, u3, u4, u5)
    downs = (down_weight, d1, d2, d3)
    bias_spec = pl.BlockSpec((16, d), lambda *_: (4 * width // 16, 0), pipeline_mode=pl.Buffered(1))
    up_specs = [any_spec()] * len(ups)
    down_specs = [any_spec()] * len(downs)
    ffn_scratch = [
        pltpu.VMEM((4, d, units), BF16),
        pltpu.VMEM((4, units, d), BF16),
    ]
    ffn_sems = pltpu.SemaphoreType.DMA((16,))
    whole_out, out_rows, grad_low, slope, down_mine, down_partner, sums_two = spread(
        functools.partial(ffn_forward_kernel, short_blocks), "ffn_forward", (blocks,),
        [row_spec, global_spec()] + up_specs + down_specs + [bias_spec] * 4 + [vec_spec],
        [global_spec(), row_spec, row_spec, own_spec(4 * units)] + [const_spec((units, d))] * 2 + [vec_spec],
        [sds((2 * rows, d), BF16), sds((rows, d), BF16), sds((rows, d), BF16), sds((rows, 4 * units), BF16)]
        + [sds((units, d), BF16)] * 2 + [sds((8, d), F32)],
        [pltpu.VMEM((4, ROWS, units), BF16), pltpu.VMEM((2, units, d), F32), pltpu.VMEM((3, 8, d), F32)]
        + ffn_scratch + [pltpu.VMEM((4, 1, units), F32), pltpu.VMEM((ROWS, d), F32), ffn_sems],
        6, 2 * rows * d * 10 * units, rows * d * 20, rows * 8 * units,
    )(*meta, side_id, normed, cotangent, *ups, *downs, a0, a1, a2, a3, vec)

    custom = lax.axis_size("dp") == 8

    line_steps = (
        [(0, 1), (3, 2)],
        [(1, 2), (2, 1)],
        [(1, 0), (2, 3)],
    )

    def along_line(values, stage):
        pairs = [(2 * i + n, 2 * j + n) for i, j in line_steps[stage] for n in range(2)]
        return lax.ppermute(values, "dp", pairs)

    class Reduction:
        def __init__(self, mine, partner, central):
            self.mine, self.size, self.central = mine, mine.shape[0], central
            self.moved = [swap(partner, 1)]
            self.stage = 0

        def part(self, count):
            return sds((self.size // count, d), BF16)

        def step(self):
            got = self.moved
            stage, self.stage = self.stage, self.stage + 1
            if not custom:
                if stage == 0:
                    total = (self.mine.astype(F32) + got[0].astype(F32)).astype(BF16)
                    self.moved = [lax.psum(total, "dp")]
                return self.moved[0]
            if stage == 0:
                self.keep, send = whole_call(
                    route_halves_kernel, "halves", side_id, [self.mine, got[0]], [self.part(2)] * 2
                )
                sent, self.moved = [send], [swap(send, 1, "dp")]
            elif self.central and stage < 4:
                (self.keep,) = whole_call(add_kernel, "add", line_id, [self.keep, got[0]], [self.part(2)])
                sent, self.moved = [self.keep], [along_line(self.keep, stage - 1)]
            elif self.central and stage == 4:
                (self.keep,) = whole_call(choose_kernel, "choose", line_id, [self.keep, got[0]], [self.part(2)])
                sent, self.moved = [self.keep], [swap(self.keep, 1, "dp")]
            elif stage == 1:
                self.keep, *sent = whole_call(
                    route_quarters_kernel, "quarters", line_id, [self.keep, got[0]], [self.part(8)] * 4
                )
                self.moved = [swap(v, 2 * (k + 1), "dp") for k, v in enumerate(sent)]
            elif stage == 2:
                (self.keep,) = whole_call(add_kernel, "add", line_id, [self.keep, *got], [self.part(8)])
                sent = [self.keep]
                self.moved = [swap(self.keep, 2 * k, "dp") for k in (1, 2, 3)]
            elif stage == 3:
                (self.keep,) = whole_call(
                    join_kernel, "join_quarters", line_id, [self.keep, *got], [self.part(2)]
                )
                sent, self.moved = [self.keep], [swap(self.keep, 1, "dp")]
            return sent[0]

        def finish(self, *sizes):
            shapes = [sds((n, d), F32) for n in sizes]
            if not custom:
                total = self.moved[0].astype(F32)
                cuts = [sum(sizes[:n]) for n in range(len(sizes))]
                return [total[at : at + n] for at, n in zip(cuts, sizes)]
            operands = [self.keep, self.moved[0]]
            return whole_call(
                finish_kernel, "finish", side_id, operands, shapes, [pltpu.VMEM((self.size, d), F32)], True
            )

    def settle(lead, reductions, *extra):
        lead, values = boundary(lead, *[v for r in reductions for v in r.moved], *extra)
        for r in reductions:
            count = len(r.moved)
            r.moved, values = values[:count], values[count:]
        return (lead, *values)

    grad_low, down_mine, down_partner = lax.optimization_barrier((grad_low, down_mine, down_partner))
    down_reduce = Reduction(down_mine, down_partner, True)
    tie = down_reduce.step()
    grad_low = after(grad_low, tie)
    moved_out = swap(after(out_rows, tie), 1)

    pack_rows = units + width + 64
    hidden_low, mine, partner = spread(
        ffn_backward_kernel, "ffn_backward", (blocks,),
        [row_spec, own_spec(4 * units), row_spec, own_spec(128), own_spec(half), vec_spec]
        + up_specs + down_specs + [vec_spec],
        [row_spec] + [const_spec((pack_rows, d))] * 2,
        [sds((rows, d), BF16)] + [sds((pack_rows, d), BF16)] * 2,
        [pltpu.VMEM((2, d, units), F32), pltpu.VMEM((half, d), F32), pltpu.VMEM((7, 8, d), F32),
         pltpu.VMEM((4, ROWS, units), BF16)] + ffn_scratch + [pltpu.VMEM((ROWS, d), F32), ffn_sems],
        1, 2 * rows * d * 10 * units, rows * d * 16, 0,
    )(side_id, grad_low, slope, normed, scale_one, mixed_near, sums_two, *ups, *downs, vec)
    hidden_low, mine, partner, moved_out = settle(hidden_low, [down_reduce], mine, partner, moved_out)
    tie = down_reduce.step()
    partner = after(partner, tie)
    up_reduce = Reduction(mine, partner, True)
    tie = up_reduce.step()
    hidden_low = after(hidden_low, tie)

    qkv_rows = 3 * width + 64
    sums = [sds((3, half, d), F32), sds((2, 8, half), F32)]
    sum_specs = [any_spec(), const_spec(sums[1].shape)]

    def near_backward(start, count, extra, extra_specs, outs, out_specs, alias):
        return spread(
            functools.partial(attention_backward_kernel, start, short_blocks), "attention_near_backward", (count,),
            [own_spec(d, start), log_spec(start), own_spec(3 * half, start), own_spec(half, start), global_spec(start)]
            + [any_spec()] * 2 + extra_specs,
            [own_spec(3 * half)] + out_specs,
            [sds((count * ROWS, 3 * half), BF16)] + outs,
            weight_scratch + [sems, pltpu.VMEM((ROWS, half), BF16), pltpu.VMEM((8, ROWS), F32),
                              pltpu.VMEM((3, half, d), F32), pltpu.VMEM((2, 8, half), F32)],
            5, count * ROWS * (10 * d * half + 3200 * half), count * ROWS * d * 16, count * ROWS * 320 * 6,
        )(*meta, hidden_low, stat_near, qkv_near, mixed_near, tokens, a0, a1, *extra)

    low_short, *sums_short = near_backward(0, short_blocks, [], [], sums, sum_specs, None)
    (low_short,) = settle(low_short, [down_reduce, up_reduce])
    tie = down_reduce.step()
    tie_two = up_reduce.step()
    sums_short[1] = after(sums_short[1], tie, tie_two)
    low_long, mine, partner = near_backward(
        short_blocks, long_blocks, sums_short, sum_specs,
        [sds((qkv_rows, d), BF16)] * 2, [const_spec((qkv_rows, d))] * 2, None,
    )
    low_long, mine, partner = settle(low_long, [down_reduce, up_reduce], mine, partner)
    ties = [down_reduce.step(), up_reduce.step()]
    qkv_reduce = Reduction(mine, after(partner, *ties), False)
    ties += [qkv_reduce.step()]

    def far_backward(start, count, low_near, extra, alias):
        return spread(
            functools.partial(attention_input_kernel, start, short_blocks), "attention_far_backward", (count,),
            [own_spec(d, start), log_spec(start), own_spec(3 * half, start), own_spec(half, start), own_spec(3 * half)]
            + [any_spec()] * (4 + len(extra)),
            [own_spec(d, start), global_spec(start)], [sds((rows, d), BF16), sds((2 * rows, d), F32)],
            weight_scratch + [pltpu.VMEM((3 * half, d), BF16), sems, pltpu.VMEM((ROWS, 3 * half), BF16),
                              pltpu.VMEM((ROWS, half), BF16), pltpu.VMEM((8, ROWS), F32)],
            5, count * ROWS * (14 * d * half + 3200 * half), count * ROWS * d * 16, count * ROWS * 320 * 6, alias,
        )(*meta, hidden_low, stat_far, qkv_far, mixed_far, low_near, a2, a3, a0, a1, *extra)

    low_short = after(low_short, *ties)
    rows_short, whole_in = far_backward(0, short_blocks, low_short, [], None)
    (rows_short,) = settle(rows_short, [down_reduce, up_reduce, qkv_reduce])
    ties = [qkv_reduce.step(), up_reduce.step(), down_reduce.step()]
    low_long = after(low_long, *ties)
    rows_all, whole_in = far_backward(
        short_blocks, long_blocks, low_long, [rows_short, whole_in], {14: 0, 15: 1}
    )
    (rows_all,) = settle(rows_all, [down_reduce, up_reduce, qkv_reduce])
    tie = qkv_reduce.step()
    tie = after(tie, up_reduce.step())
    down_reduce.moved[0] = after(down_reduce.moved[0], tie)
    (grad_down,) = down_reduce.finish(units)
    moved_rows = swap(after(rows_all, tie), 1)

    def place(whole, other, start, count):
        return spread(
            place_kernel, "place", (count,), [own_spec(d), any_spec()], global_spec(start, 1),
            sds(whole.shape, whole.dtype), (), 1, 0, other.size * 6, 0, {2: 0},
        )(core_id, other, whole)

    layer_output = place(whole_out, after(moved_out, tie), 0, blocks)
    layer_output, moved_rows = settle(layer_output, [qkv_reduce], moved_rows)
    tie = qkv_reduce.step()
    input_grad = place(whole_in, after(moved_rows, tie), 0, blocks)
    up_reduce.moved[0] = after(up_reduce.moved[0], tie)
    grad_up, grad_out, small = up_reduce.finish(units, width, 16)
    grad_up, input_grad = settle(grad_up, [qkv_reduce], input_grad)
    grad_query, grad_key, grad_value, heads = qkv_reduce.finish(width, width, width, 16)
    return (
        layer_output,
        input_grad,
        grad_query.T,
        heads[0, :width],
        grad_key.T,
        grad_value.T,
        heads[1, :width],
        grad_out,
        small[5],
        small[3],
        small[4],
        grad_up,
        small[6],
        grad_down,
        small[2],
        small[0],
        small[1],
    )

def solution(mesh):
    return jax.shard_map(
        per_device,
        mesh=mesh,
        in_specs=(
            P("dp", None),
            P("dp", None),
            P("dp"),
            P("dp"),
            P("dp"),
            P("dp"),
            P(None, "tensor"),
            P("tensor"),
            P(None, "tensor"),
            P(None, "tensor"),
            P("tensor"),
            P("tensor", None),
            P(),
            P(),
            P(),
            P(None, "tensor"),
            P("tensor"),
            P("tensor", None),
            P(),
            P(),
            P(),
        ),
        out_specs=(
            P("dp", None),
            P("dp", None),
            P(None, "tensor"),
            P("tensor"),
            P(None, "tensor"),
            P(None, "tensor"),
            P("tensor"),
            P("tensor", None),
            P(),
            P(),
            P(),
            P(None, "tensor"),
            P("tensor"),
            P("tensor", None),
            P(),
            P(),
            P(),
        ),
        check_vma=False,
    )
```

```python
import functools

import jax
import jax.numpy as jnp
from jax import lax
from jax.experimental import pallas as pl
from jax.experimental.pallas import tpu as pltpu
from jax.sharding import PartitionSpec as P

HEAD_DIM = 64
SHORT_LEN = 128
LONG_LEN = 512
ROWS = 512
SLOTS = ROWS // SHORT_LEN
PAIR = 2 * HEAD_DIM
MASKED = -30000.0
F32 = jnp.float32
BF16 = jnp.bfloat16
VMEM_LIMIT = 60 * 1024 * 1024


def nn(left, right):
    return lax.dot_general(left, right, (((1,), (0,)), ((), ())), preferred_element_type=F32)


def nt(left, right):
    return lax.dot_general(left, right, (((1,), (1,)), ((), ())), preferred_element_type=F32)


def tn(left, right):
    return lax.dot_general(left, right, (((0,), (0,)), ((), ())), preferred_element_type=F32)


def fold_rows(values):
    return jnp.sum(values.reshape(-1, 8, values.shape[-1]), axis=0)


def total_rows(values):
    return jnp.sum(values, axis=0, keepdims=True)


def by_rows(size, body):
    def step(n, carry):
        body(pl.ds(pl.multiple_of(n * 64, 64), 64))
        return carry

    lax.fori_loop(0, size // 64, step, 0)


def clear(ref):
    def body(span):
        for j in range(ref.shape[0]):
            ref[j, span] = jnp.zeros((64, ref.shape[2]), ref.dtype)

    by_rows(ref.shape[1], body)


def copy_rows(source, target, at=0):
    def body(span):
        target[pl.ds(pl.multiple_of(at + span.start, 16), 64)] = source[span].astype(target.dtype)

    if source.shape[0] % 64:
        target[pl.ds(at, source.shape[0])] = source[...].astype(target.dtype)
    else:
        by_rows(source.shape[0], body)


def half_mask(which):
    lanes = lax.broadcasted_iota(jnp.int32, (1, PAIR), 1)
    return (lanes >= HEAD_DIM) if which else (lanes < HEAD_DIM)


def short_valid(meta, block, slot):
    index = SLOTS * (2 * block + meta[0][0]) + slot
    return jnp.where(index < meta[3][0], meta[1][index], 0)


def long_valid(meta, block, short_blocks):
    index = 2 * (block - short_blocks) + 1 - meta[0][0]
    return jnp.where(index < meta[4][0], meta[2][index], 0)


def norm_rows(values):
    centre = values - jnp.mean(values, axis=-1, keepdims=True)
    scale = lax.rsqrt(jnp.mean(centre * centre, axis=-1, keepdims=True) + 1e-12)
    return centre * scale, scale


def norm_back(incoming, normed, scale, gain):
    grad = incoming * gain
    inner = grad - jnp.mean(grad, axis=-1, keepdims=True)
    inner = inner - normed * jnp.mean(grad * normed, axis=-1, keepdims=True)
    return scale * inner


def attention_copies(pieces, sems, wqkv=None, wout=None, bias=None):
    copies = []
    for j, piece in enumerate(pieces):
        width = (piece.shape[0] - 16) // 4
        pairs = []
        if wqkv is not None:
            for k in range(3):
                rows = pl.ds((2 * k + j) * width, width)
                pairs.append((k, piece.at[pl.ds(k * width, width)], wqkv.at[rows]))
        if wout is not None:
            pairs.append((3, piece.at[pl.ds(3 * width, width)], wout.at[pl.ds(j * width, width)]))
        if bias is not None:
            pairs.append((4, piece.at[pl.ds(4 * width, 16)], bias.at[pl.ds(16 * j, 16)]))
        copies += [pltpu.make_async_copy(s, d, sems.at[5 * j + n]) for n, s, d in pairs]
    return copies


def start_all(copies):
    for copy in copies:
        copy.start()


def wait_all(copies):
    for copy in copies:
        copy.wait()


def flat_row(ref):
    return ref[...].astype(F32).reshape(1, ref.shape[0])


def pack_kernel(at, wq, wk, wv, wo, qb, vb, ub, ob, g1, s1, db, g2, s2, piece, vec, wide):
    width = wq.shape[0]
    d = piece.shape[1]
    piece[0:width] = wq[...]
    piece[width : 2 * width] = wk[...]
    piece[2 * width : 3 * width] = wv[...]
    piece[3 * width : 4 * width] = wo[...]
    index = lax.broadcasted_iota(jnp.int32, (16, 1), 0)
    wide[...] = jnp.zeros_like(wide)
    wide[0:1, 0:width] = flat_row(qb)
    wide[1:2, 0:width] = flat_row(vb)
    row_q, row_v, row_u = wide[0:1], wide[1:2], flat_row(ub)
    lead = jnp.where(lax.broadcasted_iota(jnp.int32, (1, d), 1) < d // 2, row_u, 0.0)
    trail = pltpu.roll(row_u - lead, d // 2, 1)
    mine = jnp.where(at[0] == 0, lead, trail)
    far = jnp.where(at[0] == 0, trail, lead)
    rows = [row_u, row_q, pltpu.roll(row_q, width, 1), row_v, pltpu.roll(row_v, width, 1)]
    block = jnp.zeros((16, d), F32)
    for n, row in enumerate(rows + [None] * 4 + [mine, far]):
        if row is not None:
            block = jnp.where(index == n, row, block)
    piece[4 * width : 4 * width + 16] = block.astype(BF16)
    for n, row in enumerate((ob, g1, s1, db, g2, s2)):
        vec[n : n + 1] = flat_row(row)
    vec[6:8] = jnp.zeros((2, d), F32)


def place_kernel(core, other, whole, out):
    out[...] = other[...].astype(out.dtype)


def route_halves_kernel(at, mine, partner, keep, send):
    half = keep.shape[0]
    for out, which in ((keep, at[0]), (send, 1 - at[0])):
        base = which * half

        def body(span):
            rows = pl.ds(pl.multiple_of(base + span.start, 16), 64)
            out[span] = (mine[rows].astype(F32) + partner[rows].astype(F32)).astype(BF16)

        by_rows(half, body)


def route_quarters_kernel(at, keep, other, *outs):
    size = outs[0].shape[0]
    for k, out in enumerate(outs):
        span = pl.ds(pl.multiple_of((at[0] ^ k) * size, 16), size)
        out[...] = (keep[span].astype(F32) + other[span].astype(F32)).astype(BF16)


def add_kernel(at, *refs):
    def body(span):
        refs[-1][span] = sum(ref[span].astype(F32) for ref in refs[:-1]).astype(BF16)

    size = refs[-1].shape[0]
    if size % 64:
        body(pl.ds(0, size))
    else:
        by_rows(size, body)


def choose_kernel(at, own, other, out):
    central = jnp.logical_or(at[0] == 1, at[0] == 2)

    @pl.when(central)
    def _():
        out[...] = own[...]

    @pl.when(jnp.logical_not(central))
    def _():
        out[...] = other[...]


def join_kernel(at, *refs):
    out = refs[-1]
    size = refs[0].shape[0]
    for k, ref in enumerate(refs[:-1]):
        copy_rows(ref, out, pl.multiple_of((at[0] ^ k) * size, 16))


def finish_kernel(at, own, other, *refs):
    outs, whole = refs[:-1], refs[-1]
    join_kernel(at, own, other, whole)
    start = 0
    for out in outs:
        copy_rows(whole.at[pl.ds(start, out.shape[0])], out)
        start += out.shape[0]


def stacked(values):
    zero = jnp.zeros_like(values)
    return jnp.concatenate([jnp.where(half_mask(e), values, zero) for e in range(2)], axis=0)


def unstacked(values):
    size = values.shape[0] // 2
    return jnp.where(half_mask(0), values[:size], values[size:])


def attention_heads_forward(start, count, short_blocks, meta, x, weights, qkv, mixed, logs, stat):
    wqkv, bias, head_bias = weights
    block = pl.program_id(0) + start
    half = mixed.shape[1]

    @pl.when(pl.program_id(0) == 0)
    def _():
        small = bias[...].astype(F32)
        head_bias[0] = (small[1:2] + small[18:19])[:, 0:half]
        head_bias[1] = jnp.zeros((1, half), F32)
        head_bias[2] = (small[3:4] + small[20:21])[:, 0:half]

    def project(k, carry):
        span = pl.ds(pl.multiple_of(k * half, half), half)
        qkv[:, span] = (nt(x[...], wqkv[span]) + head_bias[k]).astype(BF16)
        return carry

    lax.fori_loop(0, 3, project, 0)
    stat[...] = jnp.zeros_like(stat)
    lanes = lax.broadcasted_iota(jnp.int32, (1, 128), 1)

    def tiles(pair, spans):
        column = pl.multiple_of(pair * PAIR, PAIR)
        q, scores = [], []
        for query_at, queries, key_at, keys, valid in spans:
            part = qkv[query_at : query_at + queries, pl.ds(column, PAIR)] * jnp.asarray(0.125, BF16)
            key_part = qkv[key_at : key_at + keys, pl.ds(half + column, PAIR)]
            scores.append(nt(stacked(part), key_part))
        live = [lax.broadcasted_iota(jnp.int32, (1, t[3]), 1) < t[4] for t in spans]
        scores = [jnp.where(a, v, MASKED) for a, v in zip(live, scores)]
        top = [jnp.max(v, axis=-1, keepdims=True) for v in scores]
        weights = [jnp.exp(v - m) for v, m in zip(scores, top)]
        total = [jnp.sum(v, axis=-1, keepdims=True) for v in weights]
        out = [
            nn(v.astype(BF16), qkv[t[2] : t[2] + t[3], pl.ds(2 * half + column, PAIR)])
            for v, t in zip(weights, spans)
        ]
        for (query_at, queries, *_), m, n, v in zip(spans, top, total, out):
            log = m + jnp.log(n)
            rows = stat[query_at : query_at + queries]
            rows = jnp.where(lanes == 2 * pair, log[:queries], rows)
            stat[query_at : query_at + queries] = jnp.where(lanes == 2 * pair + 1, log[queries:], rows)
            mixed[query_at : query_at + queries, pl.ds(column, PAIR)] = unstacked(v * (1.0 / n)).astype(BF16)

    def short_path():
        spans = [
            (slot * SHORT_LEN, SHORT_LEN, slot * SHORT_LEN, SHORT_LEN, short_valid(meta, block, slot))
            for slot in range(SLOTS)
        ]

        def body(pair, carry):
            tiles(pair, spans)
            return carry

        lax.fori_loop(0, half // PAIR, body, 0)

    def long_path():
        valid = long_valid(meta, block, short_blocks)
        spans = [(part * 256, 256, 0, LONG_LEN, valid) for part in range(2)]

        def body(pair, carry):
            tiles(pair, spans)
            return carry

        lax.fori_loop(0, half // PAIR, body, 0)

    if start < short_blocks:
        pl.when(block < short_blocks)(short_path)
    if start + count > short_blocks:
        pl.when(block >= short_blocks)(long_path)
    logs[...] = stat[...].T[0:8]


def attention_forward_kernel(
    start, count, short_blocks, core, slen, llen, scount, lcount, x, a0, a1, qkv, mixed, logs,
    wqkv, wout, bias, sems, stat, head_bias,
):
    copies = attention_copies((a0, a1), sems, wqkv=wqkv, bias=bias)

    @pl.when(pl.program_id(0) == 0)
    def _():
        start_all(copies)
        wait_all(copies)

    meta = (core, slen, llen, scount, lcount)
    attention_heads_forward(start, count, short_blocks, meta, x, (wqkv, bias, head_bias), qkv, mixed, logs, stat)


def attention_finish_kernel(
    start, count, short_blocks, core, slen, llen, scount, lcount, x, a2, a3, mixed_near, a0, a1, vec, *rest,
):
    qkv, mixed, logs, normed, scale_rows, wqkv, wout, bias, near_out, sems, stat, head_bias = rest[-12:]

    width = near_out.shape[0] // 2
    needed = attention_copies((a2, a3), sems, wqkv=wqkv, bias=bias)
    later = attention_copies((a2, a3), sems, wout=wout) + [
        pltpu.make_async_copy(
            piece.at[pl.ds(3 * width, width)], near_out.at[pl.ds(j * width, width)], sems.at[10 + j]
        )
        for j, piece in enumerate((a0, a1))
    ]

    @pl.when(pl.program_id(0) == 0)
    def _():
        start_all(needed + later)
        wait_all(needed)

    meta = (core, slen, llen, scount, lcount)
    attention_heads_forward(start, count, short_blocks, meta, x, (wqkv, bias, head_bias), qkv, mixed, logs, stat)

    @pl.when(pl.program_id(0) == 0)
    def _():
        wait_all(later)

    hidden = x[...].astype(F32) + vec[0:1]
    hidden = hidden + nn(mixed_near[...], near_out[...]) + nn(mixed[...], wout[...])
    rows, scale = norm_rows(hidden)
    normed[...] = rows.astype(BF16)
    scale_rows[...] = jnp.broadcast_to(scale, scale_rows.shape)


def weight_copies(side, ups, downs, up_all, down_all, sems):
    half = ups[2].shape[1]
    spans = [pl.ds(pl.multiple_of(at * half, 16), half) for at in (side[0], 1 - side[0])]
    copies = []
    for j in range(2):
        copies.append([(ups[j], up_all.at[j]), (downs[j], down_all.at[j])])
    for j in range(2):
        pairs = []
        for n in range(2):
            part = pl.ds(n * half, half)
            pairs.append((ups[2 + 2 * n + j], up_all.at[2 + j, :, part]))
            pairs.append((downs[2 + j].at[spans[n]], down_all.at[2 + j, part]))
        copies.append(pairs)
    return [
        [pltpu.make_async_copy(s, d, sems.at[4 * j + n]) for n, (s, d) in enumerate(pairs)]
        for j, pairs in enumerate(copies)
    ]


def start_weights(copies):
    for pairs in copies:
        for copy in pairs:
            copy.start()


def wait_weights(copies, step):
    for at in range(2):

        @pl.when(jnp.logical_and(pl.program_id(0) == 0, step == at))
        def _():
            for pairs in copies[2 * at : 2 * at + 2]:
                for copy in pairs:
                    copy.wait()


def ffn_forward_kernel(short_blocks, core, slen, llen, scount, lcount, side, normed, cotangent, *rest):
    ups, downs, biases = rest[0:6], rest[6:10], rest[10:14]
    vec, layer_out, layer_rows, grad_low, slope, down_mine, down_partner, sums = rest[14:22]
    active, down_sum, vec_sum, up_all, down_all, bias_all, total, sems = rest[22:]
    meta = (core, slen, llen, scount, lcount)
    block = pl.program_id(0)
    units = up_all.shape[2]
    half = units // 2
    copies = weight_copies(side, ups, downs, up_all, down_all, sems)

    @pl.when(block == 0)
    def _():
        start_weights(copies)
        clear(down_sum)
        vec_sum[...] = jnp.zeros_like(vec_sum)
        for j in range(2):
            bias_all[j] = biases[j][0:1].astype(F32)
            for n in range(2):
                bias_all[2 + j, :, n * half : (n + 1) * half] = biases[2 + j][9 + n : 10 + n, 0:half].astype(F32)

    first = normed[...].astype(F32) * vec[1:2] + vec[2:3]
    first_low = first.astype(BF16)
    total[...] = first + vec[3:4]

    def groups(step, carry):
        wait_weights(copies, step)
        for e in range(2):
            j = 2 * step + e
            inner = nn(first_low, up_all[j]) + bias_all[j]
            chance = 0.5 * (1.0 + lax.erf(inner * 0.7071067811865476))
            low_units = (inner * chance).astype(BF16)
            slope[:, pl.ds(pl.multiple_of(j * units, units), units)] = (
                chance + inner * jnp.exp(-0.5 * inner * inner) * 0.3989422804014327
            ).astype(BF16)
            active[j] = low_units
            total[...] += nn(low_units, down_all[j])
        return carry

    lax.fori_loop(0, 2, groups, 0)
    rows, scale = norm_rows(total[...])
    result = (rows * vec[4:5] + vec[5:6]).astype(BF16)
    layer_out[...] = result
    layer_rows[...] = result
    position = lax.broadcasted_iota(jnp.int32, (ROWS, 1), 0)
    slot = position // SHORT_LEN
    short_limit = jnp.zeros((ROWS, 1), jnp.int32)
    for n in range(SLOTS):
        short_limit = jnp.where(slot == n, short_valid(meta, jnp.minimum(block, short_blocks - 1), n), short_limit)
    long_limit = long_valid(meta, jnp.maximum(block, short_blocks), short_blocks)
    is_short = block < short_blocks
    alive = jnp.where(is_short, position % SHORT_LEN, position) < jnp.where(
        is_short, short_limit, long_limit
    )
    upstream = jnp.where(alive, cotangent[...].astype(F32), 0.0)
    grad = norm_back(upstream, rows, scale, vec[4:5])
    low = grad.astype(BF16)
    grad_low[...] = low
    vec_sum[0] += fold_rows(upstream * rows)
    vec_sum[1] += fold_rows(upstream)
    vec_sum[2] += fold_rows(grad)
    for j in range(2):
        down_sum[j] += tn(active[j], low)

    @pl.when(block == pl.num_programs(0) - 1)
    def _():
        copy_rows(down_sum.at[0], down_mine)
        copy_rows(down_sum.at[1], down_partner)
        sums[...] = jnp.zeros_like(sums)
        for n in range(3):
            sums[n : n + 1] = total_rows(vec_sum[n])


def ffn_backward_kernel(side, grad_low, slope, normed, stat, mixed, sums_two, *rest):
    ups, downs = rest[0:6], rest[6:10]
    vec, hidden_low, mine, partner = rest[10:14]
    up_sum, out_sum, vec_sum, kept, up_all, down_all, total, sems = rest[14:]
    block = pl.program_id(0)
    units = up_sum.shape[2]
    width = mixed.shape[1] // 2
    copies = weight_copies(side, ups, downs, up_all, down_all, sems)

    @pl.when(block == 0)
    def _():
        start_weights(copies)
        clear(up_sum)
        out_sum[...] = jnp.zeros_like(out_sum)
        vec_sum[...] = jnp.zeros_like(vec_sum)

    low = grad_low[...]
    total[...] = low.astype(F32)

    def groups(step, carry):
        wait_weights(copies, step)
        for e in range(2):
            j = 2 * step + e
            inner = nt(low, down_all[j]) * slope[:, pl.ds(pl.multiple_of(j * units, units), units)].astype(F32)
            inner_low = inner.astype(BF16)
            total[...] += nt(inner_low, up_all[j])
            vec_sum[j] += fold_rows(inner)
            kept[j] = inner_low
        return carry

    lax.fori_loop(0, 2, groups, 0)
    rows = normed[...].astype(F32)
    first_low = (rows * vec[1:2] + vec[2:3]).astype(BF16)
    for j in range(2):
        up_sum[j] += tn(first_low, kept[j])
    incoming = total[...]
    grad = norm_back(incoming, rows, stat[:, 0:1], vec[1:2])
    vec_sum[4] += fold_rows(incoming * rows)
    vec_sum[5] += fold_rows(incoming)
    vec_sum[6] += fold_rows(grad)
    grad_attn = grad.astype(BF16)
    hidden_low[...] = grad_attn
    out_sum[...] += tn(mixed[...], grad_attn)

    @pl.when(block == pl.num_programs(0) - 1)
    def _():
        index = lax.broadcasted_iota(jnp.int32, (16, 1), 0)
        shared = [sums_two[n : n + 1] for n in range(3)] + [total_rows(vec_sum[n]) for n in range(4, 7)]
        for j, out in enumerate((mine, partner)):
            copy_rows(up_sum.at[j], out)
            copy_rows(out_sum.at[pl.ds(j * width, width)], out, units)
            out[units + width :] = jnp.zeros((out.shape[0] - units - width, out.shape[1]), BF16)
            rows_out = jnp.zeros((16, out.shape[1]), F32)
            for n, row in enumerate(shared + [total_rows(vec_sum[j])]):
                rows_out = jnp.where(index == n, row, rows_out)
            out[units + width : units + width + 16] = rows_out.astype(BF16)


def attention_heads_backward(start, short_blocks, meta, logs, qkv, mixed, mixed_grad, low_qkv, delta):
    block = pl.program_id(0) + start
    half = mixed.shape[1]
    own = (mixed_grad[...].astype(F32) * mixed[...].astype(F32)).astype(BF16)
    head = lax.broadcasted_iota(jnp.int32, (8, half), 1) // HEAD_DIM
    pick = jnp.where(head == lax.broadcasted_iota(jnp.int32, (8, half), 0), 1.0, 0.0)
    delta[...] = nt(pick.astype(BF16), own)

    index = lax.broadcasted_iota(jnp.int32, (8, 1), 0)

    def tiles(pair, size, valids):
        column = pl.multiple_of(pair * PAIR, PAIR)
        spans = [pl.ds(n * size, size) for n in range(len(valids))]

        def rows(ref, span):
            picked = [total_rows(jnp.where(index == 2 * pair + e, ref[:, span], 0.0)) for e in range(2)]
            return jnp.concatenate(picked, axis=1)

        q = [stacked(qkv[t, pl.ds(column, PAIR)] * jnp.asarray(0.125, BF16)) for t in spans]
        g = [stacked(mixed_grad[t, pl.ds(column, PAIR)]) for t in spans]
        k = [qkv[t, pl.ds(half + column, PAIR)] for t in spans]
        scores = [nt(b, a) for a, b in zip(q, k)]
        grads = [nt(qkv[t, pl.ds(2 * half + column, PAIR)], a) for t, a in zip(spans, g)]
        place = lax.broadcasted_iota(jnp.int32, (size, 1), 0)
        probs = [
            jnp.where(place < valid, jnp.exp(v - rows(logs, t)), 0.0)
            for v, t, valid in zip(scores, spans, valids)
        ]
        scores = [(p * (v - rows(delta, t))).astype(BF16) for p, v, t in zip(probs, grads, spans)]
        dq = [tn(v, b) for v, b in zip(scores, k)]
        dk = [nn(v, a) for v, a in zip(scores, q)]
        dv = [nn(p.astype(BF16), a) for p, a in zip(probs, g)]
        for t, a, b, c in zip(spans, dq, dk, dv):
            low_qkv[t, pl.ds(column, PAIR)] = (unstacked(a) * 0.125).astype(BF16)
            low_qkv[t, pl.ds(half + column, PAIR)] = b.astype(BF16)
            low_qkv[t, pl.ds(2 * half + column, PAIR)] = c.astype(BF16)

    if start < short_blocks:
        valids = [short_valid(meta, block, slot) for slot in range(SLOTS)]
        size = SHORT_LEN
    else:
        valids = [long_valid(meta, block, short_blocks)]
        size = LONG_LEN

    def body(pair, carry):
        tiles(pair, size, valids)
        return carry

    lax.fori_loop(0, half // PAIR, body, 0)


def attention_backward_kernel(
    start, short_blocks, core, slen, llen, scount, lcount, hidden_low, stat, qkv, mixed, x,
    a0, a1, *rest,
):
    if start:
        sums_in, vec_in, low_qkv, mine, partner = rest[:5]
    else:
        low_qkv, qkv_out, vec_out = rest[:3]
    wqkv, wout, bias, sems, mixed_grad, delta, qkv_sum, vec_sum = rest[-8:]
    meta = (core, slen, llen, scount, lcount)
    block = pl.program_id(0)
    half = mixed.shape[1]
    width = half // 2

    copies = attention_copies((a0, a1), sems, wout=wout)
    carried = pltpu.make_async_copy(sums_in, qkv_sum, sems.at[15]) if start else None

    @pl.when(block == 0)
    def _():
        start_all(copies)
        if start:
            carried.start()
        wait_all(copies)
        if start:
            vec_sum[...] = vec_in[...]
        else:
            clear(qkv_sum)
            vec_sum[...] = jnp.zeros_like(vec_sum)

    mixed_grad[...] = nt(hidden_low[...], wout[...]).astype(BF16)
    attention_heads_backward(start, short_blocks, meta, stat, qkv, mixed, mixed_grad, low_qkv, delta)
    vec_sum[0] += fold_rows(low_qkv[:, 0:half].astype(F32))
    vec_sum[1] += fold_rows(low_qkv[:, 2 * half : 3 * half].astype(F32))

    if start:

        @pl.when(block == 0)
        def _():
            carried.wait()

    for k in range(3):
        qkv_sum[k] += tn(low_qkv[:, k * half : (k + 1) * half], x[...])

    @pl.when(block == pl.num_programs(0) - 1)
    def _():
        if not start:
            leaving = pltpu.make_async_copy(qkv_sum, qkv_out, sems.at[15])
            leaving.start()
            leaving.wait()
            vec_out[...] = vec_sum[...]
        else:
            index = lax.broadcasted_iota(jnp.int32, (16, 1), 0)
            heads = [total_rows(vec_sum[n]) for n in range(2)]
            for j, out in enumerate((mine, partner)):
                for k in range(3):
                    out[k * width : (k + 1) * width] = qkv_sum[k, j * width : (j + 1) * width].astype(BF16)
                out[3 * width :] = jnp.zeros((out.shape[0] - 3 * width, out.shape[1]), BF16)
                rows_out = jnp.zeros((16, half), F32)
                for n, row in enumerate(heads):
                    row = pltpu.roll(row, half - width, 1) if j else row
                    rows_out = jnp.where(index == n, row, rows_out)
                out[3 * width : 3 * width + 16, 0:half] = rows_out.astype(BF16)


def attention_input_kernel(
    start, short_blocks, core, slen, llen, scount, lcount, hidden_low, stat, qkv, mixed, low_near,
    a2, a3, a0, a1, *rest,
):
    input_rows, input_grad = rest[-10:-8]
    wqkv, wout, bias, near_qkv, sems, low_qkv, mixed_grad, delta = rest[-8:]
    meta = (core, slen, llen, scount, lcount)

    width = near_qkv.shape[0] // 6
    needed = attention_copies((a2, a3), sems, wout=wout)
    later = attention_copies((a2, a3), sems, wqkv=wqkv) + [
        pltpu.make_async_copy(
            piece.at[pl.ds(k * width, width)],
            near_qkv.at[pl.ds((2 * k + j) * width, width)],
            sems.at[10 + 2 * k + j],
        )
        for k in range(3)
        for j, piece in enumerate((a0, a1))
    ]

    @pl.when(pl.program_id(0) == 0)
    def _():
        start_all(needed + later)
        wait_all(needed)

    low = hidden_low[...]
    mixed_grad[...] = nt(low, wout[...]).astype(BF16)
    attention_heads_backward(start, short_blocks, meta, stat, qkv, mixed, mixed_grad, low_qkv, delta)

    @pl.when(pl.program_id(0) == 0)
    def _():
        wait_all(later)

    total = low.astype(F32) + nn(low_near[...], near_qkv[...]) + nn(low_qkv[...], wqkv[...])
    input_rows[...] = total.astype(BF16)
    input_grad[...] = total


def const_spec(shape):
    return pl.BlockSpec(
        shape, lambda *_: (0,) * len(shape), pipeline_mode=pl.Buffered(1)
    )


def any_spec():
    return pl.BlockSpec(memory_space=pl.ANY)


def own_spec(width, start=0):
    return pl.BlockSpec((ROWS, width), lambda i, *_: (i + start, 0))


def whole_call(body, name, which, operands, shapes, scratch=(), keep=False, limit=24):
    moved = sum(v.size * v.dtype.itemsize for v in list(operands) + list(shapes))
    vmem = pl.BlockSpec(memory_space=pltpu.VMEM)
    if not keep:
        operands = [pltpu.with_memory_space_constraint(v, pltpu.VMEM) for v in operands]
        shapes = [pltpu.VMEM(v.shape, v.dtype) for v in shapes]
    return pl.pallas_call(
        body,
        name=name,
        in_specs=[pl.BlockSpec(memory_space=pltpu.SMEM)] + [vmem] * len(operands),
        out_specs=[vmem] * len(shapes),
        out_shape=shapes,
        scratch_shapes=list(scratch),
        compiler_params=pltpu.CompilerParams(vmem_limit_bytes=limit * 1024 * 1024),
        cost_estimate=pl.CostEstimate(flops=0, bytes_accessed=moved, transcendentals=0),
    )(which, *operands)


def spread(body, name, grid, in_specs, out_specs, out_shape, scratch=(), prefetch=0, flops=0, moved=0, exps=0, alias=None):
    return pl.pallas_call(
        body,
        name=name,
        grid_spec=pltpu.PrefetchScalarGridSpec(
            num_scalar_prefetch=prefetch,
            grid=grid,
            in_specs=in_specs,
            out_specs=out_specs,
            scratch_shapes=list(scratch),
        ),
        out_shape=out_shape,
        input_output_aliases=alias or {},
        compiler_params=pltpu.CompilerParams(
            dimension_semantics=("arbitrary",), vmem_limit_bytes=VMEM_LIMIT
        ),
        cost_estimate=pl.CostEstimate(flops=flops, bytes_accessed=moved, transcendentals=exps),
    )


def per_device(
    tokens,
    cotangent,
    short_len,
    long_len,
    short_count,
    long_count,
    query_weight,
    query_bias,
    key_weight,
    value_weight,
    value_bias,
    output_weight,
    output_bias,
    first_gain,
    first_shift,
    up_weight,
    up_bias,
    down_weight,
    down_bias,
    second_gain,
    second_shift,
):
    d = tokens.shape[1]
    width = query_weight.shape[1]
    units = up_weight.shape[1]
    half = 2 * width
    piece_rows = 4 * width + 16
    short_blocks = short_len.shape[0] * SHORT_LEN // (2 * ROWS)
    long_blocks = long_len.shape[0] * LONG_LEN // (2 * ROWS)
    blocks = short_blocks + long_blocks
    rows = blocks * ROWS
    core = lax.axis_index("tensor") % 2
    side = lax.axis_index("dp") % 2
    core_id = core.astype(jnp.int32).reshape(1)
    meta = (core_id, short_len, long_len, short_count, long_count)
    sds = jax.ShapeDtypeStruct

    def swap(values, bit, axis="tensor"):
        size = lax.axis_size(axis)
        return lax.ppermute(values, axis, [(i, i ^ bit) for i in range(size)])

    def after(value, *others):
        return lax.optimization_barrier((value,) + others)[0]

    def global_spec(start=0, flip=0):
        def index(i, core, *_):
            i = i + start
            first = core[0] if flip == 0 else 1 - core[0]
            return (2 * i + jnp.where(i < short_blocks, first, 1 - first), 0)

        return pl.BlockSpec((ROWS, d), index)

    vec_spec = const_spec((8, d))
    row_spec = own_spec(d)

    side_id = side.astype(jnp.int32).reshape(1)
    line_id = (lax.axis_index("dp") // 2).astype(jnp.int32).reshape(1)
    vectors = [query_bias, value_bias, up_bias, output_bias, first_gain, first_shift,
               down_bias, second_gain, second_shift]
    a0, vec = whole_call(
        pack_kernel, "pack", side_id,
        [query_weight.T, key_weight.T, value_weight.T, output_weight, *vectors],
        [sds((piece_rows, d), BF16), sds((8, d), F32)], [pltpu.VMEM((8, d), F32)], True, 61,
    )
    up_split = lax.dynamic_slice_in_dim(up_weight, side * (units // 2), units // 2, 1)
    def boundary(lead, *values):
        out = lax.optimization_barrier((lead,) + values)
        return out[0], list(out[1:])

    a1 = after(swap(a0, 1), up_split)
    a2 = swap(a0, 2)

    weight_scratch = [
        pltpu.VMEM((3 * half, d), BF16),
        pltpu.VMEM((half, d), BF16),
        pltpu.VMEM((32, d), BF16),
    ]
    sems = pltpu.SemaphoreType.DMA((16,))
    stat_scratch = pltpu.VMEM((ROWS, 128), F32)

    def log_spec(start=0):
        return pl.BlockSpec((8, ROWS), lambda i, *_: (i + start, 0))

    head_shapes = [sds((rows, 3 * half), BF16), sds((rows, half), BF16), sds((8 * blocks, ROWS), F32)]
    head_flops = 2 * rows * d * 3 * half + 4 * rows * 320 * half
    qkv_near, mixed_near, stat_near = spread(
        functools.partial(attention_forward_kernel, 0, blocks, short_blocks), "attention_near", (blocks,),
        [global_spec()] + [any_spec()] * 2, [own_spec(3 * half), own_spec(half), log_spec()], head_shapes,
        weight_scratch + [sems, stat_scratch, pltpu.VMEM((3, 1, half), F32)], 5,
        head_flops, rows * d * 8, rows * 320 * 6,
    )(*meta, tokens, a0, a1)

    stat_near, (a2,) = boundary(stat_near, a2)
    u2 = swap(after(up_split, a2), 2)
    d2 = swap(after(down_weight, a2), 2)
    a3 = swap(a2, 1)
    u1 = swap(after(up_weight, a3), 1)

    def far_forward(start, count, extra, alias):
        return spread(
            functools.partial(attention_finish_kernel, start, count, short_blocks), "attention_far", (count,),
            [global_spec(start)] + [any_spec()] * 2 + [own_spec(half, start)] + [any_spec()] * 2 + [vec_spec]
            + [any_spec()] * len(extra),
            [own_spec(3 * half, start), own_spec(half, start), log_spec(start), own_spec(d, start), own_spec(128, start)],
            head_shapes + [sds((rows, d), BF16), sds((rows, 128), F32)],
            weight_scratch + [pltpu.VMEM((half, d), BF16), sems, stat_scratch, pltpu.VMEM((3, 1, half), F32)], 5,
            (head_flops + 2 * rows * d * d) * count // blocks, count * ROWS * d * 10, count * ROWS * 320 * 6, alias,
        )(*meta, tokens, a2, a3, mixed_near, a0, a1, vec, *extra)

    far = list(far_forward(0, short_blocks, [], None))
    far[3], (u2, u1, down_near) = boundary(far[3], u2, u1, down_weight)
    u4 = swap(u2, 1, "dp")
    u3, d1 = swap(u2, 1), swap(down_near, 1)
    qkv_far, mixed_far, stat_far, normed, scale_one = far_forward(
        short_blocks, long_blocks, far, {12 + n: n for n in range(5)}
    )
    normed, (u4, u3, d2, d1) = boundary(normed, u4, u3, d2, d1)
    u5, d3 = swap(u4, 1), swap(d2, 1)
    ups = (up_weight, u1, u2, u3, u4, u5)
    downs = (down_weight, d1, d2, d3)
    bias_spec = pl.BlockSpec((16, d), lambda *_: (4 * width // 16, 0), pipeline_mode=pl.Buffered(1))
    up_specs = [any_spec()] * len(ups)
    down_specs = [any_spec()] * len(downs)
    ffn_scratch = [
        pltpu.VMEM((4, d, units), BF16),
        pltpu.VMEM((4, units, d), BF16),
    ]
    ffn_sems = pltpu.SemaphoreType.DMA((16,))
    whole_out, out_rows, grad_low, slope, down_mine, down_partner, sums_two = spread(
        functools.partial(ffn_forward_kernel, short_blocks), "ffn_forward", (blocks,),
        [row_spec, global_spec()] + up_specs + down_specs + [bias_spec] * 4 + [vec_spec],
        [global_spec(), row_spec, row_spec, own_spec(4 * units)] + [const_spec((units, d))] * 2 + [vec_spec],
        [sds((2 * rows, d), BF16), sds((rows, d), BF16), sds((rows, d), BF16), sds((rows, 4 * units), BF16)]
        + [sds((units, d), BF16)] * 2 + [sds((8, d), F32)],
        [pltpu.VMEM((4, ROWS, units), BF16), pltpu.VMEM((2, units, d), F32), pltpu.VMEM((3, 8, d), F32)]
        + ffn_scratch + [pltpu.VMEM((4, 1, units), F32), pltpu.VMEM((ROWS, d), F32), ffn_sems],
        6, 2 * rows * d * 10 * units, rows * d * 20, rows * 8 * units,
    )(*meta, side_id, normed, cotangent, *ups, *downs, a0, a1, a2, a3, vec)

    custom = lax.axis_size("dp") == 8

    line_steps = (
        [(0, 1), (3, 2)],
        [(1, 2), (2, 1)],
        [(1, 0), (2, 3)],
    )

    def along_line(values, stage):
        pairs = [(2 * i + n, 2 * j + n) for i, j in line_steps[stage] for n in range(2)]
        return lax.ppermute(values, "dp", pairs)

    class Reduction:
        def __init__(self, mine, partner, central):
            self.mine, self.size, self.central = mine, mine.shape[0], central
            self.moved = [swap(partner, 1)]
            self.stage = 0

        def part(self, count):
            return sds((self.size // count, d), BF16)

        def step(self):
            got = self.moved
            stage, self.stage = self.stage, self.stage + 1
            if not custom:
                if stage == 0:
                    total = (self.mine.astype(F32) + got[0].astype(F32)).astype(BF16)
                    self.moved = [lax.psum(total, "dp")]
                return self.moved[0]
            if stage == 0:
                self.keep, send = whole_call(
                    route_halves_kernel, "halves", side_id, [self.mine, got[0]], [self.part(2)] * 2
                )
                sent, self.moved = [send], [swap(send, 1, "dp")]
            elif self.central and stage < 4:
                (self.keep,) = whole_call(add_kernel, "add", line_id, [self.keep, got[0]], [self.part(2)])
                sent, self.moved = [self.keep], [along_line(self.keep, stage - 1)]
            elif self.central and stage == 4:
                (self.keep,) = whole_call(choose_kernel, "choose", line_id, [self.keep, got[0]], [self.part(2)])
                sent, self.moved = [self.keep], [swap(self.keep, 1, "dp")]
            elif stage == 1:
                self.keep, *sent = whole_call(
                    route_quarters_kernel, "quarters", line_id, [self.keep, got[0]], [self.part(8)] * 4
                )
                self.moved = [swap(v, 2 * (k + 1), "dp") for k, v in enumerate(sent)]
            elif stage == 2:
                (self.keep,) = whole_call(add_kernel, "add", line_id, [self.keep, *got], [self.part(8)])
                sent = [self.keep]
                self.moved = [swap(self.keep, 2 * k, "dp") for k in (1, 2, 3)]
            elif stage == 3:
                (self.keep,) = whole_call(
                    join_kernel, "join_quarters", line_id, [self.keep, *got], [self.part(2)]
                )
                sent, self.moved = [self.keep], [swap(self.keep, 1, "dp")]
            return sent[0]

        def finish(self, *sizes):
            shapes = [sds((n, d), F32) for n in sizes]
            if not custom:
                total = self.moved[0].astype(F32)
                cuts = [sum(sizes[:n]) for n in range(len(sizes))]
                return [total[at : at + n] for at, n in zip(cuts, sizes)]
            operands = [self.keep, self.moved[0]]
            return whole_call(
                finish_kernel, "finish", side_id, operands, shapes, [pltpu.VMEM((self.size, d), F32)], True
            )

    def settle(lead, reductions, *extra):
        lead, values = boundary(lead, *[v for r in reductions for v in r.moved], *extra)
        for r in reductions:
            count = len(r.moved)
            r.moved, values = values[:count], values[count:]
        return (lead, *values)

    grad_low, down_mine, down_partner = lax.optimization_barrier((grad_low, down_mine, down_partner))
    down_reduce = Reduction(down_mine, down_partner, True)
    tie = down_reduce.step()
    grad_low = after(grad_low, tie)
    moved_out = swap(after(out_rows, tie), 1)

    pack_rows = units + width + 64
    hidden_low, mine, partner = spread(
        ffn_backward_kernel, "ffn_backward", (blocks,),
        [row_spec, own_spec(4 * units), row_spec, own_spec(128), own_spec(half), vec_spec]
        + up_specs + down_specs + [vec_spec],
        [row_spec] + [const_spec((pack_rows, d))] * 2,
        [sds((rows, d), BF16)] + [sds((pack_rows, d), BF16)] * 2,
        [pltpu.VMEM((2, d, units), F32), pltpu.VMEM((half, d), F32), pltpu.VMEM((7, 8, d), F32),
         pltpu.VMEM((4, ROWS, units), BF16)] + ffn_scratch + [pltpu.VMEM((ROWS, d), F32), ffn_sems],
        1, 2 * rows * d * 10 * units, rows * d * 16, 0,
    )(side_id, grad_low, slope, normed, scale_one, mixed_near, sums_two, *ups, *downs, vec)
    hidden_low, mine, partner, moved_out = settle(hidden_low, [down_reduce], mine, partner, moved_out)
    tie = down_reduce.step()
    partner = after(partner, tie)
    up_reduce = Reduction(mine, partner, True)
    tie = up_reduce.step()
    hidden_low = after(hidden_low, tie)

    qkv_rows = 3 * width + 64
    sums = [sds((3, half, d), F32), sds((2, 8, half), F32)]
    sum_specs = [any_spec(), const_spec(sums[1].shape)]

    def near_backward(start, count, extra, extra_specs, outs, out_specs, alias):
        return spread(
            functools.partial(attention_backward_kernel, start, short_blocks), "attention_near_backward", (count,),
            [own_spec(d, start), log_spec(start), own_spec(3 * half, start), own_spec(half, start), global_spec(start)]
            + [any_spec()] * 2 + extra_specs,
            [own_spec(3 * half)] + out_specs,
            [sds((count * ROWS, 3 * half), BF16)] + outs,
            weight_scratch + [sems, pltpu.VMEM((ROWS, half), BF16), pltpu.VMEM((8, ROWS), F32),
                              pltpu.VMEM((3, half, d), F32), pltpu.VMEM((2, 8, half), F32)],
            5, count * ROWS * (10 * d * half + 3200 * half), count * ROWS * d * 16, count * ROWS * 320 * 6,
        )(*meta, hidden_low, stat_near, qkv_near, mixed_near, tokens, a0, a1, *extra)

    low_short, *sums_short = near_backward(0, short_blocks, [], [], sums, sum_specs, None)
    (low_short,) = settle(low_short, [down_reduce, up_reduce])
    tie = down_reduce.step()
    tie_two = up_reduce.step()
    sums_short[1] = after(sums_short[1], tie, tie_two)
    low_long, mine, partner = near_backward(
        short_blocks, long_blocks, sums_short, sum_specs,
        [sds((qkv_rows, d), BF16)] * 2, [const_spec((qkv_rows, d))] * 2, None,
    )
    low_long, mine, partner = settle(low_long, [down_reduce, up_reduce], mine, partner)
    qkv_reduce = Reduction(mine, partner, False)
    ties = [down_reduce.step(), up_reduce.step(), qkv_reduce.step()]

    def far_backward(start, count, low_near, extra, alias):
        return spread(
            functools.partial(attention_input_kernel, start, short_blocks), "attention_far_backward", (count,),
            [own_spec(d, start), log_spec(start), own_spec(3 * half, start), own_spec(half, start), own_spec(3 * half)]
            + [any_spec()] * (4 + len(extra)),
            [own_spec(d, start), global_spec(start)], [sds((rows, d), BF16), sds((2 * rows, d), F32)],
            weight_scratch + [pltpu.VMEM((3 * half, d), BF16), sems, pltpu.VMEM((ROWS, 3 * half), BF16),
                              pltpu.VMEM((ROWS, half), BF16), pltpu.VMEM((8, ROWS), F32)],
            5, count * ROWS * (14 * d * half + 3200 * half), count * ROWS * d * 16, count * ROWS * 320 * 6, alias,
        )(*meta, hidden_low, stat_far, qkv_far, mixed_far, low_near, a2, a3, a0, a1, *extra)

    low_short = after(low_short, *ties)
    rows_short, whole_in = far_backward(0, short_blocks, low_short, [], None)
    (rows_short,) = settle(rows_short, [down_reduce, up_reduce, qkv_reduce])
    ties = [qkv_reduce.step(), up_reduce.step(), down_reduce.step()]
    low_long = after(low_long, *ties)
    rows_all, whole_in = far_backward(
        short_blocks, long_blocks, low_long, [rows_short, whole_in], {14: 0, 15: 1}
    )
    (rows_all,) = settle(rows_all, [down_reduce, up_reduce, qkv_reduce])
    tie = qkv_reduce.step()
    tie = after(tie, up_reduce.step())
    down_reduce.moved[0] = after(down_reduce.moved[0], tie)
    (grad_down,) = down_reduce.finish(units)
    moved_rows = swap(after(rows_all, tie), 1)

    def place(whole, other, start, count):
        return spread(
            place_kernel, "place", (count,), [own_spec(d), any_spec()], global_spec(start, 1),
            sds(whole.shape, whole.dtype), (), 1, 0, other.size * 6, 0, {2: 0},
        )(core_id, other, whole)

    layer_output = place(whole_out, after(moved_out, tie), 0, blocks)
    layer_output, moved_rows = settle(layer_output, [qkv_reduce], moved_rows)
    tie = qkv_reduce.step()
    input_grad = place(whole_in, after(moved_rows, tie), 0, blocks)
    up_reduce.moved[0] = after(up_reduce.moved[0], tie)
    grad_up, grad_out, small = up_reduce.finish(units, width, 16)
    grad_up, input_grad = settle(grad_up, [qkv_reduce], input_grad)
    grad_query, grad_key, grad_value, heads = qkv_reduce.finish(width, width, width, 16)
    return (
        layer_output,
        input_grad,
        grad_query.T,
        heads[0, :width],
        grad_key.T,
        grad_value.T,
        heads[1, :width],
        grad_out,
        small[5],
        small[3],
        small[4],
        grad_up,
        small[6],
        grad_down,
        small[2],
        small[0],
        small[1],
    )

def solution(mesh):
    return jax.shard_map(
        per_device,
        mesh=mesh,
        in_specs=(
            P("dp", None),
            P("dp", None),
            P("dp"),
            P("dp"),
            P("dp"),
            P("dp"),
            P(None, "tensor"),
            P("tensor"),
            P(None, "tensor"),
            P(None, "tensor"),
            P("tensor"),
            P("tensor", None),
            P(),
            P(),
            P(),
            P(None, "tensor"),
            P("tensor"),
            P("tensor", None),
            P(),
            P(),
            P(),
        ),
        out_specs=(
            P("dp", None),
            P("dp", None),
            P(None, "tensor"),
            P("tensor"),
            P(None, "tensor"),
            P(None, "tensor"),
            P("tensor"),
            P("tensor", None),
            P(),
            P(),
            P(),
            P(None, "tensor"),
            P("tensor"),
            P("tensor", None),
            P(),
            P(),
            P(),
        ),
        check_vma=False,
    )
```
